512 devices in a mesh: leaf: 32 (over x, y), front: 16 (over z, core).
Axes of the slice: x: 4, y: 8, z: 8, core: 2. Of those that a mesh axis runs over, the one named last changes fastest.
Arguments:
- coupling: bfloat16 [65536, 2048], P('leaf', 'front'), may hold values from -0.015625 to 0.015625
- block_pattern: int32 [32, 16, 16], P('leaf', None, 'front'), may hold values 0 or 1
- supernode_inverse: bfloat16 [512, 128, 128], P('leaf'), may hold values from -0.6 to 2, as said below
- subdomain_sizes: int32 [32], P('leaf'), may hold values from 512 to 2048, as said below
- block_maps: int32 [4, 32, 16], P(None, 'leaf'), may hold values from 0 to 15, as said below
- top_fronts: float32 [2, 2048, 2048], P(None, None, 'front'), may hold values from -108 to 140
Outputs:
- factored_fronts: float32 [4096, 2048], P('leaf', 'front')
The draws below stay inside these ranges and needn't reach their ends.
Inputs may be any that keep to these rules, and one draw needn't show every extreme that they name: `subdomain_sizes`: uneven interior sizes; some subdomain has exactly 2048. block_maps[k, l] is the map of the level-k tree node holding subdomain l (subdomains with equal l // 2**k share it, and its row): a permutation of 0 .. 15 sending the node's separator block b to block block_maps[k, l, b] of its parent's. `supernode_inverse`: each block is lower triangular with its diagonal between 1 and 2.
All inputs are finite; a program needn't handle non-finite values. No bound on the sum of `block_pattern` on one device may be relied on, other than what follows from the above.
Results may differ from the reference program's by a relative error of at most 0.00085.
Values may be sent and summed in bfloat16 or wider, within the bound.
A program may use at most 128 MiB of HBM per device.

```python
import jax
import jax.numpy as jnp
from jax import lax

S = 2048
BLK = 128
NMAX = 2048
PIV = 512
TOPS = 2
LEVELS = 4
SUBDOMAINS = 32
NB = 16
NBLK = 16


def permute_one(node_key):
    return jax.random.permutation(node_key, NBLK)


def draw_coupling(key, part):
    first_key = jax.random.fold_in(jax.random.fold_in(key, 11), 0)
    shape = (SUBDOMAINS * NMAX, S)
    spread = (0.5 / (NMAX * 2 ** LEVELS)) ** 0.5
    values = jnp.clip(jax.random.normal(first_key, shape, jnp.float32), -4.0, 4.0)
    return (spread * values).astype(jnp.bfloat16)


def draw_block_maps(key, part):
    row_list = []
    for tree_level in range(LEVELS):
        stride = 2 ** tree_level
        node_keys = jax.random.split(jax.random.fold_in(key, 17 + tree_level), SUBDOMAINS // stride)
        node_perms = jax.vmap(permute_one)(node_keys)
        row_list.append(jnp.repeat(node_perms, stride, axis=0))
    return jnp.stack(row_list).astype(jnp.int32)


def draw_subdomain_sizes(key, part):
    first_key, second_key = jax.random.split(jax.random.fold_in(key, 3))
    drawn = jax.random.randint(first_key, (SUBDOMAINS,), NMAX // 4, NMAX + 1)
    chosen = jax.random.randint(second_key, (), 0, SUBDOMAINS)
    return jnp.where(jnp.arange(SUBDOMAINS) == chosen, NMAX, drawn).astype(jnp.int32)


def draw_supernode_inverse(key, part):
    first_key, second_key = jax.random.split(jax.random.fold_in(key, 5))
    shape = (SUBDOMAINS * NB, BLK, BLK)
    spread = jnp.clip(0.1 * jax.random.normal(first_key, shape, jnp.float32), -0.6, 0.6)
    diagonal = jnp.exp(jax.random.uniform(second_key, (SUBDOMAINS * NB, BLK), jnp.float32, 0.0, 0.69))
    lower = jnp.tril(spread, -1) + diagonal[:, :, None] * jnp.eye(BLK, dtype=jnp.float32)
    return lower.astype(jnp.bfloat16)


def draw_top_fronts(key, part):
    first_key, second_key = jax.random.split(jax.random.fold_in(key, 7), 2)
    shape = (TOPS, S, S)
    basis = jnp.clip(jax.random.normal(first_key, shape, jnp.float32), -3.0, 3.0)
    gram = jnp.einsum('hik,hjk->hij', basis, basis, precision=lax.Precision.HIGHEST) * (12.0 / S)
    gram = 0.5 * (gram + jnp.swapaxes(gram, 1, 2))
    diagonal = jax.random.uniform(second_key, (TOPS, S), jnp.float32, 16.0, 32.0)
    identity = jnp.eye(S, dtype=jnp.float32)
    return gram + diagonal[:, :, None] * identity


def set_ends(values, stream_key, least, top_value):
    shape = values.shape
    index_at = [jax.random.randint(jax.random.fold_in(stream_key, axis), (), 0, shape[axis]) for axis in range(len(shape))]
    values = values.at[tuple(index_at)].set(least)
    longest = shape.index(max(shape))
    index_at[longest] = (index_at[longest] + 1) % shape[longest]
    return values.at[tuple(index_at)].set(top_value)


def setup_inputs(seed: int = 0) -> dict:
    splits = jax.random.split(jax.random.key(seed), 7)
    return {
        "coupling": draw_coupling(jax.random.fold_in(splits[6], 71), 0),
        "block_pattern": set_ends((jax.random.randint(splits[1], (SUBDOMAINS, NB, NBLK), 0, 2) < 1).astype(jnp.int32), jax.random.fold_in(splits[1], 1), 0, 1),
        "supernode_inverse": draw_supernode_inverse(jax.random.fold_in(splits[6], 71), 0),
        "subdomain_sizes": draw_subdomain_sizes(jax.random.fold_in(splits[6], 71), 0),
        "block_maps": draw_block_maps(jax.random.fold_in(splits[6], 71), 0),
        "top_fronts": draw_top_fronts(jax.random.fold_in(splits[6], 71), 0),
    }


def inverse_of(perm):
    positions = jnp.arange(NBLK)
    return jnp.sum(jnp.where(perm[:, None] == positions[None, :], positions[:, None], 0), axis=0).astype(jnp.int32)

def relabel(matrix, perm):
    inverse = inverse_of(perm)
    blocks = matrix.reshape(NBLK, BLK, NBLK, BLK)
    blocks = blocks[inverse][:, :, inverse]
    return blocks.reshape(S, S)

def partial_factor(front):
    l_top = jnp.linalg.cholesky(front[:PIV, :PIV])
    solved = jax.scipy.linalg.solve_triangular(l_top, front[:PIV, PIV:], lower=True)
    schur = front[PIV:, PIV:] - jnp.dot(solved.T, solved, precision=lax.Precision.HIGHEST)
    top_rows = jnp.concatenate([l_top, jnp.zeros((PIV, S - PIV), jnp.float32)], axis=1)
    bottom_rows = jnp.concatenate([solved.T, schur], axis=1)
    return jnp.concatenate([top_rows, bottom_rows], axis=0)

def reference(coupling, block_pattern, supernode_inverse, subdomain_sizes, block_maps, top_fronts):
    coupled = coupling.reshape(SUBDOMAINS, NB, BLK, NBLK, BLK)
    factors = supernode_inverse.reshape(SUBDOMAINS, NB, BLK, BLK)

    def leaf_update(index):
        masked = coupled[index] * block_pattern[index].astype(jnp.bfloat16)[:, None, :, None]
        solved = jnp.einsum('rab,rbc->rac', factors[index].astype(jnp.float32), masked.reshape(NB, BLK, S).astype(jnp.float32), precision=lax.Precision.HIGHEST)
        live_rows = (jnp.arange(NMAX) < subdomain_sizes[index]).reshape(NB, BLK, 1)
        rounded = jnp.where(live_rows, solved, 0.0).astype(jnp.bfloat16)
        rounded = lax.optimization_barrier(rounded)
        panel = rounded.astype(jnp.float32).reshape(NMAX, S)
        return -jnp.dot(panel.T, panel, precision=lax.Precision.HIGHEST)
    updates = lax.map(leaf_update, jnp.arange(SUBDOMAINS).astype(jnp.int32))
    for merge_level in range(LEVELS):
        stride = 2 ** merge_level
        node_perms = block_maps[merge_level, ::stride]
        updates = jax.vmap(relabel)(updates, node_perms)
        updates = updates.reshape(-1, 2, S, S)
        updates = updates[:, 0] + updates[:, 1]
    fronts = top_fronts + updates
    factored = jax.vmap(partial_factor)(fronts)
    return factored.reshape(TOPS * S, S)
```

```python
import jax
import jax.numpy as jnp
from jax import lax
from jax.experimental import pallas as pl
from jax.experimental.pallas import tpu as pltpu
from jax.sharding import PartitionSpec as P

NN = (((1,), (0,)), ((), ()))
NT = (((1,), (1,)), ((), ()))
TN = (((0,), (0,)), ((), ()))


def halves(x):
    hi = x.astype(jnp.bfloat16)
    return hi, (x - hi.astype(jnp.float32)).astype(jnp.bfloat16)


def mm(a, b, dims):
    return lax.dot_general(a, b, dims, preferred_element_type=jnp.float32)


def mm3(a, b, dims):
    ah, al = halves(a)
    bh, bl = halves(b)
    return mm(ah, bh, dims) + (mm(ah, bl, dims) + mm(al, bh, dims))


def finish_kernel(index_ref, a_ref, ai_ref, aj_ref, aij_ref, out_ref, y_ref, w_ref):
    n = a_ref.shape[0]
    b = ai_ref.shape[1]
    rows = lax.broadcasted_iota(jnp.int32, (n, n), 0)
    cols = lax.broadcasted_iota(jnp.int32, (n, n), 1)
    eye = (rows == cols).astype(jnp.float32)
    weight = jnp.where(rows > cols, 1.0, jnp.where(rows == cols, 0.5, 0.0))
    diag = jnp.sum(a_ref[...] * eye, axis=0, keepdims=True)
    y_ref[...] = eye * lax.rsqrt(diag)

    def rough(_, carry):
        ab = a_ref[...].astype(jnp.bfloat16)
        yb = y_ref[...].astype(jnp.bfloat16)
        g = mm(ab, yb, NT).astype(jnp.bfloat16)
        e = (mm(yb, g, NN) - eye) * weight
        y_ref[...] = y_ref[...] - mm(e.astype(jnp.bfloat16), yb, NN)
        return carry

    lax.fori_loop(0, 2, rough, 0)

    def fine(carry):
        step, _ = carry
        y = y_ref[...]
        e = (mm3(y, mm3(a_ref[...], y, NT), NN) - eye) * weight
        y_ref[...] = y - mm3(e, y, NN)
        return step + 1, jnp.max(jnp.abs(e))

    def unfinished(carry):
        step, worst = carry
        return (step < 40) & jnp.logical_not(worst < 2e-3)

    _, worst = lax.while_loop(unfinished, fine, (jnp.int32(0), jnp.float32(1.0)))

    @pl.when(jnp.logical_not(worst < 2e-3))
    def _():
        w_ref[...] = a_ref[...]
        y_ref[...] = eye
        row_id = lax.broadcasted_iota(jnp.int32, (n, 1), 0)
        col_id = lax.broadcasted_iota(jnp.int32, (1, n), 1)

        def eliminate(k, carry):
            w = w_ref[...]
            y = y_ref[...]
            row = w_ref[pl.ds(k, 1), :]
            scale = lax.rsqrt(jnp.sum(jnp.where(col_id == k, row, 0.0)))
            row = row * scale
            row_y = y_ref[pl.ds(k, 1), :] * scale
            col = jnp.sum(jnp.where(col_id == k, w, 0.0), axis=1, keepdims=True) * scale
            below = jnp.where(row_id > k, col, 0.0)
            here = row_id == k
            w_ref[...] = jnp.where(here, row, w - below * row)
            y_ref[...] = jnp.where(here, row_y, y - below * row_y)
            return carry

        lax.fori_loop(0, n, eliminate, 0)

    block_row = index_ref[0]
    block_col = index_ref[1]
    pivots = n // b
    y = y_ref[...]
    xi = mm3(y, ai_ref[...], NN)
    xj = mm3(y, aj_ref[...], NN)
    schur = aij_ref[...] - mm3(xi, xj, TN)
    w_ref[:, :b] = xi
    picked = w_ref[pl.ds(pl.multiple_of(jnp.minimum(block_col, pivots - 1) * b, b), b), :b].T
    r = block_row * b + lax.broadcasted_iota(jnp.int32, (b, b), 0)
    c = block_col * b + lax.broadcasted_iota(jnp.int32, (b, b), 1)
    left = jnp.where(c <= r, picked, 0.0)
    right = jnp.where(block_row >= pivots, schur, 0.0)
    out_ref[...] = jnp.where(block_col >= pivots, right, left)


def finish(index, a, ai, aj, aij):
    n = a.shape[0]
    b = ai.shape[1]
    vmem = pl.BlockSpec(memory_space=pltpu.VMEM)
    return pl.pallas_call(
        finish_kernel,
        out_shape=jax.ShapeDtypeStruct((b, b), jnp.float32),
        in_specs=[pl.BlockSpec(memory_space=pltpu.SMEM)] + [vmem] * 4,
        out_specs=vmem,
        scratch_shapes=[pltpu.VMEM((n, n), jnp.float32), pltpu.VMEM((n, n), jnp.float32)],
    )(index, a, ai, aj, aij)

PIV = 512


def from_partner(value, axis, bit):
    mask = 2**bit
    pairs = [(source, source ^ mask) for source in range(lax.axis_size(axis))]
    return lax.ppermute(value, axis, pairs)


def shards(coupling, block_pattern, supernode_inverse, subdomain_sizes, block_maps, top_fronts):
    leaf_count = lax.axis_size("leaf")
    leaf_index = lax.axis_index("leaf")
    front_index = lax.axis_index("front")
    levels = block_maps.shape[0]
    group_size = leaf_count // top_fronts.shape[0]
    row_count, col_count = coupling.shape
    block_size = supernode_inverse.shape[1]
    row_blocks = row_count // block_size
    front_order = top_fronts.shape[1]
    front_blocks = front_order // block_size
    masked = coupling.reshape(row_blocks, block_size, col_count) * block_pattern[0].astype(
        jnp.bfloat16
    ).reshape(row_blocks, 1, 1)
    solved = jnp.einsum(
        "rbc,rab->cra", masked, supernode_inverse, preferred_element_type=jnp.float32
    ).reshape(col_count, row_count)
    live_rows = jnp.arange(row_count)[None, :] < subdomain_sizes[0]
    panel = jnp.where(live_rows, solved, 0.0).astype(jnp.bfloat16)
    gathered = lax.all_gather(panel, "front", axis=0, tiled=False)
    positions = jnp.arange(front_blocks)
    composite = block_maps[0, 0]
    for merge_level in range(1, levels):
        level_map = block_maps[merge_level, 0]
        composite = jnp.sum(
            jnp.where(composite[:, None] == positions[None, :], level_map[None, :], 0), axis=1
        )
    inverse = jnp.sum(
        jnp.where(composite[:, None] == positions[None, :], positions[:, None], 0), axis=0
    )
    source = lax.dynamic_index_in_dim(inverse, front_index, 0, keepdims=False)
    selected = lax.dynamic_index_in_dim(gathered, source, 0, keepdims=False)
    products = jnp.einsum("bck,dk->bcd", gathered, selected, preferred_element_type=jnp.float32)
    summed = -products[inverse]
    for merge_level in range(levels):
        summed = summed + from_partner(summed.astype(jnp.bfloat16), "leaf", merge_level).astype(
            summed.dtype
        )
    top_index = leaf_index // group_size
    top = lax.dynamic_index_in_dim(top_fronts, top_index, 0, keepdims=False)
    column = top + summed.reshape(front_order, col_count)
    block_row = leaf_index % group_size
    strips = lax.all_gather(column[:PIV], "front", axis=0, tiled=False)
    pivots = PIV // block_size
    corner = strips[:pivots].transpose(1, 0, 2).reshape(PIV, PIV)
    own_row = lax.dynamic_index_in_dim(strips, block_row, 0, keepdims=False)
    own = lax.dynamic_slice_in_dim(column, block_row * block_size, block_size)
    index = jnp.stack([block_row, front_index]).astype(jnp.int32)
    return finish(index, corner, own_row, column[:PIV], own)


def solution(mesh):
    return jax.shard_map(
        shards,
        mesh=mesh,
        in_specs=(
            P("leaf", "front"),
            P("leaf", None, "front"),
            P("leaf", None, None),
            P("leaf"),
            P(None, "leaf", None),
            P(None, None, "front"),
        ),
        out_specs=P("leaf", "front"),
        check_vma=False,
    )
```

```python
import functools

import jax
import jax.numpy as jnp
from jax import lax
from jax.experimental import pallas as pl
from jax.experimental.pallas import tpu as pltpu
from jax.sharding import PartitionSpec as P

NN = (((1,), (0,)), ((), ()))
NT = (((1,), (1,)), ((), ()))
TN = (((0,), (0,)), ((), ()))


def halves(x):
    hi = x.astype(jnp.bfloat16)
    return hi, (x - hi.astype(jnp.float32)).astype(jnp.bfloat16)


def mm(a, b, dims):
    return lax.dot_general(a, b, dims, preferred_element_type=jnp.float32)


def mm3(a, b, dims):
    ah, al = halves(a)
    bh, bl = halves(b)
    return mm(ah, bh, dims) + (mm(ah, bl, dims) + mm(al, bh, dims))


def finish_kernel(index_ref, corner_ref, ai_ref, aj_ref, aij_ref, out_ref, a_ref, y_ref, w_ref):
    n = a_ref.shape[0]
    b = ai_ref.shape[1]
    for p in range(n // b):
        for q in range(p + 1):
            block = corner_ref[p, q]
            a_ref[p * b : (p + 1) * b, q * b : (q + 1) * b] = block
            if q < p:
                a_ref[q * b : (q + 1) * b, p * b : (p + 1) * b] = block.T
    rows = lax.broadcasted_iota(jnp.int32, (n, n), 0)
    cols = lax.broadcasted_iota(jnp.int32, (n, n), 1)
    eye = (rows == cols).astype(jnp.float32)
    weight = jnp.where(rows > cols, 1.0, jnp.where(rows == cols, 0.5, 0.0))
    diag = jnp.sum(a_ref[...] * eye, axis=0, keepdims=True)
    y_ref[...] = eye * lax.rsqrt(diag)

    def rough(_, carry):
        ab = a_ref[...].astype(jnp.bfloat16)
        yb = y_ref[...].astype(jnp.bfloat16)
        g = mm(ab, yb, NT).astype(jnp.bfloat16)
        e = (mm(yb, g, NN) - eye) * weight
        y_ref[...] = y_ref[...] - mm(e.astype(jnp.bfloat16), yb, NN)
        return carry

    lax.fori_loop(0, 2, rough, 0)

    def fine(carry):
        step, _ = carry
        y = y_ref[...]
        e = (mm3(y, mm3(a_ref[...], y, NT), NN) - eye) * weight
        y_ref[...] = y - mm3(e, y, NN)
        return step + 1, jnp.max(jnp.abs(e))

    def unfinished(carry):
        step, worst = carry
        return (step < 40) & jnp.logical_not(worst < 2e-3)

    _, worst = lax.while_loop(unfinished, fine, (jnp.int32(0), jnp.float32(1.0)))

    @pl.when(jnp.logical_not(worst < 2e-3))
    def _():
        w_ref[...] = a_ref[...]
        y_ref[...] = eye
        row_id = lax.broadcasted_iota(jnp.int32, (n, 1), 0)
        col_id = lax.broadcasted_iota(jnp.int32, (1, n), 1)

        def eliminate(k, carry):
            w = w_ref[...]
            y = y_ref[...]
            row = w_ref[pl.ds(k, 1), :]
            scale = lax.rsqrt(jnp.sum(jnp.where(col_id == k, row, 0.0)))
            row = row * scale
            row_y = y_ref[pl.ds(k, 1), :] * scale
            col = jnp.sum(jnp.where(col_id == k, w, 0.0), axis=1, keepdims=True) * scale
            below = jnp.where(row_id > k, col, 0.0)
            here = row_id == k
            w_ref[...] = jnp.where(here, row, w - below * row)
            y_ref[...] = jnp.where(here, row_y, y - below * row_y)
            return carry

        lax.fori_loop(0, n, eliminate, 0)

    block_row = index_ref[0]
    block_col = index_ref[1]
    pivots = n // b
    y = y_ref[...]
    xi = mm3(y, ai_ref[...], NN)
    xj = mm3(y, aj_ref[...], NN)
    schur = aij_ref[...] - mm3(xi, xj, TN)
    w_ref[:, :b] = xi
    picked = w_ref[pl.ds(pl.multiple_of(jnp.minimum(block_col, pivots - 1) * b, b), b), :b].T
    r = block_row * b + lax.broadcasted_iota(jnp.int32, (b, b), 0)
    c = block_col * b + lax.broadcasted_iota(jnp.int32, (b, b), 1)
    left = jnp.where(c <= r, picked, 0.0)
    right = jnp.where(block_row >= pivots, schur, 0.0)
    out_ref[...] = jnp.where(block_col >= pivots, right, left)


def finish(index, corner, ai, aj, aij):
    n, b = ai.shape
    vmem = pl.BlockSpec(memory_space=pltpu.VMEM)
    return pl.pallas_call(
        finish_kernel,
        out_shape=jax.ShapeDtypeStruct((b, b), jnp.float32),
        in_specs=[pl.BlockSpec(memory_space=pltpu.SMEM)] + [vmem] * 4,
        out_specs=vmem,
        scratch_shapes=[pltpu.VMEM((n, n), jnp.float32)] * 3,
    )(index, corner, ai, aj, aij)

PIV = 512
MESH = pl.DeviceIdType.MESH


def leaf_sum_kernel(
    group, chips, part_ref, top_ref, own_ref, corner_ref, row_ref, col_ref,
    got_slice, got_block, piece, pieces,
    slice_send, slice_recv, block_send, block_recv, piece_send, piece_recv,
    plus_send, minus_send, twin_send, item_recv,
):
    blocks, b, _ = part_ref.shape
    pivots = corner_ref.shape[0]
    rows = piece.shape[0]
    per_block = b // rows
    leaf = lax.axis_index("leaf")
    front = lax.axis_index("front")
    base = leaf // group * group
    me = leaf - base
    z = front // 2
    core = front % 2
    twin = z * 2 + 1 - core
    above = (z + 1) % chips * 2 + core
    below = (z + chips - 1) % chips * 2 + core

    def other(d):
        return (me + d) % group

    barrier = pltpu.get_barrier_semaphore()

    def greet(d, carry):
        pl.semaphore_signal(barrier, 1, device_id=(base + other(d), front), device_id_type=MESH)
        return carry

    lax.fori_loop(1, group, greet, 0)
    for side in (twin, above, below):
        pl.semaphore_signal(barrier, 1, device_id=(leaf, side), device_id_type=MESH)
    pl.semaphore_wait(barrier, group - 1 + 3)

    def slice_copy(to, src):
        return pltpu.make_async_remote_copy(
            part_ref.at[to // per_block, pl.ds(to % per_block * rows, rows), :],
            got_slice.at[src], slice_send.at[to], slice_recv.at[src],
            device_id=(base + to, front), device_id_type=MESH,
        )

    def block_copy(to, src):
        return pltpu.make_async_remote_copy(
            part_ref.at[to], got_block.at[src], block_send.at[to], block_recv.at[src],
            device_id=(base + to, front), device_id_type=MESH,
        )

    def piece_copy(to, src):
        return pltpu.make_async_remote_copy(
            piece, pieces.at[src], piece_send.at[to], piece_recv.at[src],
            device_id=(base + to, front), device_id_type=MESH,
        )

    inner = front >= pivots

    def send_slice(d, carry):
        slice_copy(other(d), me).start()
        return carry

    def send_block(d, carry):
        to = other(d)

        @pl.when(inner & (to >= pivots))
        def _():
            block_copy(to, me).start()

        return carry

    lax.fori_loop(1, group, send_slice, 0)
    lax.fori_loop(1, group, send_block, 0)

    def add_slice(d, total):
        src = other(d)
        slice_copy(src, src).wait_recv()
        return total + got_slice[src].astype(jnp.float32)

    mine = part_ref[me // per_block, pl.ds(pl.multiple_of(me % per_block * rows, rows), rows), :]
    total = lax.fori_loop(1, group, add_slice, mine.astype(jnp.float32))
    piece[...] = total.astype(jnp.bfloat16)
    pieces[me] = total.astype(jnp.bfloat16)

    def send_piece(d, carry):
        piece_copy(other(d), me).start()
        return carry

    lax.fori_loop(1, group, send_piece, 0)

    def wait_piece(d, carry):
        src = other(d)
        piece_copy(src, src).wait_recv()
        return carry

    lax.fori_loop(1, group, wait_piece, 0)
    for p in range(pivots):
        got = pieces[p * per_block : (p + 1) * per_block].astype(jnp.float32)
        col_ref[p] = top_ref[p * b : (p + 1) * b, :] + got.reshape(b, b)

    items = [(corner_ref, (p, q), q) for q in range(pivots) for p in range(q, pivots)]
    items += [(row_ref, (p,), me) for p in range(pivots)]

    def item_copy(n, sem, to):
        ref, at, _ = items[n]
        return pltpu.make_async_remote_copy(
            ref.at[at], ref.at[at], sem.at[n], item_recv.at[n],
            device_id=(leaf, to), device_id_type=MESH,
        )

    def roles(source):
        lane = core == source % 2
        far = (z + chips - source // 2) % chips
        half = chips // 2
        return lane, far, lane & (far < half), lane & ((far == 0) | (far > half + 1))

    for n, (ref, at, source) in enumerate(items):
        lane, far, plus, minus = roles(source)

        @pl.when(lane & (far == 0))
        def _():
            ref[at] = col_ref[at[0]]

        @pl.when(lane & (far != 0))
        def _():
            item_copy(n, twin_send, twin).wait_recv()

        @pl.when(plus)
        def _():
            item_copy(n, plus_send, above).start()

        @pl.when(minus)
        def _():
            item_copy(n, minus_send, below).start()

        @pl.when(lane)
        def _():
            item_copy(n, twin_send, twin).start()

    for n, (ref, at, source) in enumerate(items):
        lane, far, plus, minus = roles(source)

        @pl.when(jnp.logical_not(lane))
        def _():
            item_copy(n, twin_send, twin).wait_recv()

    own_ref[...] = part_ref[me].astype(jnp.float32)

    @pl.when(inner & (me >= pivots))
    def _():
        def add_block(d, carry):
            src = other(d)
            block_copy(src, src).wait_recv()
            own_ref[...] = own_ref[...] + got_block[src].astype(jnp.float32)
            return carry

        lax.fori_loop(1, group, add_block, 0)

    def drain(d, carry):
        to = other(d)
        slice_copy(to, me).wait_send()
        piece_copy(to, me).wait_send()

        @pl.when(inner & (to >= pivots))
        def _():
            block_copy(to, me).wait_send()

        return carry

    lax.fori_loop(1, group, drain, 0)
    for n, (ref, at, source) in enumerate(items):
        lane, far, plus, minus = roles(source)

        @pl.when(plus)
        def _():
            item_copy(n, plus_send, above).wait_send()

        @pl.when(minus)
        def _():
            item_copy(n, minus_send, below).wait_send()

        @pl.when(lane)
        def _():
            item_copy(n, twin_send, twin).wait_send()


def leaf_sum(part, top, group, chips):
    blocks, b, _ = part.shape
    pivots = PIV // b
    rows = PIV // group
    items = pivots * (pivots + 1) // 2 + pivots
    vmem = pl.BlockSpec(memory_space=pltpu.VMEM)
    dma = pltpu.SemaphoreType.DMA
    f32 = jnp.float32
    bf16 = jnp.bfloat16
    return pl.pallas_call(
        functools.partial(leaf_sum_kernel, group, chips),
        out_shape=(
            jax.ShapeDtypeStruct((b, b), f32),
            jax.ShapeDtypeStruct((pivots, pivots, b, b), f32),
            jax.ShapeDtypeStruct((pivots, b, b), f32),
            jax.ShapeDtypeStruct((pivots, b, b), f32),
        ),
        in_specs=[vmem] * 2,
        out_specs=[vmem] * 4,
        scratch_shapes=[
            pltpu.VMEM((group, rows, b), bf16),
            pltpu.VMEM((group, b, b), bf16),
            pltpu.VMEM((rows, b), bf16),
            pltpu.VMEM((group, rows, b), bf16),
        ]
        + [dma((group,))] * 6
        + [dma((items,))] * 4,
        compiler_params=pltpu.CompilerParams(collective_id=1, has_side_effects=True),
    )(part, top)


def shards(coupling, block_pattern, supernode_inverse, subdomain_sizes, block_maps, top_fronts):
    leaf_count = lax.axis_size("leaf")
    leaf_index = lax.axis_index("leaf")
    front_index = lax.axis_index("front")
    levels = block_maps.shape[0]
    group_size = leaf_count // top_fronts.shape[0]
    row_count, col_count = coupling.shape
    block_size = supernode_inverse.shape[1]
    row_blocks = row_count // block_size
    front_order = top_fronts.shape[1]
    front_blocks = front_order // block_size
    masked = coupling.reshape(row_blocks, block_size, col_count) * block_pattern[0].astype(
        jnp.bfloat16
    ).reshape(row_blocks, 1, 1)
    solved = jnp.einsum(
        "rbc,rab->cra", masked, supernode_inverse, preferred_element_type=jnp.float32
    ).reshape(col_count, row_count)
    live_rows = jnp.arange(row_count)[None, :] < subdomain_sizes[0]
    panel = jnp.where(live_rows, solved, 0.0).astype(jnp.bfloat16)
    gathered = lax.all_gather(panel, "front", axis=0, tiled=False)
    positions = jnp.arange(front_blocks)
    composite = block_maps[0, 0]
    for merge_level in range(1, levels):
        level_map = block_maps[merge_level, 0]
        composite = jnp.sum(
            jnp.where(composite[:, None] == positions[None, :], level_map[None, :], 0), axis=1
        )
    inverse = jnp.sum(
        jnp.where(composite[:, None] == positions[None, :], positions[:, None], 0), axis=0
    )
    source = lax.dynamic_index_in_dim(inverse, front_index, 0, keepdims=False)
    selected = lax.dynamic_index_in_dim(gathered, source, 0, keepdims=False)
    products = jnp.einsum("bck,dk->bcd", gathered, selected, preferred_element_type=jnp.float32)
    part = -products.astype(jnp.bfloat16)[inverse]
    top_index = leaf_index // group_size
    top = lax.dynamic_index_in_dim(top_fronts, top_index, 0, keepdims=False)
    block_row = leaf_index % group_size
    chips = lax.axis_size("front") // 2
    own, corner, own_row, own_col = leaf_sum(part, top[:PIV], group_size, chips)
    own = own + lax.dynamic_slice_in_dim(top, block_row * block_size, block_size)
    index = jnp.stack([block_row, front_index]).astype(jnp.int32)
    flat = (PIV, block_size)
    return finish(index, corner, own_row.reshape(flat), own_col.reshape(flat), own)


def solution(mesh):
    return jax.shard_map(
        shards,
        mesh=mesh,
        in_specs=(
            P("leaf", "front"),
            P("leaf", None, "front"),
            P("leaf", None, None),
            P("leaf"),
            P(None, "leaf", None),
            P(None, None, "front"),
        ),
        out_specs=P("leaf", "front"),
        check_vma=False,
    )
```

```python
import functools

import jax
import jax.numpy as jnp
from jax import lax
from jax.experimental import pallas as pl
from jax.experimental.pallas import tpu as pltpu
from jax.sharding import PartitionSpec as P

NN = (((1,), (0,)), ((), ()))
NT = (((1,), (1,)), ((), ()))
TN = (((0,), (0,)), ((), ()))


def halves(x):
    hi = x.astype(jnp.bfloat16)
    return hi, (x - hi.astype(jnp.float32)).astype(jnp.bfloat16)


def mm(a, b, dims):
    return lax.dot_general(a, b, dims, preferred_element_type=jnp.float32)


def mm3(a, b, dims):
    ah, al = halves(a)
    bh, bl = halves(b)
    return mm(ah, bh, dims) + (mm(ah, bl, dims) + mm(al, bh, dims))


def finish_kernel(group, corner_ref, ai_ref, aj_ref, aij_ref, out_ref, a_ref, y_ref, w_ref):
    n = a_ref.shape[0]
    b = ai_ref.shape[1]
    for p in range(n // b):
        for q in range(p + 1):
            block = corner_ref[p, q]
            a_ref[p * b : (p + 1) * b, q * b : (q + 1) * b] = block
            if q < p:
                a_ref[q * b : (q + 1) * b, p * b : (p + 1) * b] = block.T
    rows = lax.broadcasted_iota(jnp.int32, (n, n), 0)
    cols = lax.broadcasted_iota(jnp.int32, (n, n), 1)
    eye = (rows == cols).astype(jnp.float32)
    weight = jnp.where(rows > cols, 1.0, jnp.where(rows == cols, 0.5, 0.0))
    diag = jnp.sum(a_ref[...] * eye, axis=0, keepdims=True)
    y_ref[...] = eye * lax.rsqrt(diag)

    def rough(_, carry):
        ab = a_ref[...].astype(jnp.bfloat16)
        yb = y_ref[...].astype(jnp.bfloat16)
        g = mm(ab, yb, NT).astype(jnp.bfloat16)
        e = (mm(yb, g, NN) - eye) * weight
        y_ref[...] = y_ref[...] - mm(e.astype(jnp.bfloat16), yb, NN)
        return carry

    lax.fori_loop(0, 2, rough, 0)

    def fine(carry):
        step, _ = carry
        y = y_ref[...]
        e = (mm3(y, mm3(a_ref[...], y, NT), NN) - eye) * weight
        y_ref[...] = y - mm3(e, y, NN)
        return step + 1, jnp.max(jnp.abs(e))

    def unfinished(carry):
        step, worst = carry
        return (step < 40) & jnp.logical_not(worst < 2e-3)

    _, worst = lax.while_loop(unfinished, fine, (jnp.int32(0), jnp.float32(1.0)))

    @pl.when(jnp.logical_not(worst < 2e-3))
    def _():
        w_ref[...] = a_ref[...]
        y_ref[...] = eye
        row_id = lax.broadcasted_iota(jnp.int32, (n, 1), 0)
        col_id = lax.broadcasted_iota(jnp.int32, (1, n), 1)

        def eliminate(k, carry):
            w = w_ref[...]
            y = y_ref[...]
            row = w_ref[pl.ds(k, 1), :]
            scale = lax.rsqrt(jnp.sum(jnp.where(col_id == k, row, 0.0)))
            row = row * scale
            row_y = y_ref[pl.ds(k, 1), :] * scale
            col = jnp.sum(jnp.where(col_id == k, w, 0.0), axis=1, keepdims=True) * scale
            below = jnp.where(row_id > k, col, 0.0)
            here = row_id == k
            w_ref[...] = jnp.where(here, row, w - below * row)
            y_ref[...] = jnp.where(here, row_y, y - below * row_y)
            return carry

        lax.fori_loop(0, n, eliminate, 0)

    block_row = lax.axis_index("leaf") % group
    block_col = lax.axis_index("front")
    pivots = n // b
    y = y_ref[...]
    xi = mm3(y, ai_ref[...], NN)
    xj = mm3(y, aj_ref[...], NN)
    schur = aij_ref[...] - mm3(xi, xj, TN)
    w_ref[:, :b] = xi
    picked = w_ref[pl.ds(pl.multiple_of(jnp.minimum(block_col, pivots - 1) * b, b), b), :b].T
    r = block_row * b + lax.broadcasted_iota(jnp.int32, (b, b), 0)
    c = block_col * b + lax.broadcasted_iota(jnp.int32, (b, b), 1)
    left = jnp.where(c <= r, picked, 0.0)
    right = jnp.where(block_row >= pivots, schur, 0.0)
    out_ref[...] = jnp.where(block_col >= pivots, right, left)


def finish(group, corner, ai, aj, aij):
    n, b = ai.shape
    vmem = pl.BlockSpec(memory_space=pltpu.VMEM)
    return pl.pallas_call(
        functools.partial(finish_kernel, group),
        out_shape=jax.ShapeDtypeStruct((b, b), jnp.float32),
        in_specs=[vmem] * 4,
        out_specs=vmem,
        scratch_shapes=[pltpu.VMEM((n, n), jnp.float32)] * 3,
    )(corner, ai, aj, aij)

PIV = 512
MESH = pl.DeviceIdType.MESH


def assemble_kernel(
    group, chips, coupling_ref, factor_ref, tops_ref, pattern_ref, size_ref, map_ref,
    own_ref, corner_ref, row_ref, col_ref,
    bufs, acc, part_ref, top_ref, block_ref,
    got_slice, got_block, piece, pieces,
    chunk_recv, chunk_plus, chunk_minus, chunk_twin, top_sem,
    slice_send, slice_recv, block_send, block_recv, piece_send, piece_recv,
    plus_send, minus_send, twin_send, item_recv,
):
    blocks, b, _ = part_ref.shape
    pivots = corner_ref.shape[0]
    rows = piece.shape[0]
    per_block = b // rows
    leaf = lax.axis_index("leaf")
    front = lax.axis_index("front")
    base = leaf // group * group
    me = leaf - base
    z = front // 2
    core = front % 2
    twin = z * 2 + 1 - core
    above = (z + 1) % chips * 2 + core
    below = (z + chips - 1) % chips * 2 + core

    def other(d):
        return (me + d) % group

    top_copy = pltpu.make_async_copy(
        tops_ref.at[leaf // group, pl.ds(0, pivots * b), :], top_ref, top_sem.at[0]
    )
    own_copy = pltpu.make_async_copy(
        tops_ref.at[leaf // group, pl.ds(pl.multiple_of(me * b, b), b), :], block_ref, top_sem.at[1]
    )
    top_copy.start()
    own_copy.start()

    barrier = pltpu.get_barrier_semaphore()

    def greet(d, carry):
        pl.semaphore_signal(barrier, 1, device_id=(base + other(d), front), device_id_type=MESH)
        return carry

    lax.fori_loop(1, group, greet, 0)
    for side in (twin, above, below):
        pl.semaphore_signal(barrier, 1, device_id=(leaf, side), device_id_type=MESH)

    parts = len(bufs)
    supers = factor_ref.shape[0] // parts
    half = chips // 2
    row_id = lax.broadcasted_iota(jnp.int32, (b, b), 0)

    def solve(k):
        for r in range(supers):
            n = k * supers + r
            solved = mm(factor_ref[n], coupling_ref[n * b : (n + 1) * b, :], NN)
            live = jnp.where(row_id + n * b < size_ref[0], pattern_ref[0, n, 0], 0)
            kept = jnp.where(live > 0, solved, 0.0)
            bufs[k][front, :, r * b : (r + 1) * b] = kept.T.astype(jnp.bfloat16)

    def chunk_copy(k, block, sem, to):
        return pltpu.make_async_remote_copy(
            bufs[k].at[block], bufs[k].at[block], sem.at[k, block], chunk_recv.at[k, block],
            device_id=(leaf, to), device_id_type=MESH,
        )

    def block_at(d):
        return (z + d + chips) % chips * 2 + core

    def reach(k):
        return (half, half - 1) if k % 2 == 0 else (half - 1, half)

    def launch(k):
        chunk_copy(k, front, chunk_plus, above).start()
        chunk_copy(k, front, chunk_minus, below).start()
        chunk_copy(k, front, chunk_twin, twin).start()

    def relay(k, d):
        up, down = reach(k)
        if d <= up:
            block = block_at(-d)
            chunk_copy(k, block, chunk_plus, above).wait_recv()
            if d < up:
                chunk_copy(k, block, chunk_plus, above).start()
            chunk_copy(k, block, chunk_twin, twin).start()
        if d <= down:
            block = block_at(d)
            chunk_copy(k, block, chunk_minus, below).wait_recv()
            if d < down:
                chunk_copy(k, block, chunk_minus, below).start()
            chunk_copy(k, block, chunk_twin, twin).start()

    def twins(k):
        def one(n, carry):
            chunk_copy(k, n * 2 + 1 - core, chunk_twin, twin).wait_recv()
            return carry

        lax.fori_loop(0, chips, one, 0)

    places = []
    for n in range(blocks):
        place = n
        for level in range(map_ref.shape[0]):
            place = map_ref[level, 0, place]
        places.append(place)

    def source(at):
        found = [jnp.where(places[n] == at, n, 0) for n in range(blocks)]
        return functools.reduce(jnp.maximum, found)

    def gram(k):
        picked = bufs[k][source(front)]

        def one(n, carry):
            two = bufs[k][pl.ds(n * 2, 2)].reshape(2 * b, picked.shape[1])
            add = mm(two, picked, NT).reshape(2, b, b)
            if k == 0:
                acc[pl.ds(n * 2, 2)] = add
            else:
                acc[pl.ds(n * 2, 2)] = acc[pl.ds(n * 2, 2)] + add
            return carry

        lax.fori_loop(0, blocks // 2, one, 0, unroll=True)

    solve(0)
    pl.semaphore_wait(barrier, group - 1 + 3)
    launch(0)
    solve(1)
    launch(1)
    for k in range(2, parts):
        solve(k)
    for d in range(1, half + 1):
        for k in (0, 1):
            relay(k, d)
            if d == half - 1:
                launch(k + 2)
    twins(0)
    relay(2, 1)
    relay(3, 1)
    gram(0)
    relay(2, 2)
    relay(3, 2)
    twins(1)
    gram(1)
    for d in range(3, half + 1):
        relay(2, d)
        relay(3, d)
    twins(2)
    gram(2)
    twins(3)
    gram(3)
    for at in range(blocks):
        part_ref[at] = -acc[source(at)].astype(jnp.bfloat16)

    def slice_copy(to, src):
        return pltpu.make_async_remote_copy(
            part_ref.at[to // per_block, pl.ds(to % per_block * rows, rows), :],
            got_slice.at[src], slice_send.at[to], slice_recv.at[src],
            device_id=(base + to, front), device_id_type=MESH,
        )

    def block_copy(to, src):
        return pltpu.make_async_remote_copy(
            part_ref.at[to], got_block.at[src], block_send.at[to], block_recv.at[src],
            device_id=(base + to, front), device_id_type=MESH,
        )

    def piece_copy(to, src):
        return pltpu.make_async_remote_copy(
            piece, pieces.at[src], piece_send.at[to], piece_recv.at[src],
            device_id=(base + to, front), device_id_type=MESH,
        )

    inner = front >= pivots

    def send_slice(d, carry):
        slice_copy(other(d), me).start()
        return carry

    def send_block(d, carry):
        to = other(d)

        @pl.when(inner & (to >= pivots))
        def _():
            block_copy(to, me).start()

        return carry

    lax.fori_loop(1, group, send_slice, 0)
    lax.fori_loop(1, group, send_block, 0)

    def add_slice(d, total):
        src = other(d)
        slice_copy(src, src).wait_recv()
        return total + got_slice[src].astype(jnp.float32)

    mine = part_ref[me // per_block, pl.ds(pl.multiple_of(me % per_block * rows, rows), rows), :]
    total = lax.fori_loop(1, group, add_slice, mine.astype(jnp.float32))
    piece[...] = total.astype(jnp.bfloat16)
    pieces[me] = total.astype(jnp.bfloat16)

    def send_piece(d, carry):
        piece_copy(other(d), me).start()
        return carry

    lax.fori_loop(1, group, send_piece, 0)

    def wait_piece(d, carry):
        src = other(d)
        piece_copy(src, src).wait_recv()
        return carry

    lax.fori_loop(1, group, wait_piece, 0)
    top_copy.wait()
    own_copy.wait()
    for p in range(pivots):
        got = pieces[p * per_block : (p + 1) * per_block].astype(jnp.float32)
        col_ref[p] = top_ref[p * b : (p + 1) * b, :] + got.reshape(b, b)

    items = [(corner_ref, (p, q), q) for q in range(pivots) for p in range(q, pivots)]
    items += [(row_ref, (p,), me) for p in range(pivots)]

    def item_copy(n, sem, to):
        ref, at, _ = items[n]
        return pltpu.make_async_remote_copy(
            ref.at[at], ref.at[at], sem.at[n], item_recv.at[n],
            device_id=(leaf, to), device_id_type=MESH,
        )

    def roles(source):
        lane = core == source % 2
        far = (z + chips - source // 2) % chips
        half = chips // 2
        return lane, far, lane & (far < half), lane & ((far == 0) | (far > half + 1))

    for n, (ref, at, source) in enumerate(items):
        lane, far, plus, minus = roles(source)

        @pl.when(lane & (far == 0))
        def _():
            ref[at] = col_ref[at[0]]

        @pl.when(lane & (far != 0))
        def _():
            item_copy(n, twin_send, twin).wait_recv()

        @pl.when(plus)
        def _():
            item_copy(n, plus_send, above).start()

        @pl.when(minus)
        def _():
            item_copy(n, minus_send, below).start()

        @pl.when(lane)
        def _():
            item_copy(n, twin_send, twin).start()

    for n, (ref, at, source) in enumerate(items):
        lane, far, plus, minus = roles(source)

        @pl.when(jnp.logical_not(lane))
        def _():
            item_copy(n, twin_send, twin).wait_recv()

    own_ref[...] = block_ref[...] + part_ref[me].astype(jnp.float32)

    @pl.when(inner & (me >= pivots))
    def _():
        def add_block(d, carry):
            src = other(d)
            block_copy(src, src).wait_recv()
            own_ref[...] = own_ref[...] + got_block[src].astype(jnp.float32)
            return carry

        lax.fori_loop(1, group, add_block, 0)

    def drain(d, carry):
        to = other(d)
        slice_copy(to, me).wait_send()
        piece_copy(to, me).wait_send()

        @pl.when(inner & (to >= pivots))
        def _():
            block_copy(to, me).wait_send()

        return carry

    lax.fori_loop(1, group, drain, 0)
    for n, (ref, at, source) in enumerate(items):
        lane, far, plus, minus = roles(source)

        @pl.when(plus)
        def _():
            item_copy(n, plus_send, above).wait_send()

        @pl.when(minus)
        def _():
            item_copy(n, minus_send, below).wait_send()

        @pl.when(lane)
        def _():
            item_copy(n, twin_send, twin).wait_send()

    for k in range(parts):
        up, down = reach(k)
        for d in range(half + 1):
            if d < up:
                chunk_copy(k, block_at(-d), chunk_plus, above).wait_send()
            if d < down:
                chunk_copy(k, block_at(d), chunk_minus, below).wait_send()

        def sent(n, carry):
            chunk_copy(k, n * 2 + core, chunk_twin, twin).wait_send()
            return carry

        lax.fori_loop(0, chips, sent, 0)


def assemble(group, chips, coupling, factors, tops, pattern, sizes, maps):
    b = coupling.shape[1]
    blocks = tops.shape[1] // b
    pivots = PIV // b
    rows = PIV // group
    items = pivots * (pivots + 1) // 2 + pivots
    parts = 4
    vmem = pl.BlockSpec(memory_space=pltpu.VMEM)
    smem = pl.BlockSpec(memory_space=pltpu.SMEM)
    dma = pltpu.SemaphoreType.DMA
    f32 = jnp.float32
    bf16 = jnp.bfloat16
    return pl.pallas_call(
        functools.partial(assemble_kernel, group, chips),
        out_shape=(
            jax.ShapeDtypeStruct((b, b), f32),
            jax.ShapeDtypeStruct((pivots, pivots, b, b), f32),
            jax.ShapeDtypeStruct((pivots, b, b), f32),
            jax.ShapeDtypeStruct((pivots, b, b), f32),
        ),
        in_specs=[vmem] * 2 + [pl.BlockSpec(memory_space=pl.ANY)] + [smem] * 3,
        out_specs=[vmem] * 4,
        scratch_shapes=[
            [pltpu.VMEM((blocks, b, coupling.shape[0] // parts), bf16)] * parts,
            pltpu.VMEM((blocks, b, b), f32),
            pltpu.VMEM((blocks, b, b), bf16),
            pltpu.VMEM((PIV, b), f32),
            pltpu.VMEM((b, b), f32),
            pltpu.VMEM((group, rows, b), bf16),
            pltpu.VMEM((group, b, b), bf16),
            pltpu.VMEM((rows, b), bf16),
            pltpu.VMEM((group, rows, b), bf16),
        ]
        + [dma((parts, blocks))] * 4
        + [dma((2,))]
        + [dma((group,))] * 6
        + [dma((items,))] * 4,
        compiler_params=pltpu.CompilerParams(collective_id=1, has_side_effects=True),
    )(coupling, factors, tops, pattern, sizes, maps)


def shards(coupling, block_pattern, supernode_inverse, subdomain_sizes, block_maps, top_fronts):
    group = lax.axis_size("leaf") // top_fronts.shape[0]
    chips = lax.axis_size("front") // 2
    own, corner, own_row, own_col = assemble(
        group, chips, coupling, supernode_inverse, top_fronts,
        block_pattern, subdomain_sizes, block_maps,
    )
    flat = (PIV, coupling.shape[1])
    return finish(group, corner, own_row.reshape(flat), own_col.reshape(flat), own)


def solution(mesh):
    return jax.shard_map(
        shards,
        mesh=mesh,
        in_specs=(
            P("leaf", "front"),
            P("leaf", None, "front"),
            P("leaf", None, None),
            P("leaf"),
            P(None, "leaf", None),
            P(None, None, "front"),
        ),
        out_specs=P("leaf", "front"),
        check_vma=False,
    )
```

```python
import functools

import jax
import jax.numpy as jnp
from jax import lax
from jax.experimental import pallas as pl
from jax.experimental.pallas import tpu as pltpu
from jax.sharding import PartitionSpec as P

NN = (((1,), (0,)), ((), ()))
NT = (((1,), (1,)), ((), ()))
TN = (((0,), (0,)), ((), ()))


def halves(x):
    hi = x.astype(jnp.bfloat16)
    return hi, (x - hi.astype(jnp.float32)).astype(jnp.bfloat16)


def mm(a, b, dims):
    return lax.dot_general(a, b, dims, preferred_element_type=jnp.float32)


def mm3(a, b, dims):
    ah, al = halves(a)
    bh, bl = halves(b)
    return mm(ah, bh, dims) + (mm(ah, bl, dims) + mm(al, bh, dims))


def finish_kernel(group, corner_ref, ai_ref, aj_ref, aij_ref, out_ref, a_ref, y_ref, w_ref):
    n = a_ref.shape[0]
    b = ai_ref.shape[1]
    for p in range(n // b):
        for q in range(p + 1):
            block = corner_ref[p, q]
            a_ref[p * b : (p + 1) * b, q * b : (q + 1) * b] = block
            if q < p:
                a_ref[q * b : (q + 1) * b, p * b : (p + 1) * b] = block.T
    rows = lax.broadcasted_iota(jnp.int32, (n, n), 0)
    cols = lax.broadcasted_iota(jnp.int32, (n, n), 1)
    eye = (rows == cols).astype(jnp.float32)
    weight = jnp.where(rows > cols, 1.0, jnp.where(rows == cols, 0.5, 0.0))
    diag = jnp.sum(a_ref[...] * eye, axis=0, keepdims=True)
    y_ref[...] = eye * lax.rsqrt(diag)

    def rough(_, carry):
        ab = a_ref[...].astype(jnp.bfloat16)
        yb = y_ref[...].astype(jnp.bfloat16)
        g = mm(ab, yb, NT).astype(jnp.bfloat16)
        e = (mm(yb, g, NN) - eye) * weight
        y_ref[...] = y_ref[...] - mm(e.astype(jnp.bfloat16), yb, NN)
        return carry

    lax.fori_loop(0, 2, rough, 0)

    def fine(carry):
        step, _ = carry
        y = y_ref[...]
        e = (mm3(y, mm3(a_ref[...], y, NT), NN) - eye) * weight
        y_ref[...] = y - mm3(e, y, NN)
        return step + 1, jnp.max(jnp.abs(e))

    def unfinished(carry):
        step, worst = carry
        return (step < 40) & jnp.logical_not(worst < 2e-3)

    _, worst = lax.while_loop(unfinished, fine, (jnp.int32(0), jnp.float32(1.0)))

    @pl.when(jnp.logical_not(worst < 2e-3))
    def _():
        w_ref[...] = a_ref[...]
        y_ref[...] = eye
        row_id = lax.broadcasted_iota(jnp.int32, (n, 1), 0)
        col_id = lax.broadcasted_iota(jnp.int32, (1, n), 1)

        def eliminate(k, carry):
            w = w_ref[...]
            y = y_ref[...]
            row = w_ref[pl.ds(k, 1), :]
            scale = lax.rsqrt(jnp.sum(jnp.where(col_id == k, row, 0.0)))
            row = row * scale
            row_y = y_ref[pl.ds(k, 1), :] * scale
            col = jnp.sum(jnp.where(col_id == k, w, 0.0), axis=1, keepdims=True) * scale
            below = jnp.where(row_id > k, col, 0.0)
            here = row_id == k
            w_ref[...] = jnp.where(here, row, w - below * row)
            y_ref[...] = jnp.where(here, row_y, y - below * row_y)
            return carry

        lax.fori_loop(0, n, eliminate, 0)

    block_row = lax.axis_index("leaf") % group
    block_col = lax.axis_index("front")
    pivots = n // b
    y = y_ref[...]
    xi = mm3(y, ai_ref[...], NN)
    xj = mm3(y, aj_ref[...], NN)
    schur = aij_ref[...] - mm3(xi, xj, TN)
    w_ref[:, :b] = xi
    picked = w_ref[pl.ds(pl.multiple_of(jnp.minimum(block_col, pivots - 1) * b, b), b), :b].T
    r = block_row * b + lax.broadcasted_iota(jnp.int32, (b, b), 0)
    c = block_col * b + lax.broadcasted_iota(jnp.int32, (b, b), 1)
    left = jnp.where(c <= r, picked, 0.0)
    right = jnp.where(block_row >= pivots, schur, 0.0)
    out_ref[...] = jnp.where(block_col >= pivots, right, left)


def finish(group, corner, ai, aj, aij):
    n, b = ai.shape
    vmem = pl.BlockSpec(memory_space=pltpu.VMEM)
    return pl.pallas_call(
        functools.partial(finish_kernel, group),
        out_shape=jax.ShapeDtypeStruct((b, b), jnp.float32),
        in_specs=[vmem] * 4,
        out_specs=vmem,
        scratch_shapes=[pltpu.VMEM((n, n), jnp.float32)] * 3,
    )(corner, ai, aj, aij)

PIV = 512
MESH = pl.DeviceIdType.MESH


def assemble_kernel(
    group, chips, coupling_ref, factor_ref, tops_ref, pattern_ref, size_ref, map_ref,
    own_ref, corner_ref, row_ref, col_ref,
    bufs, acc, part_ref, top_ref, block_ref,
    got_slice, got_block, piece, pieces,
    chunk_recv, chunk_plus, chunk_minus, chunk_twin, top_sem,
    slice_send, slice_recv, block_send, block_recv, piece_send, piece_recv,
    plus_send, minus_send, twin_send, item_recv,
):
    blocks, b, _ = part_ref.shape
    pivots = corner_ref.shape[0]
    rows = piece.shape[0]
    per_block = b // rows
    leaf = lax.axis_index("leaf")
    front = lax.axis_index("front")
    base = leaf // group * group
    me = leaf - base
    z = front // 2
    core = front % 2
    twin = z * 2 + 1 - core
    above = (z + 1) % chips * 2 + core
    below = (z + chips - 1) % chips * 2 + core

    def other(d):
        return (me + d) % group

    top_copy = pltpu.make_async_copy(
        tops_ref.at[leaf // group, pl.ds(0, pivots * b), :], top_ref, top_sem.at[0]
    )
    own_copy = pltpu.make_async_copy(
        tops_ref.at[leaf // group, pl.ds(pl.multiple_of(me * b, b), b), :], block_ref, top_sem.at[1]
    )
    top_copy.start()
    own_copy.start()

    barrier = pltpu.get_barrier_semaphore()

    def greet(d, carry):
        pl.semaphore_signal(barrier, 1, device_id=(base + other(d), front), device_id_type=MESH)
        return carry

    lax.fori_loop(1, group, greet, 0)
    for side in (twin, above, below):
        pl.semaphore_signal(barrier, 1, device_id=(leaf, side), device_id_type=MESH)

    parts = len(bufs)
    supers = factor_ref.shape[0] // parts
    half = chips // 2
    row_id = lax.broadcasted_iota(jnp.int32, (b, b), 0)

    def solve(k):
        for r in range(supers):
            n = k * supers + r
            solved = mm(factor_ref[n], coupling_ref[n * b : (n + 1) * b, :], NN)
            live = jnp.where(row_id + n * b < size_ref[0], pattern_ref[0, n, 0], 0)
            kept = jnp.where(live > 0, solved, 0.0)
            bufs[k][front, :, r * b : (r + 1) * b] = kept.T.astype(jnp.bfloat16)

    def chunk_copy(k, block, sem, to):
        return pltpu.make_async_remote_copy(
            bufs[k].at[block], bufs[k].at[block], sem.at[k, block], chunk_recv.at[k, block],
            device_id=(leaf, to), device_id_type=MESH,
        )

    def block_at(d):
        return (z + d + chips) % chips * 2 + core

    def reach(k):
        return (half, half - 1) if k % 2 == 0 else (half - 1, half)

    def launch(k):
        chunk_copy(k, front, chunk_plus, above).start()
        chunk_copy(k, front, chunk_minus, below).start()
        chunk_copy(k, front, chunk_twin, twin).start()

    def relay(k, d):
        up, down = reach(k)
        if d <= up:
            block = block_at(-d)
            chunk_copy(k, block, chunk_plus, above).wait_recv()
            if d < up:
                chunk_copy(k, block, chunk_plus, above).start()
            chunk_copy(k, block, chunk_twin, twin).start()
        if d <= down:
            block = block_at(d)
            chunk_copy(k, block, chunk_minus, below).wait_recv()
            if d < down:
                chunk_copy(k, block, chunk_minus, below).start()
            chunk_copy(k, block, chunk_twin, twin).start()

    def twins(k):
        def one(n, carry):
            chunk_copy(k, n * 2 + 1 - core, chunk_twin, twin).wait_recv()
            return carry

        lax.fori_loop(0, chips, one, 0)

    places = []
    for n in range(blocks):
        place = n
        for level in range(map_ref.shape[0]):
            place = map_ref[level, 0, place]
        places.append(place)

    def source(at):
        found = [jnp.where(places[n] == at, n, 0) for n in range(blocks)]
        return functools.reduce(jnp.maximum, found)

    def gram(k):
        picked = bufs[k][source(front)]

        def one(n, carry):
            two = bufs[k][pl.ds(n * 2, 2)].reshape(2 * b, picked.shape[1])
            add = mm(two, picked, NT).reshape(2, b, b)
            if k == 0:
                acc[pl.ds(n * 2, 2)] = add
            else:
                acc[pl.ds(n * 2, 2)] = acc[pl.ds(n * 2, 2)] + add
            return carry

        lax.fori_loop(0, blocks // 2, one, 0, unroll=True)

    solve(0)
    pl.semaphore_wait(barrier, group - 1 + 3)
    launch(0)
    solve(1)
    launch(1)
    for k in range(2, parts):
        solve(k)
    for d in range(1, half + 1):
        for k in (0, 1):
            relay(k, d)
            if d == half - 1:
                launch(k + 2)
    twins(0)
    relay(2, 1)
    relay(3, 1)
    gram(0)
    relay(2, 2)
    relay(3, 2)
    twins(1)
    gram(1)
    for d in range(3, half + 1):
        relay(2, d)
        relay(3, d)
    twins(2)
    gram(2)
    twins(3)
    gram(3)
    for at in range(blocks):
        part_ref[at] = -acc[source(at)].astype(jnp.bfloat16)

    def slice_copy(to, src):
        return pltpu.make_async_remote_copy(
            part_ref.at[to // per_block, pl.ds(to % per_block * rows, rows), :],
            got_slice.at[src], slice_send.at[to], slice_recv.at[src],
            device_id=(base + to, front), device_id_type=MESH,
        )

    def block_copy(to, src):
        return pltpu.make_async_remote_copy(
            part_ref.at[to], got_block.at[src], block_send.at[to], block_recv.at[src],
            device_id=(base + to, front), device_id_type=MESH,
        )

    def piece_copy(to, src):
        return pltpu.make_async_remote_copy(
            piece, pieces.at[src], piece_send.at[to], piece_recv.at[src],
            device_id=(base + to, front), device_id_type=MESH,
        )

    inner = front >= pivots

    def send_slice(d, carry):
        slice_copy(other(d), me).start()
        return carry

    def send_block(d, carry):
        to = other(d)

        @pl.when(inner & (to >= pivots))
        def _():
            block_copy(to, me).start()

        return carry

    lax.fori_loop(1, group, send_slice, 0)

    def add_slice(d, total):
        src = other(d)
        slice_copy(src, src).wait_recv()
        return total + got_slice[src].astype(jnp.float32)

    mine = part_ref[me // per_block, pl.ds(pl.multiple_of(me % per_block * rows, rows), rows), :]
    total = lax.fori_loop(1, group, add_slice, mine.astype(jnp.float32))
    piece[...] = total.astype(jnp.bfloat16)
    pieces[me] = total.astype(jnp.bfloat16)

    def send_piece(d, carry):
        piece_copy(other(d), me).start()
        return carry

    lax.fori_loop(1, group, send_piece, 0)
    lax.fori_loop(1, group, send_block, 0)

    def wait_piece(d, carry):
        src = other(d)
        piece_copy(src, src).wait_recv()
        return carry

    lax.fori_loop(1, group, wait_piece, 0)
    top_copy.wait()
    own_copy.wait()
    for p in range(pivots):
        got = pieces[p * per_block : (p + 1) * per_block].astype(jnp.float32)
        col_ref[p] = top_ref[p * b : (p + 1) * b, :] + got.reshape(b, b)

    items = [(corner_ref, (p, q), q) for q in range(pivots) for p in range(q, pivots)]
    items += [(row_ref, (p,), me) for p in range(pivots)]

    def item_copy(n, sem, to):
        ref, at, _ = items[n]
        return pltpu.make_async_remote_copy(
            ref.at[at], ref.at[at], sem.at[n], item_recv.at[n],
            device_id=(leaf, to), device_id_type=MESH,
        )

    def roles(source):
        lane = core == source % 2
        far = (z + chips - source // 2) % chips
        half = chips // 2
        return lane, far, lane & (far < half), lane & ((far == 0) | (far > half + 1))

    for n, (ref, at, source) in enumerate(items):
        lane, far, plus, minus = roles(source)

        @pl.when(lane & (far == 0))
        def _():
            ref[at] = col_ref[at[0]]
            item_copy(n, plus_send, above).start()
            item_copy(n, minus_send, below).start()
            item_copy(n, twin_send, twin).start()

    def hop(t, carry):
        for n, (ref, at, source) in enumerate(items):
            lane, far, plus, minus = roles(source)

            @pl.when(lane & (jnp.minimum(far, chips - far) == t))
            def _():
                item_copy(n, twin_send, twin).wait_recv()

                @pl.when(plus)
                def _():
                    item_copy(n, plus_send, above).start()

                @pl.when(minus)
                def _():
                    item_copy(n, minus_send, below).start()

                item_copy(n, twin_send, twin).start()

        return carry

    lax.fori_loop(1, chips // 2 + 1, hop, 0)

    for n, (ref, at, source) in enumerate(items):
        lane, far, plus, minus = roles(source)

        @pl.when(jnp.logical_not(lane))
        def _():
            item_copy(n, twin_send, twin).wait_recv()

    own_ref[...] = block_ref[...] + part_ref[me].astype(jnp.float32)

    @pl.when(inner & (me >= pivots))
    def _():
        def add_block(d, carry):
            src = other(d)
            block_copy(src, src).wait_recv()
            own_ref[...] = own_ref[...] + got_block[src].astype(jnp.float32)
            return carry

        lax.fori_loop(1, group, add_block, 0)

    def drain(d, carry):
        to = other(d)
        slice_copy(to, me).wait_send()
        piece_copy(to, me).wait_send()

        @pl.when(inner & (to >= pivots))
        def _():
            block_copy(to, me).wait_send()

        return carry

    lax.fori_loop(1, group, drain, 0)
    for n, (ref, at, source) in enumerate(items):
        lane, far, plus, minus = roles(source)

        @pl.when(plus)
        def _():
            item_copy(n, plus_send, above).wait_send()

        @pl.when(minus)
        def _():
            item_copy(n, minus_send, below).wait_send()

        @pl.when(lane)
        def _():
            item_copy(n, twin_send, twin).wait_send()

    for k in range(parts):
        up, down = reach(k)
        for d in range(half + 1):
            if d < up:
                chunk_copy(k, block_at(-d), chunk_plus, above).wait_send()
            if d < down:
                chunk_copy(k, block_at(d), chunk_minus, below).wait_send()

        def sent(n, carry):
            chunk_copy(k, n * 2 + core, chunk_twin, twin).wait_send()
            return carry

        lax.fori_loop(0, chips, sent, 0)


def assemble(group, chips, coupling, factors, tops, pattern, sizes, maps):
    b = coupling.shape[1]
    blocks = tops.shape[1] // b
    pivots = PIV // b
    rows = PIV // group
    items = pivots * (pivots + 1) // 2 + pivots
    parts = 4
    vmem = pl.BlockSpec(memory_space=pltpu.VMEM)
    smem = pl.BlockSpec(memory_space=pltpu.SMEM)
    dma = pltpu.SemaphoreType.DMA
    f32 = jnp.float32
    bf16 = jnp.bfloat16
    return pl.pallas_call(
        functools.partial(assemble_kernel, group, chips),
        out_shape=(
            jax.ShapeDtypeStruct((b, b), f32),
            jax.ShapeDtypeStruct((pivots, pivots, b, b), f32),
            jax.ShapeDtypeStruct((pivots, b, b), f32),
            jax.ShapeDtypeStruct((pivots, b, b), f32),
        ),
        in_specs=[vmem] * 2 + [pl.BlockSpec(memory_space=pl.ANY)] + [smem] * 3,
        out_specs=[vmem] * 4,
        scratch_shapes=[
            [pltpu.VMEM((blocks, b, coupling.shape[0] // parts), bf16)] * parts,
            pltpu.VMEM((blocks, b, b), f32),
            pltpu.VMEM((blocks, b, b), bf16),
            pltpu.VMEM((PIV, b), f32),
            pltpu.VMEM((b, b), f32),
            pltpu.VMEM((group, rows, b), bf16),
            pltpu.VMEM((group, b, b), bf16),
            pltpu.VMEM((rows, b), bf16),
            pltpu.VMEM((group, rows, b), bf16),
        ]
        + [dma((parts, blocks))] * 4
        + [dma((2,))]
        + [dma((group,))] * 6
        + [dma((items,))] * 4,
        compiler_params=pltpu.CompilerParams(collective_id=1, has_side_effects=True),
    )(coupling, factors, tops, pattern, sizes, maps)


def shards(coupling, block_pattern, supernode_inverse, subdomain_sizes, block_maps, top_fronts):
    group = lax.axis_size("leaf") // top_fronts.shape[0]
    chips = lax.axis_size("front") // 2
    own, corner, own_row, own_col = assemble(
        group, chips, coupling, supernode_inverse, top_fronts,
        block_pattern, subdomain_sizes, block_maps,
    )
    flat = (PIV, coupling.shape[1])
    return finish(group, corner, own_row.reshape(flat), own_col.reshape(flat), own)


def solution(mesh):
    return jax.shard_map(
        shards,
        mesh=mesh,
        in_specs=(
            P("leaf", "front"),
            P("leaf", None, "front"),
            P("leaf", None, None),
            P("leaf"),
            P(None, "leaf", None),
            P(None, None, "front"),
        ),
        out_specs=P("leaf", "front"),
        check_vma=False,
    )
```

```python
import functools

import jax
import jax.numpy as jnp
from jax import lax
from jax.experimental import pallas as pl
from jax.experimental.pallas import tpu as pltpu
from jax.sharding import PartitionSpec as P

NN = (((1,), (0,)), ((), ()))
NT = (((1,), (1,)), ((), ()))
TN = (((0,), (0,)), ((), ()))


def halves(x):
    hi = x.astype(jnp.bfloat16)
    return hi, (x - hi.astype(jnp.float32)).astype(jnp.bfloat16)


def mm(a, b, dims):
    return lax.dot_general(a, b, dims, preferred_element_type=jnp.float32)


def mm3(a, b, dims):
    ah, al = halves(a)
    bh, bl = halves(b)
    return mm(ah, bh, dims) + (mm(ah, bl, dims) + mm(al, bh, dims))


def finish_kernel(group, corner_ref, ai_ref, aj_ref, aij_ref, out_ref, a_ref, y_ref, w_ref, ah_ref, al_ref):
    n = a_ref.shape[0]
    h = n // 2
    b = ai_ref.shape[1]
    for p in range(n // b):
        for q in range(p + 1):
            block = corner_ref[p, q]
            a_ref[p * b : (p + 1) * b, q * b : (q + 1) * b] = block
            if q < p:
                a_ref[q * b : (q + 1) * b, p * b : (p + 1) * b] = block.T
    rows = lax.broadcasted_iota(jnp.int32, (h, h), 0)
    cols = lax.broadcasted_iota(jnp.int32, (h, h), 1)
    eye = (rows == cols).astype(jnp.float32)
    weight = jnp.where(rows > cols, 1.0, jnp.where(rows == cols, 0.5, 0.0))
    for at in (0, h):
        diag = jnp.sum(a_ref[at : at + h, at : at + h] * eye, axis=0, keepdims=True)
        y_ref[at : at + h, at : at + h] = eye * lax.rsqrt(diag)
        y_ref[at : at + h, h - at : n - at] = jnp.zeros((h, h), jnp.float32)
    ah, al = halves(a_ref[...])
    ah_ref[...] = ah
    al_ref[...] = al

    def rough(_, carry):
        ab = ah_ref[...]
        y1 = y_ref[:h, :h].astype(jnp.bfloat16)
        y2 = y_ref[h:, :].astype(jnp.bfloat16)
        g1 = mm(ab[:, :h], y1, NT).astype(jnp.bfloat16)
        g2 = mm(ab, y2, NT).astype(jnp.bfloat16)
        e1 = (mm(y1, g1[:h], NN) - eye) * weight
        e21 = mm(y2, g1, NN)
        e22 = (mm(y2, g2, NN) - eye) * weight
        e1 = e1.astype(jnp.bfloat16)
        e21 = e21.astype(jnp.bfloat16)
        e22 = e22.astype(jnp.bfloat16)
        y_ref[:h, :h] = y_ref[:h, :h] - mm(e1, y1, NN)
        y_ref[h:, :h] = y_ref[h:, :h] - mm(e21, y1, NN) - mm(e22, y2[:, :h], NN)
        y_ref[h:, h:] = y_ref[h:, h:] - mm(e22, y2[:, h:], NN)
        return carry

    lax.fori_loop(0, 2, rough, 0)

    def pair(x, y, dims):
        (xh, xl), (yh, yl) = x, y
        return mm(xh, yh, dims) + (mm(xh, yl, dims) + mm(xl, yh, dims))

    def fine(carry):
        step, _ = carry
        y1 = halves(y_ref[:h, :h])
        y2 = halves(y_ref[h:, :])
        y21 = (y2[0][:, :h], y2[1][:, :h])
        y22 = (y2[0][:, h:], y2[1][:, h:])
        g1 = halves(pair((ah_ref[:, :h], al_ref[:, :h]), y1, NT))
        g2 = halves(pair((ah_ref[...], al_ref[...]), y2, NT))
        e1 = (pair(y1, (g1[0][:h], g1[1][:h]), NN) - eye) * weight
        e21 = pair(y2, g1, NN)
        e22 = (pair(y2, g2, NN) - eye) * weight
        worst = jnp.maximum(jnp.max(jnp.abs(e1)), jnp.maximum(jnp.max(jnp.abs(e21)), jnp.max(jnp.abs(e22))))
        e1 = halves(e1)
        e21 = halves(e21)
        e22 = halves(e22)
        y_ref[:h, :h] = y_ref[:h, :h] - pair(e1, y1, NN)
        y_ref[h:, :h] = y_ref[h:, :h] - (pair(e21, y1, NN) + pair(e22, y21, NN))
        y_ref[h:, h:] = y_ref[h:, h:] - pair(e22, y22, NN)
        return step + 1, worst

    def unfinished(carry):
        step, worst = carry
        return (step < 40) & jnp.logical_not(worst < LIMIT)

    _, worst = lax.while_loop(unfinished, fine, (jnp.int32(0), jnp.float32(1.0)))

    @pl.when(jnp.logical_not(worst < LIMIT))
    def _():
        row_id = lax.broadcasted_iota(jnp.int32, (n, 1), 0)
        col_id = lax.broadcasted_iota(jnp.int32, (1, n), 1)
        w_ref[...] = a_ref[...]
        y_ref[...] = jnp.where(row_id == col_id, 1.0, 0.0)

        def eliminate(k, carry):
            w = w_ref[...]
            y = y_ref[...]
            row = w_ref[pl.ds(k, 1), :]
            scale = lax.rsqrt(jnp.sum(jnp.where(col_id == k, row, 0.0)))
            row = row * scale
            row_y = y_ref[pl.ds(k, 1), :] * scale
            col = jnp.sum(jnp.where(col_id == k, w, 0.0), axis=1, keepdims=True) * scale
            below = jnp.where(row_id > k, col, 0.0)
            here = row_id == k
            w_ref[...] = jnp.where(here, row, w - below * row)
            y_ref[...] = jnp.where(here, row_y, y - below * row_y)
            return carry

        lax.fori_loop(0, n, eliminate, 0)

    block_row = lax.axis_index("leaf") % group
    block_col = lax.axis_index("front")
    pivots = n // b
    y = halves(y_ref[...])
    xi = pair(y, halves(ai_ref[...]), NN)
    xj = pair(y, halves(aj_ref[...]), NN)
    schur = aij_ref[...] - mm3(xi, xj, TN)
    w_ref[:, :b] = xi
    picked = w_ref[pl.ds(pl.multiple_of(jnp.minimum(block_col, pivots - 1) * b, b), b), :b].T
    r = block_row * b + lax.broadcasted_iota(jnp.int32, (b, b), 0)
    c = block_col * b + lax.broadcasted_iota(jnp.int32, (b, b), 1)
    left = jnp.where(c <= r, picked, 0.0)
    right = jnp.where(block_row >= pivots, schur, 0.0)
    out_ref[...] = jnp.where(block_col >= pivots, right, left)


def finish(group, corner, ai, aj, aij):
    n, b = ai.shape
    vmem = pl.BlockSpec(memory_space=pltpu.VMEM)
    return pl.pallas_call(
        functools.partial(finish_kernel, group),
        out_shape=jax.ShapeDtypeStruct((b, b), jnp.float32),
        in_specs=[vmem] * 4,
        out_specs=vmem,
        scratch_shapes=[pltpu.VMEM((n, n), jnp.float32)] * 3 + [pltpu.VMEM((n, n), jnp.bfloat16)] * 2,
    )(corner, ai, aj, aij)

PIV = 512
LIMIT = 2e-3
MESH = pl.DeviceIdType.MESH


def assemble_kernel(
    group, chips, coupling_ref, factor_ref, tops_ref, pattern_ref, size_ref, map_ref,
    own_ref, corner_ref, row_ref, col_ref,
    bufs, acc, part_ref, top_ref, block_ref,
    got_slice, got_block, piece, pieces,
    chunk_recv, chunk_plus, chunk_minus, chunk_twin, top_sem,
    slice_send, slice_recv, block_send, block_recv, piece_send, piece_recv,
    corner_top, row_top, corner_sum, row_sum,
    top_send, top_recv, sum_send, sum_recv,
):
    blocks, b, _ = part_ref.shape
    pivots = corner_ref.shape[0]
    rows = piece.shape[0]
    per_block = b // rows
    leaf = lax.axis_index("leaf")
    front = lax.axis_index("front")
    base = leaf // group * group
    me = leaf - base
    z = front // 2
    core = front % 2
    twin = z * 2 + 1 - core
    above = (z + 1) % chips * 2 + core
    below = (z + chips - 1) % chips * 2 + core

    def other(d):
        return (me + d) % group

    top_copy = pltpu.make_async_copy(
        tops_ref.at[leaf // group, pl.ds(0, pivots * b), :], top_ref, top_sem.at[0]
    )
    own_copy = pltpu.make_async_copy(
        tops_ref.at[leaf // group, pl.ds(pl.multiple_of(me * b, b), b), :], block_ref, top_sem.at[1]
    )
    top_copy.start()
    own_copy.start()

    barrier = pltpu.get_barrier_semaphore()

    def greet(d, carry):
        pl.semaphore_signal(barrier, 1, device_id=(base + other(d), front), device_id_type=MESH)
        return carry

    lax.fori_loop(1, group, greet, 0)
    for side in (twin, above, below):
        pl.semaphore_signal(barrier, 1, device_id=(leaf, side), device_id_type=MESH)

    parts = len(bufs)
    supers = factor_ref.shape[0] // parts
    half = chips // 2
    row_id = lax.broadcasted_iota(jnp.int32, (b, b), 0)

    def solve(k):
        for r in range(supers):
            n = k * supers + r
            solved = mm(factor_ref[n], coupling_ref[n * b : (n + 1) * b, :], NN)
            live = jnp.where(row_id + n * b < size_ref[0], pattern_ref[0, n, 0], 0)
            kept = jnp.where(live > 0, solved, 0.0)
            bufs[k][front, :, r * b : (r + 1) * b] = kept.T.astype(jnp.bfloat16)

    def chunk_copy(k, block, sem, to):
        return pltpu.make_async_remote_copy(
            bufs[k].at[block], bufs[k].at[block], sem.at[k, block], chunk_recv.at[k, block],
            device_id=(leaf, to), device_id_type=MESH,
        )

    def block_at(d):
        return (z + d + chips) % chips * 2 + core

    def reach(k):
        return (half, half - 1) if k % 2 else (half - 1, half)

    def launch(k):
        chunk_copy(k, front, chunk_plus, above).start()
        chunk_copy(k, front, chunk_minus, below).start()
        chunk_copy(k, front, chunk_twin, twin).start()

    def relay(k, d):
        up, down = reach(k)
        if d <= up:
            block = block_at(-d)
            chunk_copy(k, block, chunk_plus, above).wait_recv()
            if d < up:
                chunk_copy(k, block, chunk_plus, above).start()
            chunk_copy(k, block, chunk_twin, twin).start()
        if d <= down:
            block = block_at(d)
            chunk_copy(k, block, chunk_minus, below).wait_recv()
            if d < down:
                chunk_copy(k, block, chunk_minus, below).start()
            chunk_copy(k, block, chunk_twin, twin).start()

    def twins(k):
        def one(n, carry):
            chunk_copy(k, n * 2 + 1 - core, chunk_twin, twin).wait_recv()
            return carry

        lax.fori_loop(0, chips, one, 0)

    places = []
    for n in range(blocks):
        place = n
        for level in range(map_ref.shape[0]):
            place = map_ref[level, 0, place]
        places.append(place)

    def source(at):
        found = [jnp.where(places[n] == at, n, 0) for n in range(blocks)]
        return functools.reduce(jnp.maximum, found)

    def gram(k):
        picked = bufs[k][source(front)]

        def one(n, carry):
            two = bufs[k][pl.ds(n * 2, 2)].reshape(2 * b, picked.shape[1])
            add = mm(two, picked, NT).reshape(2, b, b)
            if k == 0:
                acc[pl.ds(n * 2, 2)] = add
            else:
                acc[pl.ds(n * 2, 2)] = acc[pl.ds(n * 2, 2)] + add
            return carry

        lax.fori_loop(0, blocks // 2, one, 0, unroll=True)

    items = [(0, (p, q), q) for q in range(pivots) for p in range(q, pivots)]
    items += [(1, (p,), me) for p in range(pivots)]
    top_set = ((corner_top, row_top), top_send, top_recv)
    sum_set = ((corner_sum, row_sum), sum_send, sum_recv)

    def top_block(p):
        return top_ref.at[p * b : (p + 1) * b, :]

    def piece_block(p):
        return pieces.at[p * b : (p + 1) * b, :]

    def item_copy(chosen, n, src, way, to):
        refs, send, recv = chosen
        which, at, _ = items[n]
        dst = refs[which].at[at]
        return pltpu.make_async_remote_copy(
            dst if src is None else src, dst, send.at[way, n], recv.at[n],
            device_id=(leaf, to), device_id_type=MESH,
        )

    def roles(source):
        lane = core == source % 2
        far = (z + chips - source // 2) % chips
        return lane, far, lane & (far < half), lane & ((far == 0) | (far > half + 1))

    def items_launch(chosen, block):
        for n, (which, at, source) in enumerate(items):
            lane, far, plus, minus = roles(source)

            @pl.when(lane & (far == 0))
            def _():
                src = block(at[0])
                item_copy(chosen, n, src, 0, above).start()
                item_copy(chosen, n, src, 1, below).start()
                item_copy(chosen, n, src, 2, twin).start()
                chosen[0][which][at] = src[...]

    def relay_hop(t, chosen):
        for n, (which, at, source) in enumerate(items):
            lane, far, plus, minus = roles(source)

            @pl.when(lane & (jnp.minimum(far, chips - far) == t))
            def _():
                item_copy(chosen, n, None, 2, twin).wait_recv()

                @pl.when(plus)
                def _():
                    item_copy(chosen, n, None, 0, above).start()

                @pl.when(minus)
                def _():
                    item_copy(chosen, n, None, 1, below).start()

                item_copy(chosen, n, None, 2, twin).start()

    def gather(window):
        solve(0)
        pl.semaphore_wait(barrier, group - 1 + 3)
        launch(0)
        for k in range(1, parts):
            solve(k)
            if k < window:
                launch(k)
        for first in range(0, parts, window):
            last = first + window == parts
            for d in range(1, half + 1):
                for k in range(first, first + window):
                    relay(k, d)
                    if d == half - 1 and not last:
                        launch(k + window)
                    if d == half and last:
                        if k == first:
                            top_copy.wait()
                            own_copy.wait()
                            items_launch(top_set, top_block)
                        twins(k)
                        gram(k)
                if first:
                    for k in range(first - window, first)[d - 1 :: half]:
                        twins(k)
                        gram(k)

    gather(2)
    for at in range(blocks):
        part_ref[at] = -acc[source(at)].astype(jnp.bfloat16)

    def slice_copy(to, src):
        return pltpu.make_async_remote_copy(
            part_ref.at[to // per_block, pl.ds(to % per_block * rows, rows), :],
            got_slice.at[src], slice_send.at[to], slice_recv.at[src],
            device_id=(base + to, front), device_id_type=MESH,
        )

    def block_copy(to, src):
        return pltpu.make_async_remote_copy(
            part_ref.at[to], got_block.at[src], block_send.at[to], block_recv.at[src],
            device_id=(base + to, front), device_id_type=MESH,
        )

    def piece_copy(to, src):
        return pltpu.make_async_remote_copy(
            piece, pieces.at[pl.ds(pl.multiple_of(src * rows, rows), rows), :], piece_send.at[to], piece_recv.at[src],
            device_id=(base + to, front), device_id_type=MESH,
        )

    inner = front >= pivots

    def send_slice(d, carry):
        slice_copy(other(d), me).start()
        return carry

    def send_block(d, carry):
        to = other(d)

        @pl.when(inner & (to >= pivots))
        def _():
            block_copy(to, me).start()

        return carry

    lax.fori_loop(1, group, send_slice, 0)
    relay_hop(1, top_set)

    def add_slice(d, total):
        src = other(d)
        slice_copy(src, src).wait_recv()
        return total + got_slice[src].astype(jnp.float32)

    mine = part_ref[me // per_block, pl.ds(pl.multiple_of(me % per_block * rows, rows), rows), :]
    total = lax.fori_loop(1, group, add_slice, mine.astype(jnp.float32))
    piece[...] = total.astype(jnp.bfloat16)
    pieces[pl.ds(pl.multiple_of(me * rows, rows), rows), :] = total.astype(jnp.bfloat16)

    def send_piece(d, carry):
        piece_copy(other(d), me).start()
        return carry

    lax.fori_loop(1, group, send_piece, 0)
    lax.fori_loop(1, group, send_block, 0)

    def wait_piece(d, carry):
        src = other(d)
        piece_copy(src, src).wait_recv()
        return carry

    relay_hop(2, top_set)
    relay_hop(3, top_set)
    lax.fori_loop(1, group, wait_piece, 0)
    relay_hop(half, top_set)
    items_launch(sum_set, piece_block)
    for t in range(1, half + 1):
        relay_hop(t, sum_set)
    for chosen in (top_set, sum_set):
        for n in range(len(items)):

            @pl.when(jnp.logical_not(roles(items[n][2])[0]))
            def _():
                item_copy(chosen, n, None, 2, twin).wait_recv()

    for p in range(pivots):
        rows_p = slice(p * b, (p + 1) * b)
        col_ref[p] = top_ref[rows_p, :] + pieces[rows_p, :].astype(jnp.float32)
        row_ref[p] = row_top[p] + row_sum[p].astype(jnp.float32)
        for q in range(p + 1):
            corner_ref[p, q] = corner_top[p, q] + corner_sum[p, q].astype(jnp.float32)

    own_ref[...] = block_ref[...] + part_ref[me].astype(jnp.float32)

    @pl.when(inner & (me >= pivots))
    def _():
        def add_block(d, carry):
            src = other(d)
            block_copy(src, src).wait_recv()
            own_ref[...] = own_ref[...] + got_block[src].astype(jnp.float32)
            return carry

        lax.fori_loop(1, group, add_block, 0)

    def drain(d, carry):
        to = other(d)
        slice_copy(to, me).wait_send()
        piece_copy(to, me).wait_send()

        @pl.when(inner & (to >= pivots))
        def _():
            block_copy(to, me).wait_send()

        return carry

    lax.fori_loop(1, group, drain, 0)
    for chosen in (top_set, sum_set):
        for n in range(len(items)):
            lane, far, plus, minus = roles(items[n][2])

            @pl.when(plus)
            def _():
                item_copy(chosen, n, None, 0, above).wait_send()

            @pl.when(minus)
            def _():
                item_copy(chosen, n, None, 1, below).wait_send()

            @pl.when(lane)
            def _():
                item_copy(chosen, n, None, 2, twin).wait_send()

    for k in range(parts):
        up, down = reach(k)
        for d in range(half + 1):
            if d < up:
                chunk_copy(k, block_at(-d), chunk_plus, above).wait_send()
            if d < down:
                chunk_copy(k, block_at(d), chunk_minus, below).wait_send()

        def sent(n, carry):
            chunk_copy(k, n * 2 + core, chunk_twin, twin).wait_send()
            return carry

        lax.fori_loop(0, chips, sent, 0)


def assemble(group, chips, coupling, factors, tops, pattern, sizes, maps):
    b = coupling.shape[1]
    blocks = tops.shape[1] // b
    pivots = PIV // b
    rows = PIV // group
    items = pivots * (pivots + 1) // 2 + pivots
    parts = 4
    vmem = pl.BlockSpec(memory_space=pltpu.VMEM)
    smem = pl.BlockSpec(memory_space=pltpu.SMEM)
    dma = pltpu.SemaphoreType.DMA
    f32 = jnp.float32
    bf16 = jnp.bfloat16
    return pl.pallas_call(
        functools.partial(assemble_kernel, group, chips),
        out_shape=(
            jax.ShapeDtypeStruct((b, b), f32),
            jax.ShapeDtypeStruct((pivots, pivots, b, b), f32),
            jax.ShapeDtypeStruct((pivots, b, b), f32),
            jax.ShapeDtypeStruct((pivots, b, b), f32),
        ),
        in_specs=[vmem] * 2 + [pl.BlockSpec(memory_space=pl.ANY)] + [smem] * 3,
        out_specs=[vmem] * 4,
        scratch_shapes=[
            [pltpu.VMEM((blocks, b, coupling.shape[0] // parts), bf16)] * parts,
            pltpu.VMEM((blocks, b, b), f32),
            pltpu.VMEM((blocks, b, b), bf16),
            pltpu.VMEM((PIV, b), f32),
            pltpu.VMEM((b, b), f32),
            pltpu.VMEM((group, rows, b), bf16),
            pltpu.VMEM((group, b, b), bf16),
            pltpu.VMEM((rows, b), bf16),
            pltpu.VMEM((PIV, b), bf16),
        ]
        + [dma((parts, blocks))] * 4
        + [dma((2,))]
        + [dma((group,))] * 6
        + [
            pltpu.VMEM((pivots, pivots, b, b), f32),
            pltpu.VMEM((pivots, b, b), f32),
            pltpu.VMEM((pivots, pivots, b, b), bf16),
            pltpu.VMEM((pivots, b, b), bf16),
        ]
        + [dma((3, items)), dma((items,))] * 2,
        compiler_params=pltpu.CompilerParams(collective_id=1, has_side_effects=True),
    )(coupling, factors, tops, pattern, sizes, maps)


def shards(coupling, block_pattern, supernode_inverse, subdomain_sizes, block_maps, top_fronts):
    group = lax.axis_size("leaf") // top_fronts.shape[0]
    chips = lax.axis_size("front") // 2
    own, corner, own_row, own_col = assemble(
        group, chips, coupling, supernode_inverse, top_fronts,
        block_pattern, subdomain_sizes, block_maps,
    )
    flat = (PIV, coupling.shape[1])
    return finish(group, corner, own_row.reshape(flat), own_col.reshape(flat), own)


def solution(mesh):
    return jax.shard_map(
        shards,
        mesh=mesh,
        in_specs=(
            P("leaf", "front"),
            P("leaf", None, "front"),
            P("leaf", None, None),
            P("leaf"),
            P(None, "leaf", None),
            P(None, None, "front"),
        ),
        out_specs=P("leaf", "front"),
        check_vma=False,
    )
```

```python
import functools

import jax
import jax.numpy as jnp
from jax import lax
from jax.experimental import pallas as pl
from jax.experimental.pallas import tpu as pltpu
from jax.sharding import PartitionSpec as P

NN = (((1,), (0,)), ((), ()))
NT = (((1,), (1,)), ((), ()))
TN = (((0,), (0,)), ((), ()))


def halves(x):
    hi = x.astype(jnp.bfloat16)
    return hi, (x - hi.astype(jnp.float32)).astype(jnp.bfloat16)


def mm(a, b, dims):
    return lax.dot_general(a, b, dims, preferred_element_type=jnp.float32)


def mm3(a, b, dims):
    ah, al = halves(a)
    bh, bl = halves(b)
    return mm(ah, bh, dims) + (mm(ah, bl, dims) + mm(al, bh, dims))


def finish_kernel(group, corner_ref, ai_ref, aj_ref, aij_ref, out_ref, a_ref, y_ref, w_ref, ah_ref, al_ref):
    n = a_ref.shape[0]
    h = n // 2
    b = ai_ref.shape[1]
    for p in range(n // b):
        for q in range(p + 1):
            block = corner_ref[p, q]
            a_ref[p * b : (p + 1) * b, q * b : (q + 1) * b] = block
            if q < p:
                a_ref[q * b : (q + 1) * b, p * b : (p + 1) * b] = block.T
    rows = lax.broadcasted_iota(jnp.int32, (h, h), 0)
    cols = lax.broadcasted_iota(jnp.int32, (h, h), 1)
    eye = (rows == cols).astype(jnp.float32)
    weight = jnp.where(rows > cols, 1.0, jnp.where(rows == cols, 0.5, 0.0))
    for at in (0, h):
        diag = jnp.sum(a_ref[at : at + h, at : at + h] * eye, axis=0, keepdims=True)
        y_ref[at : at + h, at : at + h] = eye * lax.rsqrt(diag)
        y_ref[at : at + h, h - at : n - at] = jnp.zeros((h, h), jnp.float32)
    ah, al = halves(a_ref[...])
    ah_ref[...] = ah
    al_ref[...] = al

    def rough(_, carry):
        ab = ah_ref[...]
        y1 = y_ref[:h, :h].astype(jnp.bfloat16)
        y2 = y_ref[h:, :].astype(jnp.bfloat16)
        g1 = mm(ab[:, :h], y1, NT).astype(jnp.bfloat16)
        g2 = mm(ab, y2, NT).astype(jnp.bfloat16)
        e1 = (mm(y1, g1[:h], NN) - eye) * weight
        e21 = mm(y2, g1, NN)
        e22 = (mm(y2, g2, NN) - eye) * weight
        e1 = e1.astype(jnp.bfloat16)
        e21 = e21.astype(jnp.bfloat16)
        e22 = e22.astype(jnp.bfloat16)
        y_ref[:h, :h] = y_ref[:h, :h] - mm(e1, y1, NN)
        y_ref[h:, :h] = y_ref[h:, :h] - mm(e21, y1, NN) - mm(e22, y2[:, :h], NN)
        y_ref[h:, h:] = y_ref[h:, h:] - mm(e22, y2[:, h:], NN)
        return carry

    lax.fori_loop(0, 2, rough, 0)

    def pair(x, y, dims):
        (xh, xl), (yh, yl) = x, y
        return mm(xh, yh, dims) + (mm(xh, yl, dims) + mm(xl, yh, dims))

    def fine(carry):
        step, _ = carry
        y1 = halves(y_ref[:h, :h])
        y2 = halves(y_ref[h:, :])
        y21 = (y2[0][:, :h], y2[1][:, :h])
        y22 = (y2[0][:, h:], y2[1][:, h:])
        g1 = halves(pair((ah_ref[:, :h], al_ref[:, :h]), y1, NT))
        g2 = halves(pair((ah_ref[...], al_ref[...]), y2, NT))
        e1 = (pair(y1, (g1[0][:h], g1[1][:h]), NN) - eye) * weight
        e21 = pair(y2, g1, NN)
        e22 = (pair(y2, g2, NN) - eye) * weight
        worst = jnp.sum(e1 * e1) + jnp.sum(e21 * e21) + jnp.sum(e22 * e22)
        e1 = halves(e1)
        e21 = halves(e21)
        e22 = halves(e22)
        y_ref[:h, :h] = y_ref[:h, :h] - pair(e1, y1, NN)
        y_ref[h:, :h] = y_ref[h:, :h] - (pair(e21, y1, NN) + pair(e22, y21, NN))
        y_ref[h:, h:] = y_ref[h:, h:] - pair(e22, y22, NN)
        return step + 1, worst

    def unfinished(carry):
        step, worst = carry
        return (step < 40) & jnp.logical_not(worst < LIMIT)

    _, worst = lax.while_loop(unfinished, fine, (jnp.int32(0), jnp.float32(1.0)))

    @pl.when(jnp.logical_not(worst < LIMIT))
    def _():
        row_id = lax.broadcasted_iota(jnp.int32, (n, 1), 0)
        col_id = lax.broadcasted_iota(jnp.int32, (1, n), 1)
        w_ref[...] = a_ref[...]
        y_ref[...] = jnp.where(row_id == col_id, 1.0, 0.0)

        def eliminate(k, carry):
            w = w_ref[...]
            y = y_ref[...]
            row = w_ref[pl.ds(k, 1), :]
            scale = lax.rsqrt(jnp.sum(jnp.where(col_id == k, row, 0.0)))
            row = row * scale
            row_y = y_ref[pl.ds(k, 1), :] * scale
            col = jnp.sum(jnp.where(col_id == k, w, 0.0), axis=1, keepdims=True) * scale
            below = jnp.where(row_id > k, col, 0.0)
            here = row_id == k
            w_ref[...] = jnp.where(here, row, w - below * row)
            y_ref[...] = jnp.where(here, row_y, y - below * row_y)
            return carry

        lax.fori_loop(0, n, eliminate, 0)

    block_row = lax.axis_index("leaf") % group
    block_col = lax.axis_index("front")
    pivots = n // b
    y = halves(y_ref[...])
    xi = pair(y, halves(ai_ref[...]), NN)
    xj = pair(y, halves(aj_ref[...]), NN)
    schur = aij_ref[...] - mm3(xi, xj, TN)
    w_ref[:, :b] = xi
    picked = w_ref[pl.ds(pl.multiple_of(jnp.minimum(block_col, pivots - 1) * b, b), b), :b].T
    r = block_row * b + lax.broadcasted_iota(jnp.int32, (b, b), 0)
    c = block_col * b + lax.broadcasted_iota(jnp.int32, (b, b), 1)
    left = jnp.where(c <= r, picked, 0.0)
    right = jnp.where(block_row >= pivots, schur, 0.0)
    out_ref[...] = jnp.where(block_col >= pivots, right, left)


def finish(group, corner, ai, aj, aij):
    n, b = ai.shape
    vmem = pl.BlockSpec(memory_space=pltpu.VMEM)
    return pl.pallas_call(
        functools.partial(finish_kernel, group),
        out_shape=jax.ShapeDtypeStruct((b, b), jnp.float32),
        in_specs=[vmem] * 4,
        out_specs=vmem,
        scratch_shapes=[pltpu.VMEM((n, n), jnp.float32)] * 3 + [pltpu.VMEM((n, n), jnp.bfloat16)] * 2,
    )(corner, ai, aj, aij)

PIV = 512
LIMIT = 4e-3
MESH = pl.DeviceIdType.MESH


def assemble_kernel(
    group, chips, coupling_hbm, factor_hbm, tops_ref, pattern_ref, size_ref, map_ref,
    own_ref, corner_ref, row_ref, col_ref,
    coupling_ref, factor_ref, in_sem,
    bufs, acc, part_ref, top_ref, block_ref,
    got_slice, got_block, piece, pieces,
    chunk_recv, chunk_plus, chunk_minus, chunk_twin, top_sem,
    slice_send, slice_recv, block_send, block_recv, piece_send, piece_recv,
    corner_top, row_top, corner_sum, row_sum,
    top_send, top_recv, sum_send, sum_recv,
):
    blocks, b, _ = part_ref.shape
    pivots = corner_ref.shape[0]
    rows = piece.shape[0]
    per_block = b // rows
    leaf = lax.axis_index("leaf")
    front = lax.axis_index("front")
    base = leaf // group * group
    me = leaf - base
    z = front // 2
    core = front % 2
    twin = z * 2 + 1 - core
    above = (z + 1) % chips * 2 + core
    below = (z + chips - 1) % chips * 2 + core

    def other(d):
        return (me + d) % group

    parts = len(bufs)
    supers = factor_ref.shape[0] // parts

    def input_copies(k):
        first = k * supers
        return (
            pltpu.make_async_copy(
                coupling_hbm.at[pl.ds(first * b, supers * b), :],
                coupling_ref.at[pl.ds(first * b, supers * b), :],
                in_sem.at[0, k],
            ),
            pltpu.make_async_copy(
                factor_hbm.at[pl.ds(first, supers)], factor_ref.at[pl.ds(first, supers)],
                in_sem.at[1, k],
            ),
        )

    for k in range(parts):
        for copy in input_copies(k):
            copy.start()
    top_copy = pltpu.make_async_copy(
        tops_ref.at[leaf // group, pl.ds(0, pivots * b), :], top_ref, top_sem.at[0]
    )
    own_copy = pltpu.make_async_copy(
        tops_ref.at[leaf // group, pl.ds(pl.multiple_of(me * b, b), b), :], block_ref, top_sem.at[1]
    )
    top_copy.start()
    own_copy.start()

    barrier = pltpu.get_barrier_semaphore()

    def greet(d, carry):
        pl.semaphore_signal(barrier, 1, device_id=(base + other(d), front), device_id_type=MESH)
        return carry

    lax.fori_loop(1, group, greet, 0)
    for side in (twin, above, below):
        pl.semaphore_signal(barrier, 1, device_id=(leaf, side), device_id_type=MESH)

    half = chips // 2
    row_id = lax.broadcasted_iota(jnp.int32, (b, b), 0)

    def solve(k):
        for copy in input_copies(k):
            copy.wait()
        for r in range(supers):
            n = k * supers + r
            solved = mm(factor_ref[n], coupling_ref[n * b : (n + 1) * b, :], NN)
            live = jnp.where(row_id + n * b < size_ref[0], pattern_ref[0, 0, n], 0)
            kept = jnp.where(live > 0, solved, 0.0)
            bufs[k][front, :, r * b : (r + 1) * b] = kept.T.astype(jnp.bfloat16)

    def chunk_copy(k, block, sem, to):
        return pltpu.make_async_remote_copy(
            bufs[k].at[block], bufs[k].at[block], sem.at[k, block], chunk_recv.at[k, block],
            device_id=(leaf, to), device_id_type=MESH,
        )

    def block_at(d):
        return (z + d + chips) % chips * 2 + core

    def reach(k):
        return (half, half - 1) if k % 2 else (half - 1, half)

    def launch(k):
        chunk_copy(k, front, chunk_plus, above).start()
        chunk_copy(k, front, chunk_minus, below).start()
        chunk_copy(k, front, chunk_twin, twin).start()

    def relay(k, d):
        up, down = reach(k)
        if d <= up:
            block = block_at(-d)
            chunk_copy(k, block, chunk_plus, above).wait_recv()
            if d < up:
                chunk_copy(k, block, chunk_plus, above).start()
            chunk_copy(k, block, chunk_twin, twin).start()
        if d <= down:
            block = block_at(d)
            chunk_copy(k, block, chunk_minus, below).wait_recv()
            if d < down:
                chunk_copy(k, block, chunk_minus, below).start()
            chunk_copy(k, block, chunk_twin, twin).start()

    def twins(k):
        def one(n, carry):
            chunk_copy(k, n * 2 + 1 - core, chunk_twin, twin).wait_recv()
            return carry

        lax.fori_loop(0, chips, one, 0)

    places = []
    for n in range(blocks):
        place = n
        for level in range(map_ref.shape[0]):
            place = map_ref[level, 0, place]
        places.append(place)

    def source(at):
        found = [jnp.where(places[n] == at, n, 0) for n in range(blocks)]
        return functools.reduce(jnp.maximum, found)

    def gram(k):
        picked = bufs[k][source(front)]

        def one(n, carry):
            two = bufs[k][pl.ds(n * 2, 2)].reshape(2 * b, picked.shape[1])
            add = mm(two, picked, NT).reshape(2, b, b)
            if k == 0:
                acc[pl.ds(n * 2, 2)] = add
            else:
                acc[pl.ds(n * 2, 2)] = acc[pl.ds(n * 2, 2)] + add
            return carry

        lax.fori_loop(0, blocks // 2, one, 0, unroll=True)

    items = [(0, (p, q), q) for q in range(pivots) for p in range(q, pivots)]
    items += [(1, (p,), me) for p in range(pivots)]
    top_set = ((corner_top, row_top), top_send, top_recv)
    sum_set = ((corner_sum, row_sum), sum_send, sum_recv)

    def top_block(p):
        return top_ref.at[p * b : (p + 1) * b, :]

    def piece_block(p):
        return pieces.at[p * b : (p + 1) * b, :]

    def item_copy(chosen, n, src, way, to):
        refs, send, recv = chosen
        which, at, _ = items[n]
        dst = refs[which].at[at]
        return pltpu.make_async_remote_copy(
            dst if src is None else src, dst, send.at[way, n], recv.at[n],
            device_id=(leaf, to), device_id_type=MESH,
        )

    def roles(source):
        lane = core == source % 2
        far = (z + chips - source // 2) % chips
        return lane, far, lane & (far < half), lane & ((far == 0) | (far > half + 1))

    def items_launch(chosen, block):
        for n, (which, at, source) in enumerate(items):
            lane, far, plus, minus = roles(source)

            @pl.when(lane & (far == 0))
            def _():
                src = block(at[0])
                item_copy(chosen, n, src, 0, above).start()
                item_copy(chosen, n, src, 1, below).start()
                item_copy(chosen, n, src, 2, twin).start()
                chosen[0][which][at] = src[...]

    def relay_hop(t, chosen):
        for n, (which, at, source) in enumerate(items):
            lane, far, plus, minus = roles(source)

            @pl.when(lane & (jnp.minimum(far, chips - far) == t))
            def _():
                item_copy(chosen, n, None, 2, twin).wait_recv()

                @pl.when(plus)
                def _():
                    item_copy(chosen, n, None, 0, above).start()

                @pl.when(minus)
                def _():
                    item_copy(chosen, n, None, 1, below).start()

                item_copy(chosen, n, None, 2, twin).start()

    def gather(window):
        solve(0)
        pl.semaphore_wait(barrier, group - 1 + 3)
        launch(0)
        for k in range(1, parts):
            solve(k)
            if k < window:
                launch(k)
        for first in range(0, parts, window):
            last = first + window == parts
            for d in range(1, half + 1):
                for k in range(first, first + window):
                    relay(k, d)
                    if d == half - 1 and not last:
                        launch(k + window)
                    if d == half and last:
                        if k == first:
                            top_copy.wait()
                            own_copy.wait()
                            items_launch(top_set, top_block)
                        twins(k)
                        gram(k)
                if first:
                    for k in range(first - window, first)[d - 1 :: half]:
                        twins(k)
                        gram(k)

    gather(2)
    for at in range(blocks):
        part_ref[at] = -acc[source(at)].astype(jnp.bfloat16)

    def slice_copy(to, src):
        return pltpu.make_async_remote_copy(
            part_ref.at[to // per_block, pl.ds(to % per_block * rows, rows), :],
            got_slice.at[src], slice_send.at[to], slice_recv.at[src],
            device_id=(base + to, front), device_id_type=MESH,
        )

    def block_copy(to, src):
        return pltpu.make_async_remote_copy(
            part_ref.at[to], got_block.at[src], block_send.at[to], block_recv.at[src],
            device_id=(base + to, front), device_id_type=MESH,
        )

    def piece_copy(to, src):
        return pltpu.make_async_remote_copy(
            piece, pieces.at[pl.ds(pl.multiple_of(src * rows, rows), rows), :], piece_send.at[to], piece_recv.at[src],
            device_id=(base + to, front), device_id_type=MESH,
        )

    inner = front >= pivots

    def send_slice(d, carry):
        slice_copy(other(d), me).start()
        return carry

    def send_block(d, carry):
        to = other(d)

        @pl.when(inner & (to >= pivots))
        def _():
            block_copy(to, me).start()

        return carry

    lax.fori_loop(1, group, send_slice, 0)
    relay_hop(1, top_set)

    def add_slice(d, total):
        src = other(d)
        slice_copy(src, src).wait_recv()
        return total + got_slice[src].astype(jnp.float32)

    mine = part_ref[me // per_block, pl.ds(pl.multiple_of(me % per_block * rows, rows), rows), :]
    total = lax.fori_loop(1, group, add_slice, mine.astype(jnp.float32))
    piece[...] = total.astype(jnp.bfloat16)
    pieces[pl.ds(pl.multiple_of(me * rows, rows), rows), :] = total.astype(jnp.bfloat16)

    def send_piece(d, carry):
        piece_copy(other(d), me).start()
        return carry

    lax.fori_loop(1, group, send_piece, 0)
    lax.fori_loop(1, group, send_block, 0)

    def wait_piece(d, carry):
        src = other(d)
        piece_copy(src, src).wait_recv()
        return carry

    relay_hop(2, top_set)
    relay_hop(3, top_set)
    lax.fori_loop(1, group, wait_piece, 0)
    items_launch(sum_set, piece_block)
    relay_hop(1, sum_set)
    relay_hop(half, top_set)
    for t in range(2, half + 1):
        relay_hop(t, sum_set)
    for chosen in (top_set, sum_set):
        for n in range(len(items)):

            @pl.when(jnp.logical_not(roles(items[n][2])[0]))
            def _():
                item_copy(chosen, n, None, 2, twin).wait_recv()

    for p in range(pivots):
        rows_p = slice(p * b, (p + 1) * b)
        col_ref[p] = top_ref[rows_p, :] + pieces[rows_p, :].astype(jnp.float32)
        row_ref[p] = row_top[p] + row_sum[p].astype(jnp.float32)
        for q in range(p + 1):
            corner_ref[p, q] = corner_top[p, q] + corner_sum[p, q].astype(jnp.float32)

    own_ref[...] = block_ref[...] + part_ref[me].astype(jnp.float32)

    @pl.when(inner & (me >= pivots))
    def _():
        def add_block(d, carry):
            src = other(d)
            block_copy(src, src).wait_recv()
            own_ref[...] = own_ref[...] + got_block[src].astype(jnp.float32)
            return carry

        lax.fori_loop(1, group, add_block, 0)

    def drain(d, carry):
        to = other(d)
        slice_copy(to, me).wait_send()
        piece_copy(to, me).wait_send()

        @pl.when(inner & (to >= pivots))
        def _():
            block_copy(to, me).wait_send()

        return carry

    lax.fori_loop(1, group, drain, 0)
    for chosen in (top_set, sum_set):
        for n in range(len(items)):
            lane, far, plus, minus = roles(items[n][2])

            @pl.when(plus)
            def _():
                item_copy(chosen, n, None, 0, above).wait_send()

            @pl.when(minus)
            def _():
                item_copy(chosen, n, None, 1, below).wait_send()

            @pl.when(lane)
            def _():
                item_copy(chosen, n, None, 2, twin).wait_send()

    for k in range(parts):
        up, down = reach(k)
        for d in range(half + 1):
            if d < up:
                chunk_copy(k, block_at(-d), chunk_plus, above).wait_send()
            if d < down:
                chunk_copy(k, block_at(d), chunk_minus, below).wait_send()

        def sent(n, carry):
            chunk_copy(k, n * 2 + core, chunk_twin, twin).wait_send()
            return carry

        lax.fori_loop(0, chips, sent, 0)


def assemble(group, chips, coupling, factors, tops, pattern, sizes, maps):
    b = coupling.shape[1]
    blocks = tops.shape[1] // b
    pivots = PIV // b
    rows = PIV // group
    items = pivots * (pivots + 1) // 2 + pivots
    parts = 4
    vmem = pl.BlockSpec(memory_space=pltpu.VMEM)
    smem = pl.BlockSpec(memory_space=pltpu.SMEM)
    dma = pltpu.SemaphoreType.DMA
    f32 = jnp.float32
    bf16 = jnp.bfloat16
    return pl.pallas_call(
        functools.partial(assemble_kernel, group, chips),
        out_shape=(
            jax.ShapeDtypeStruct((b, b), f32),
            jax.ShapeDtypeStruct((pivots, pivots, b, b), f32),
            jax.ShapeDtypeStruct((pivots, b, b), f32),
            jax.ShapeDtypeStruct((pivots, b, b), f32),
        ),
        in_specs=[pl.BlockSpec(memory_space=pltpu.MemorySpace.HBM)] * 3 + [smem] * 3,
        out_specs=[vmem] * 4,
        scratch_shapes=[
            pltpu.VMEM(coupling.shape, bf16),
            pltpu.VMEM(factors.shape, bf16),
            dma((2, parts)),
            [pltpu.VMEM((blocks, b, coupling.shape[0] // parts), bf16)] * parts,
            pltpu.VMEM((blocks, b, b), f32),
            pltpu.VMEM((blocks, b, b), bf16),
            pltpu.VMEM((PIV, b), f32),
            pltpu.VMEM((b, b), f32),
            pltpu.VMEM((group, rows, b), bf16),
            pltpu.VMEM((group, b, b), bf16),
            pltpu.VMEM((rows, b), bf16),
            pltpu.VMEM((PIV, b), bf16),
        ]
        + [dma((parts, blocks))] * 4
        + [dma((2,))]
        + [dma((group,))] * 6
        + [
            pltpu.VMEM((pivots, pivots, b, b), f32),
            pltpu.VMEM((pivots, b, b), f32),
            pltpu.VMEM((pivots, pivots, b, b), bf16),
            pltpu.VMEM((pivots, b, b), bf16),
        ]
        + [dma((3, items)), dma((items,))] * 2,
        compiler_params=pltpu.CompilerParams(collective_id=1, has_side_effects=True),
    )(coupling, factors, tops, pattern, sizes, maps)


def shards(coupling, block_pattern, supernode_inverse, subdomain_sizes, block_maps, top_fronts):
    group = lax.axis_size("leaf") // top_fronts.shape[0]
    chips = lax.axis_size("front") // 2
    own, corner, own_row, own_col = assemble(
        group, chips, coupling, supernode_inverse, top_fronts,
        block_pattern.transpose(0, 2, 1), subdomain_sizes, block_maps,
    )
    flat = (PIV, coupling.shape[1])
    return finish(group, corner, own_row.reshape(flat), own_col.reshape(flat), own)


def solution(mesh):
    return jax.shard_map(
        shards,
        mesh=mesh,
        in_specs=(
            P("leaf", "front"),
            P("leaf", None, "front"),
            P("leaf", None, None),
            P("leaf"),
            P(None, "leaf", None),
            P(None, None, "front"),
        ),
        out_specs=P("leaf", "front"),
        check_vma=False,
    )
```

```python
import functools

import jax
import jax.numpy as jnp
from jax import lax
from jax.experimental import pallas as pl
from jax.experimental.pallas import tpu as pltpu
from jax.sharding import PartitionSpec as P

NN = (((1,), (0,)), ((), ()))
NT = (((1,), (1,)), ((), ()))
TN = (((0,), (0,)), ((), ()))


def halves(x):
    hi = x.astype(jnp.bfloat16)
    return hi, (x - hi.astype(jnp.float32)).astype(jnp.bfloat16)


def mm(a, b, dims):
    return lax.dot_general(a, b, dims, preferred_element_type=jnp.float32)


def mm3(a, b, dims):
    ah, al = halves(a)
    bh, bl = halves(b)
    return mm(ah, bh, dims) + (mm(ah, bl, dims) + mm(al, bh, dims))


def finish_kernel(group, corner_ref, ai_ref, aj_ref, aij_ref, out_ref, a_ref, y_ref, w_ref, ah_ref, al_ref):
    n = a_ref.shape[0]
    h = n // 2
    b = ai_ref.shape[1]
    for p in range(n // b):
        for q in range(p + 1):
            block = corner_ref[p * (p + 1) // 2 + q]
            a_ref[p * b : (p + 1) * b, q * b : (q + 1) * b] = block
            if q < p:
                a_ref[q * b : (q + 1) * b, p * b : (p + 1) * b] = block.T
    rows = lax.broadcasted_iota(jnp.int32, (h, h), 0)
    cols = lax.broadcasted_iota(jnp.int32, (h, h), 1)
    eye = (rows == cols).astype(jnp.float32)
    weight = jnp.where(rows > cols, 1.0, jnp.where(rows == cols, 0.5, 0.0))
    for at in (0, h):
        diag = jnp.sum(a_ref[at : at + h, at : at + h] * eye, axis=0, keepdims=True)
        y_ref[at : at + h, at : at + h] = eye * lax.rsqrt(diag)
        y_ref[at : at + h, h - at : n - at] = jnp.zeros((h, h), jnp.float32)
    ah, al = halves(a_ref[...])
    ah_ref[...] = ah
    al_ref[...] = al

    def rough(_, carry):
        ab = ah_ref[...]
        y1 = y_ref[:h, :h].astype(jnp.bfloat16)
        y2 = y_ref[h:, :].astype(jnp.bfloat16)
        g1 = mm(ab[:, :h], y1, NT).astype(jnp.bfloat16)
        g2 = mm(ab, y2, NT).astype(jnp.bfloat16)
        e1 = (mm(y1, g1[:h], NN) - eye) * weight
        e21 = mm(y2, g1, NN)
        e22 = (mm(y2, g2, NN) - eye) * weight
        e1 = e1.astype(jnp.bfloat16)
        e21 = e21.astype(jnp.bfloat16)
        e22 = e22.astype(jnp.bfloat16)
        y_ref[:h, :h] = y_ref[:h, :h] - mm(e1, y1, NN)
        y_ref[h:, :h] = y_ref[h:, :h] - mm(e21, y1, NN) - mm(e22, y2[:, :h], NN)
        y_ref[h:, h:] = y_ref[h:, h:] - mm(e22, y2[:, h:], NN)
        return carry

    lax.fori_loop(0, 2, rough, 0)

    def pair(x, y, dims):
        (xh, xl), (yh, yl) = x, y
        return mm(xh, yh, dims) + (mm(xh, yl, dims) + mm(xl, yh, dims))

    def fine(carry):
        step, _ = carry
        y1 = halves(y_ref[:h, :h])
        y2 = halves(y_ref[h:, :])
        y21 = (y2[0][:, :h], y2[1][:, :h])
        y22 = (y2[0][:, h:], y2[1][:, h:])
        g1 = halves(pair((ah_ref[:, :h], al_ref[:, :h]), y1, NT))
        g2 = halves(pair((ah_ref[...], al_ref[...]), y2, NT))
        e1 = (pair(y1, (g1[0][:h], g1[1][:h]), NN) - eye) * weight
        e21 = pair(y2, g1, NN)
        e22 = (pair(y2, g2, NN) - eye) * weight
        worst = jnp.sum(e1 * e1) + jnp.sum(e21 * e21) + jnp.sum(e22 * e22)
        e1 = halves(e1)
        e21 = halves(e21)
        e22 = halves(e22)
        y_ref[:h, :h] = y_ref[:h, :h] - pair(e1, y1, NN)
        y_ref[h:, :h] = y_ref[h:, :h] - (pair(e21, y1, NN) + pair(e22, y21, NN))
        y_ref[h:, h:] = y_ref[h:, h:] - pair(e22, y22, NN)
        return step + 1, worst

    def unfinished(carry):
        step, worst = carry
        return (step < 40) & jnp.logical_not(worst < LIMIT)

    _, worst = lax.while_loop(unfinished, fine, (jnp.int32(0), jnp.float32(1.0)))

    @pl.when(jnp.logical_not(worst < LIMIT))
    def _():
        row_id = lax.broadcasted_iota(jnp.int32, (n, 1), 0)
        col_id = lax.broadcasted_iota(jnp.int32, (1, n), 1)
        w_ref[...] = a_ref[...]
        y_ref[...] = jnp.where(row_id == col_id, 1.0, 0.0)

        def eliminate(k, carry):
            w = w_ref[...]
            y = y_ref[...]
            row = w_ref[pl.ds(k, 1), :]
            scale = lax.rsqrt(jnp.sum(jnp.where(col_id == k, row, 0.0)))
            row = row * scale
            row_y = y_ref[pl.ds(k, 1), :] * scale
            col = jnp.sum(jnp.where(col_id == k, w, 0.0), axis=1, keepdims=True) * scale
            below = jnp.where(row_id > k, col, 0.0)
            here = row_id == k
            w_ref[...] = jnp.where(here, row, w - below * row)
            y_ref[...] = jnp.where(here, row_y, y - below * row_y)
            return carry

        lax.fori_loop(0, n, eliminate, 0)

    block_row = lax.axis_index("leaf") % group
    block_col = lax.axis_index("front")
    pivots = n // b
    y = halves(y_ref[...])
    xi = pair(y, halves(ai_ref[...]), NN)
    xj = pair(y, halves(aj_ref[...]), NN)
    schur = aij_ref[...] - mm3(xi, xj, TN)
    w_ref[:, :b] = xi
    picked = w_ref[pl.ds(pl.multiple_of(jnp.minimum(block_col, pivots - 1) * b, b), b), :b].T
    r = block_row * b + lax.broadcasted_iota(jnp.int32, (b, b), 0)
    c = block_col * b + lax.broadcasted_iota(jnp.int32, (b, b), 1)
    left = jnp.where(c <= r, picked, 0.0)
    right = jnp.where(block_row >= pivots, schur, 0.0)
    out_ref[...] = jnp.where(block_col >= pivots, right, left)


def finish(group, corner, ai, aj, aij):
    n, b = ai.shape
    vmem = pl.BlockSpec(memory_space=pltpu.VMEM)
    return pl.pallas_call(
        functools.partial(finish_kernel, group),
        out_shape=jax.ShapeDtypeStruct((b, b), jnp.float32),
        in_specs=[vmem] * 4,
        out_specs=vmem,
        scratch_shapes=[pltpu.VMEM((n, n), jnp.float32)] * 3 + [pltpu.VMEM((n, n), jnp.bfloat16)] * 2,
    )(corner, ai, aj, aij)

PIV = 512
LIMIT = 4e-3
MESH = pl.DeviceIdType.MESH


def assemble_kernel(
    group, chips, coupling_hbm, factor_hbm, tops_ref, pattern_ref, size_ref, map_ref,
    own_ref, corner_ref, row_ref, col_ref,
    coupling_ref, factor_ref, in_sem,
    bufs, acc, part_ref, top_ref, block_ref,
    got_slice, got_block, piece, pieces,
    chunk_recv, chunk_plus, chunk_minus, chunk_twin, top_sem,
    slice_send, slice_recv, block_send, block_recv, piece_send, piece_recv,
    corner_top, row_top, corner_sum, row_sum,
    top_send, top_recv, sum_send, sum_recv,
):
    blocks, b, _ = part_ref.shape
    pivots = row_ref.shape[0]
    rows = piece.shape[0]
    per_block = b // rows
    leaf = lax.axis_index("leaf")
    front = lax.axis_index("front")
    base = leaf // group * group
    me = leaf - base
    z = front // 2
    core = front % 2
    twin = z * 2 + 1 - core
    above = (z + 1) % chips * 2 + core
    below = (z + chips - 1) % chips * 2 + core

    def other(d):
        return (me + d) % group

    parts = len(bufs)
    supers = factor_ref.shape[0] // parts

    def input_copies(k):
        first = k * supers
        return (
            pltpu.make_async_copy(
                coupling_hbm.at[pl.ds(first * b, supers * b), :],
                coupling_ref.at[pl.ds(first * b, supers * b), :],
                in_sem.at[0, k],
            ),
            pltpu.make_async_copy(
                factor_hbm.at[pl.ds(first, supers)], factor_ref.at[pl.ds(first, supers)],
                in_sem.at[1, k],
            ),
        )

    for k in range(parts):
        for copy in input_copies(k):
            copy.start()
    top_copy = pltpu.make_async_copy(
        tops_ref.at[leaf // group, pl.ds(0, pivots * b), :], top_ref, top_sem.at[0]
    )
    own_copy = pltpu.make_async_copy(
        tops_ref.at[leaf // group, pl.ds(pl.multiple_of(me * b, b), b), :], block_ref, top_sem.at[1]
    )
    top_copy.start()
    own_copy.start()

    barrier = pltpu.get_barrier_semaphore()

    def greet(d, carry):
        pl.semaphore_signal(barrier, 1, device_id=(base + other(d), front), device_id_type=MESH)
        return carry

    lax.fori_loop(1, group, greet, 0)
    for side in (twin, above, below):
        pl.semaphore_signal(barrier, 1, device_id=(leaf, side), device_id_type=MESH)

    half = chips // 2
    row_id = lax.broadcasted_iota(jnp.int32, (b, b), 0)

    def solve(k):
        for copy in input_copies(k):
            copy.wait()
        for r in range(supers):
            n = k * supers + r
            solved = mm(factor_ref[n], coupling_ref[n * b : (n + 1) * b, :], NN)
            live = jnp.where(row_id + n * b < size_ref[0], pattern_ref[0, 0, n], 0)
            kept = jnp.where(live > 0, solved, 0.0)
            bufs[k][front, :, r * b : (r + 1) * b] = kept.T.astype(jnp.bfloat16)

    def chunk_copy(k, block, sem, to):
        return pltpu.make_async_remote_copy(
            bufs[k].at[block], bufs[k].at[block], sem.at[k, block], chunk_recv.at[k, block],
            device_id=(leaf, to), device_id_type=MESH,
        )

    def block_at(d):
        return (z + d + chips) % chips * 2 + core

    def reach(k):
        return (half, half - 1) if k % 2 else (half - 1, half)

    def launch(k):
        chunk_copy(k, front, chunk_plus, above).start()
        chunk_copy(k, front, chunk_minus, below).start()
        chunk_copy(k, front, chunk_twin, twin).start()

    def relay(k, d):
        up, down = reach(k)
        if d <= up:
            block = block_at(-d)
            chunk_copy(k, block, chunk_plus, above).wait_recv()
            if d < up:
                chunk_copy(k, block, chunk_plus, above).start()
            chunk_copy(k, block, chunk_twin, twin).start()
        if d <= down:
            block = block_at(d)
            chunk_copy(k, block, chunk_minus, below).wait_recv()
            if d < down:
                chunk_copy(k, block, chunk_minus, below).start()
            chunk_copy(k, block, chunk_twin, twin).start()

    def twins(k):
        def one(n, carry):
            chunk_copy(k, n * 2 + 1 - core, chunk_twin, twin).wait_recv()
            return carry

        lax.fori_loop(0, chips, one, 0)

    places = []
    for n in range(blocks):
        place = n
        for level in range(map_ref.shape[0]):
            place = map_ref[level, 0, place]
        places.append(place)

    def source(at):
        found = [jnp.where(places[n] == at, n, 0) for n in range(blocks)]
        return functools.reduce(jnp.maximum, found)

    def gram(k):
        picked = bufs[k][source(front)]

        def one(n, carry):
            two = bufs[k][pl.ds(n * 2, 2)].reshape(2 * b, picked.shape[1])
            add = mm(two, picked, NT).reshape(2, b, b)
            if k == 0:
                acc[pl.ds(n * 2, 2)] = add
            else:
                acc[pl.ds(n * 2, 2)] = acc[pl.ds(n * 2, 2)] + add
            return carry

        lax.fori_loop(0, blocks // 2, one, 0, unroll=True)

    items = [(0, (p, q), q) for q in range(pivots) for p in range(q, pivots)]
    items += [(1, (p,), me) for p in range(pivots)]
    top_set = ((corner_top, row_top), top_send, top_recv)
    sum_set = ((corner_sum, row_sum), sum_send, sum_recv)

    def top_block(p):
        return top_ref.at[p * b : (p + 1) * b, :]

    def piece_block(p):
        return pieces.at[p * b : (p + 1) * b, :]

    def item_copy(chosen, n, src, way, to):
        refs, send, recv = chosen
        which, at, _ = items[n]
        dst = refs[which].at[at]
        return pltpu.make_async_remote_copy(
            dst if src is None else src, dst, send.at[way, n], recv.at[n],
            device_id=(leaf, to), device_id_type=MESH,
        )

    def roles(source):
        lane = core == source % 2
        far = (z + chips - source // 2) % chips
        return lane, far, lane & (far < half), lane & ((far == 0) | (far > half + 1))

    def items_launch(chosen, block):
        for n, (which, at, source) in enumerate(items):
            lane, far, plus, minus = roles(source)

            @pl.when(lane & (far == 0))
            def _():
                src = block(at[0])
                item_copy(chosen, n, src, 0, above).start()
                item_copy(chosen, n, src, 1, below).start()
                item_copy(chosen, n, src, 2, twin).start()
                chosen[0][which][at] = src[...]

    def relay_hop(t, chosen):
        for n, (which, at, source) in enumerate(items):
            lane, far, plus, minus = roles(source)

            @pl.when(lane & (jnp.minimum(far, chips - far) == t))
            def _():
                item_copy(chosen, n, None, 2, twin).wait_recv()

                @pl.when(plus)
                def _():
                    item_copy(chosen, n, None, 0, above).start()

                @pl.when(minus)
                def _():
                    item_copy(chosen, n, None, 1, below).start()

                item_copy(chosen, n, None, 2, twin).start()

    def gather(window):
        solve(0)
        pl.semaphore_wait(barrier, group - 1 + 3)
        launch(0)
        for k in range(1, parts):
            solve(k)
            if k < window:
                launch(k)
        for first in range(0, parts, window):
            last = first + window == parts
            for d in range(1, half + 1):
                for k in range(first, first + window):
                    relay(k, d)
                    if d == half - 1 and not last:
                        launch(k + window)
                    if d == half and last:
                        if k == first:
                            top_copy.wait()
                            own_copy.wait()
                            items_launch(top_set, top_block)
                        twins(k)
                        if k < parts - 1:
                            gram(k)
                if first:
                    for k in range(first - window, first)[d - 1 :: half]:
                        twins(k)
                        gram(k)

    gather(2)
    final = parts - 1
    picked = bufs[final][source(front)]
    for at in range(pivots):
        found = source(at)
        part_ref[at] = -(acc[found] + mm(bufs[final][found], picked, NT)).astype(jnp.bfloat16)

    def slice_copy(to, src):
        return pltpu.make_async_remote_copy(
            part_ref.at[to // per_block, pl.ds(to % per_block * rows, rows), :],
            got_slice.at[src], slice_send.at[to], slice_recv.at[src],
            device_id=(base + to, front), device_id_type=MESH,
        )

    def block_copy(to, src):
        return pltpu.make_async_remote_copy(
            part_ref.at[to], got_block.at[src], block_send.at[to], block_recv.at[src],
            device_id=(base + to, front), device_id_type=MESH,
        )

    def piece_copy(to, src):
        return pltpu.make_async_remote_copy(
            piece, pieces.at[pl.ds(pl.multiple_of(src * rows, rows), rows), :], piece_send.at[to], piece_recv.at[src],
            device_id=(base + to, front), device_id_type=MESH,
        )

    inner = front >= pivots

    def send_slice(d, carry):
        slice_copy(other(d), me).start()
        return carry

    def send_block(d, carry):
        to = other(d)

        @pl.when(inner & (to >= pivots))
        def _():
            block_copy(to, me).start()

        return carry

    lax.fori_loop(1, group, send_slice, 0)
    gram(final)
    for at in range(pivots, blocks):
        part_ref[at] = -acc[source(at)].astype(jnp.bfloat16)
    relay_hop(1, top_set)

    def add_slice(d, total):
        src = other(d)
        slice_copy(src, src).wait_recv()
        return total + got_slice[src].astype(jnp.float32)

    mine = part_ref[me // per_block, pl.ds(pl.multiple_of(me % per_block * rows, rows), rows), :]
    total = lax.fori_loop(1, group, add_slice, mine.astype(jnp.float32))
    piece[...] = total.astype(jnp.bfloat16)
    pieces[pl.ds(pl.multiple_of(me * rows, rows), rows), :] = total.astype(jnp.bfloat16)

    def send_piece(d, carry):
        piece_copy(other(d), me).start()
        return carry

    lax.fori_loop(1, group, send_piece, 0)
    lax.fori_loop(1, group, send_block, 0)

    def wait_piece(d, carry):
        src = other(d)
        piece_copy(src, src).wait_recv()
        return carry

    relay_hop(2, top_set)
    relay_hop(3, top_set)
    lax.fori_loop(1, group, wait_piece, 0)
    items_launch(sum_set, piece_block)
    for t in range(1, half + 1):
        if t == half:
            relay_hop(half, top_set)
        relay_hop(t, sum_set)
    for chosen in (top_set, sum_set):
        for n in range(len(items)):

            @pl.when(jnp.logical_not(roles(items[n][2])[0]))
            def _():
                item_copy(chosen, n, None, 2, twin).wait_recv()

    for p in range(pivots):
        rows_p = slice(p * b, (p + 1) * b)
        col_ref[p] = top_ref[rows_p, :] + pieces[rows_p, :].astype(jnp.float32)
        row_ref[p] = row_top[p] + row_sum[p].astype(jnp.float32)
        for q in range(p + 1):
            corner_ref[p * (p + 1) // 2 + q] = corner_top[p, q] + corner_sum[p, q].astype(jnp.float32)

    own_ref[...] = block_ref[...] + part_ref[me].astype(jnp.float32)

    @pl.when(inner & (me >= pivots))
    def _():
        def add_block(d, carry):
            src = other(d)
            block_copy(src, src).wait_recv()
            own_ref[...] = own_ref[...] + got_block[src].astype(jnp.float32)
            return carry

        lax.fori_loop(1, group, add_block, 0)

    def drain(d, carry):
        to = other(d)
        slice_copy(to, me).wait_send()
        piece_copy(to, me).wait_send()

        @pl.when(inner & (to >= pivots))
        def _():
            block_copy(to, me).wait_send()

        return carry

    lax.fori_loop(1, group, drain, 0)
    for chosen in (top_set, sum_set):
        for n in range(len(items)):
            lane, far, plus, minus = roles(items[n][2])

            @pl.when(plus)
            def _():
                item_copy(chosen, n, None, 0, above).wait_send()

            @pl.when(minus)
            def _():
                item_copy(chosen, n, None, 1, below).wait_send()

            @pl.when(lane)
            def _():
                item_copy(chosen, n, None, 2, twin).wait_send()

    for k in range(parts):
        up, down = reach(k)
        for d in range(half + 1):
            if d < up:
                chunk_copy(k, block_at(-d), chunk_plus, above).wait_send()
            if d < down:
                chunk_copy(k, block_at(d), chunk_minus, below).wait_send()

        def sent(n, carry):
            chunk_copy(k, n * 2 + core, chunk_twin, twin).wait_send()
            return carry

        lax.fori_loop(0, chips, sent, 0)


def assemble(group, chips, coupling, factors, tops, pattern, sizes, maps):
    b = coupling.shape[1]
    blocks = tops.shape[1] // b
    pivots = PIV // b
    rows = PIV // group
    items = pivots * (pivots + 1) // 2 + pivots
    parts = 4
    vmem = pl.BlockSpec(memory_space=pltpu.VMEM)
    smem = pl.BlockSpec(memory_space=pltpu.SMEM)
    dma = pltpu.SemaphoreType.DMA
    f32 = jnp.float32
    bf16 = jnp.bfloat16
    return pl.pallas_call(
        functools.partial(assemble_kernel, group, chips),
        out_shape=(
            jax.ShapeDtypeStruct((b, b), f32),
            jax.ShapeDtypeStruct((pivots * (pivots + 1) // 2, b, b), f32),
            jax.ShapeDtypeStruct((pivots, b, b), f32),
            jax.ShapeDtypeStruct((pivots, b, b), f32),
        ),
        in_specs=[pl.BlockSpec(memory_space=pltpu.MemorySpace.HBM)] * 3 + [smem] * 3,
        out_specs=[vmem] * 4,
        scratch_shapes=[
            pltpu.VMEM(coupling.shape, bf16),
            pltpu.VMEM(factors.shape, bf16),
            dma((2, parts)),
            [pltpu.VMEM((blocks, b, coupling.shape[0] // parts), bf16)] * parts,
            pltpu.VMEM((blocks, b, b), f32),
            pltpu.VMEM((blocks, b, b), bf16),
            pltpu.VMEM((PIV, b), f32),
            pltpu.VMEM((b, b), f32),
            pltpu.VMEM((group, rows, b), bf16),
            pltpu.VMEM((group, b, b), bf16),
            pltpu.VMEM((rows, b), bf16),
            pltpu.VMEM((PIV, b), bf16),
        ]
        + [dma((parts, blocks))] * 4
        + [dma((2,))]
        + [dma((group,))] * 6
        + [
            pltpu.VMEM((pivots, pivots, b, b), f32),
            pltpu.VMEM((pivots, b, b), f32),
            pltpu.VMEM((pivots, pivots, b, b), bf16),
            pltpu.VMEM((pivots, b, b), bf16),
        ]
        + [dma((3, items)), dma((items,))] * 2,
        compiler_params=pltpu.CompilerParams(collective_id=1, has_side_effects=True),
    )(coupling, factors, tops, pattern, sizes, maps)


def shards(coupling, block_pattern, supernode_inverse, subdomain_sizes, block_maps, top_fronts):
    group = lax.axis_size("leaf") // top_fronts.shape[0]
    chips = lax.axis_size("front") // 2
    own, corner, own_row, own_col = assemble(
        group, chips, coupling, supernode_inverse, top_fronts,
        block_pattern.transpose(0, 2, 1), subdomain_sizes, block_maps,
    )
    flat = (PIV, coupling.shape[1])
    return finish(group, corner, own_row.reshape(flat), own_col.reshape(flat), own)


def solution(mesh):
    return jax.shard_map(
        shards,
        mesh=mesh,
        in_specs=(
            P("leaf", "front"),
            P("leaf", None, "front"),
            P("leaf", None, None),
            P("leaf"),
            P(None, "leaf", None),
            P(None, None, "front"),
        ),
        out_specs=P("leaf", "front"),
        check_vma=False,
    )
```

```python
import functools

import jax
import jax.numpy as jnp
from jax import lax
from jax.experimental import pallas as pl
from jax.experimental.pallas import tpu as pltpu
from jax.sharding import PartitionSpec as P

NN = (((1,), (0,)), ((), ()))
NT = (((1,), (1,)), ((), ()))
TN = (((0,), (0,)), ((), ()))


def halves(x):
    hi = x.astype(jnp.bfloat16)
    return hi, (x - hi.astype(jnp.float32)).astype(jnp.bfloat16)


def mm(a, b, dims):
    return lax.dot_general(a, b, dims, preferred_element_type=jnp.float32)


def mm3(a, b, dims):
    ah, al = halves(a)
    bh, bl = halves(b)
    return mm(ah, bh, dims) + (mm(ah, bl, dims) + mm(al, bh, dims))


def finish_kernel(group, corner_ref, ai_ref, aj_ref, aij_ref, out_ref, a_ref, y_ref, w_ref, ah_ref, al_ref):
    n = a_ref.shape[0]
    h = n // 2
    b = ai_ref.shape[1]
    for p in range(n // b):
        for q in range(p + 1):
            block = corner_ref[p * (p + 1) // 2 + q]
            a_ref[p * b : (p + 1) * b, q * b : (q + 1) * b] = block
            if q < p:
                a_ref[q * b : (q + 1) * b, p * b : (p + 1) * b] = block.T
    rows = lax.broadcasted_iota(jnp.int32, (h, h), 0)
    cols = lax.broadcasted_iota(jnp.int32, (h, h), 1)
    eye = (rows == cols).astype(jnp.float32)
    weight = jnp.where(rows > cols, 1.0, jnp.where(rows == cols, 0.5, 0.0))
    for at in (0, h):
        diag = jnp.sum(a_ref[at : at + h, at : at + h] * eye, axis=0, keepdims=True)
        y_ref[at : at + h, at : at + h] = eye * lax.rsqrt(diag)
        y_ref[at : at + h, h - at : n - at] = jnp.zeros((h, h), jnp.float32)
    ah, al = halves(a_ref[...])
    ah_ref[...] = ah
    al_ref[...] = al

    def rough(_, carry):
        ab = ah_ref[...]
        y1 = y_ref[:h, :h].astype(jnp.bfloat16)
        y2 = y_ref[h:, :].astype(jnp.bfloat16)
        g1 = mm(ab[:, :h], y1, NT).astype(jnp.bfloat16)
        g2 = mm(ab, y2, NT).astype(jnp.bfloat16)
        e1 = (mm(y1, g1[:h], NN) - eye) * weight
        e21 = mm(y2, g1, NN)
        e22 = (mm(y2, g2, NN) - eye) * weight
        e1 = e1.astype(jnp.bfloat16)
        e21 = e21.astype(jnp.bfloat16)
        e22 = e22.astype(jnp.bfloat16)
        y_ref[:h, :h] = y_ref[:h, :h] - mm(e1, y1, NN)
        y_ref[h:, :h] = y_ref[h:, :h] - mm(e21, y1, NN) - mm(e22, y2[:, :h], NN)
        y_ref[h:, h:] = y_ref[h:, h:] - mm(e22, y2[:, h:], NN)
        return carry

    lax.fori_loop(0, 2, rough, 0)

    def pair(x, y, dims):
        (xh, xl), (yh, yl) = x, y
        return mm(xh, yh, dims) + (mm(xh, yl, dims) + mm(xl, yh, dims))

    def fine(carry):
        step, _ = carry
        y1 = halves(y_ref[:h, :h])
        y2 = halves(y_ref[h:, :])
        y21 = y2[0][:, :h]
        y22 = y2[0][:, h:]
        g1 = halves(pair((ah_ref[:, :h], al_ref[:, :h]), y1, NT))
        g2 = halves(pair((ah_ref[...], al_ref[...]), y2, NT))
        e1 = (pair(y1, (g1[0][:h], g1[1][:h]), NN) - eye) * weight
        e21 = pair(y2, g1, NN)
        e22 = (pair(y2, g2, NN) - eye) * weight
        worst = jnp.sum(e1 * e1) + jnp.sum(e21 * e21) + jnp.sum(e22 * e22)
        e1 = e1.astype(jnp.bfloat16)
        e21 = e21.astype(jnp.bfloat16)
        e22 = e22.astype(jnp.bfloat16)
        y_ref[:h, :h] = y_ref[:h, :h] - mm(e1, y1[0], NN)
        y_ref[h:, :h] = y_ref[h:, :h] - (mm(e21, y1[0], NN) + mm(e22, y21, NN))
        y_ref[h:, h:] = y_ref[h:, h:] - mm(e22, y22, NN)
        return step + 1, worst

    def unfinished(carry):
        step, worst = carry
        return (step < 40) & jnp.logical_not(worst < LIMIT)

    _, worst = lax.while_loop(unfinished, fine, (jnp.int32(0), jnp.float32(1.0)))

    @pl.when(jnp.logical_not(worst < LIMIT))
    def _():
        row_id = lax.broadcasted_iota(jnp.int32, (n, 1), 0)
        col_id = lax.broadcasted_iota(jnp.int32, (1, n), 1)
        w_ref[...] = a_ref[...]
        y_ref[...] = jnp.where(row_id == col_id, 1.0, 0.0)

        def eliminate(k, carry):
            w = w_ref[...]
            y = y_ref[...]
            row = w_ref[pl.ds(k, 1), :]
            scale = lax.rsqrt(jnp.sum(jnp.where(col_id == k, row, 0.0)))
            row = row * scale
            row_y = y_ref[pl.ds(k, 1), :] * scale
            col = jnp.sum(jnp.where(col_id == k, w, 0.0), axis=1, keepdims=True) * scale
            below = jnp.where(row_id > k, col, 0.0)
            here = row_id == k
            w_ref[...] = jnp.where(here, row, w - below * row)
            y_ref[...] = jnp.where(here, row_y, y - below * row_y)
            return carry

        lax.fori_loop(0, n, eliminate, 0)

    block_row = lax.axis_index("leaf") % group
    block_col = lax.axis_index("front")
    pivots = n // b
    w_ref[:, :b] = ai_ref[...]
    w_ref[:, b : 2 * b] = aj_ref[...]
    right_h, right_l = halves(w_ref[:, : 2 * b])
    y1 = halves(y_ref[:h, :h])
    y2 = halves(y_ref[h:, :])
    w_ref[:h, : 2 * b] = pair(y1, (right_h[:h], right_l[:h]), NN)
    w_ref[h:, : 2 * b] = pair(y2, (right_h, right_l), NN)
    schur = aij_ref[...] - mm3(w_ref[:, :b], w_ref[:, b : 2 * b], TN)
    picked = w_ref[pl.ds(pl.multiple_of(jnp.minimum(block_col, pivots - 1) * b, b), b), :b].T
    r = block_row * b + lax.broadcasted_iota(jnp.int32, (b, b), 0)
    c = block_col * b + lax.broadcasted_iota(jnp.int32, (b, b), 1)
    left = jnp.where(c <= r, picked, 0.0)
    right = jnp.where(block_row >= pivots, schur, 0.0)
    out_ref[...] = jnp.where(block_col >= pivots, right, left)


def finish(group, corner, ai, aj, aij):
    n, b = ai.shape
    vmem = pl.BlockSpec(memory_space=pltpu.VMEM)
    return pl.pallas_call(
        functools.partial(finish_kernel, group),
        out_shape=jax.ShapeDtypeStruct((b, b), jnp.float32),
        in_specs=[vmem] * 4,
        out_specs=vmem,
        scratch_shapes=[pltpu.VMEM((n, n), jnp.float32)] * 3 + [pltpu.VMEM((n, n), jnp.bfloat16)] * 2,
    )(corner, ai, aj, aij)

PIV = 512
LIMIT = 4e-3
CHUNKS = (4, 4, 4, 4)
EARLY = 6
MESH = pl.DeviceIdType.MESH


def assemble_kernel(
    group, chips, coupling_hbm, factor_hbm, tops_ref, pattern_ref, size_ref, map_ref,
    own_ref, corner_ref, row_ref, col_ref,
    coupling_ref, factor_ref, in_sem,
    bufs, acc, part_ref, top_ref, block_ref,
    got_slice, got_block, piece, pieces,
    chunk_recv, chunk_plus, chunk_minus, chunk_twin, top_sem,
    slice_send, slice_recv, block_send, block_recv, piece_send, piece_recv,
    corner_top, row_top, corner_sum, row_sum,
    top_send, top_recv, sum_send, sum_recv,
):
    blocks, b, _ = part_ref.shape
    pivots = row_ref.shape[0]
    rows = piece.shape[0]
    per_block = b // rows
    leaf = lax.axis_index("leaf")
    front = lax.axis_index("front")
    base = leaf // group * group
    me = leaf - base
    z = front // 2
    core = front % 2
    twin = z * 2 + 1 - core
    above = (z + 1) % chips * 2 + core
    below = (z + chips - 1) % chips * 2 + core

    def other(d):
        return (me + d) % group

    parts = len(bufs)
    firsts = [sum(CHUNKS[:k]) for k in range(parts)]

    def input_copies(k):
        first, supers = firsts[k], CHUNKS[k]
        return (
            pltpu.make_async_copy(
                coupling_hbm.at[pl.ds(first * b, supers * b), :],
                coupling_ref.at[pl.ds(first * b, supers * b), :],
                in_sem.at[0, k],
            ),
            pltpu.make_async_copy(
                factor_hbm.at[pl.ds(first, supers)], factor_ref.at[pl.ds(first, supers)],
                in_sem.at[1, k],
            ),
        )

    for k in range(parts):
        for copy in input_copies(k):
            copy.start()
    top_copy = pltpu.make_async_copy(
        tops_ref.at[leaf // group, pl.ds(0, pivots * b), :], top_ref, top_sem.at[0]
    )
    own_copy = pltpu.make_async_copy(
        tops_ref.at[leaf // group, pl.ds(pl.multiple_of(me * b, b), b), :], block_ref, top_sem.at[1]
    )
    top_copy.start()
    own_copy.start()

    barrier = pltpu.get_barrier_semaphore()

    def greet(d, carry):
        pl.semaphore_signal(barrier, 1, device_id=(base + other(d), front), device_id_type=MESH)
        return carry

    lax.fori_loop(1, group, greet, 0)
    for side in (twin, above, below):
        pl.semaphore_signal(barrier, 1, device_id=(leaf, side), device_id_type=MESH)

    half = chips // 2
    row_id = lax.broadcasted_iota(jnp.int32, (b, b), 0)

    def solve(k):
        for copy in input_copies(k):
            copy.wait()
        for r in range(CHUNKS[k]):
            n = firsts[k] + r
            solved = mm(factor_ref[n], coupling_ref[n * b : (n + 1) * b, :], NN)
            live = jnp.where(row_id + n * b < size_ref[0], pattern_ref[0, 0, n], 0)
            kept = jnp.where(live > 0, solved, 0.0)
            bufs[k][front, :, r * b : (r + 1) * b] = kept.T.astype(jnp.bfloat16)

    def chunk_copy(k, block, sem, to):
        return pltpu.make_async_remote_copy(
            bufs[k].at[block], bufs[k].at[block], sem.at[k, block], chunk_recv.at[k, block],
            device_id=(leaf, to), device_id_type=MESH,
        )

    def block_at(d):
        return (z + d + chips) % chips * 2 + core

    def reach(k):
        return (half, half - 1) if k % 2 else (half - 1, half)

    def launch(k):
        chunk_copy(k, front, chunk_plus, above).start()
        chunk_copy(k, front, chunk_minus, below).start()
        chunk_copy(k, front, chunk_twin, twin).start()

    def relay(k, d):
        up, down = reach(k)
        if d <= up:
            block = block_at(-d)
            chunk_copy(k, block, chunk_plus, above).wait_recv()
            if d < up:
                chunk_copy(k, block, chunk_plus, above).start()
            chunk_copy(k, block, chunk_twin, twin).start()
        if d <= down:
            block = block_at(d)
            chunk_copy(k, block, chunk_minus, below).wait_recv()
            if d < down:
                chunk_copy(k, block, chunk_minus, below).start()
            chunk_copy(k, block, chunk_twin, twin).start()

    def twins(k):
        def one(n, carry):
            chunk_copy(k, n * 2 + 1 - core, chunk_twin, twin).wait_recv()
            return carry

        lax.fori_loop(0, chips, one, 0)

    places = []
    for n in range(blocks):
        place = n
        for level in range(map_ref.shape[0]):
            place = map_ref[level, 0, place]
        places.append(place)

    def source(at):
        found = [jnp.where(places[n] == at, n, 0) for n in range(blocks)]
        return functools.reduce(jnp.maximum, found)

    def gram(k):
        picked = bufs[k][source(front)]

        def one(n, carry):
            two = bufs[k][pl.ds(n * 2, 2)].reshape(2 * b, picked.shape[1])
            add = mm(two, picked, NT).reshape(2, b, b)
            if k == 0:
                acc[pl.ds(n * 2, 2)] = add
            else:
                acc[pl.ds(n * 2, 2)] = acc[pl.ds(n * 2, 2)] + add
            return carry

        lax.fori_loop(0, blocks // 2, one, 0, unroll=True)

    items = [(0, (p, q), q) for q in range(pivots) for p in range(q, pivots)]
    items += [(1, (p,), me) for p in range(pivots)]
    top_set = ((corner_top, row_top), top_send, top_recv)
    sum_set = ((corner_sum, row_sum), sum_send, sum_recv)

    def top_block(p):
        return top_ref.at[p * b : (p + 1) * b, :]

    def piece_block(p):
        return pieces.at[p * b : (p + 1) * b, :]

    def item_copy(chosen, n, src, way, to):
        refs, send, recv = chosen
        which, at, _ = items[n]
        dst = refs[which].at[at]
        return pltpu.make_async_remote_copy(
            dst if src is None else src, dst, send.at[way, n], recv.at[n],
            device_id=(leaf, to), device_id_type=MESH,
        )

    def roles(source):
        lane = core == source % 2
        far = (z + chips - source // 2) % chips
        return lane, far, lane & (far < half), lane & ((far == 0) | (far > half + 1))

    def items_launch(chosen, block):
        for n, (which, at, source) in enumerate(items):
            lane, far, plus, minus = roles(source)

            @pl.when(lane & (far == 0))
            def _():
                src = block(at[0])
                item_copy(chosen, n, src, 0, above).start()
                item_copy(chosen, n, src, 1, below).start()
                item_copy(chosen, n, src, 2, twin).start()
                chosen[0][which][at] = src[...]

    def relay_hop(t, chosen):
        for n, (which, at, source) in enumerate(items):
            lane, far, plus, minus = roles(source)

            @pl.when(lane & (jnp.minimum(far, chips - far) == t))
            def _():
                item_copy(chosen, n, None, 2, twin).wait_recv()

                @pl.when(plus)
                def _():
                    item_copy(chosen, n, None, 0, above).start()

                @pl.when(minus)
                def _():
                    item_copy(chosen, n, None, 1, below).start()

                item_copy(chosen, n, None, 2, twin).start()

    def gather(window):
        solve(0)
        pl.semaphore_wait(barrier, group - 1 + 3)
        launch(0)
        for k in range(1, parts):
            solve(k)
            if k < window:
                launch(k)
        for first in range(0, parts, window):
            last = first + window == parts
            for d in range(1, half + 1):
                for k in range(first, first + window):
                    relay(k, d)
                    if d == half - 1 and not last:
                        launch(k + window)
                    if d == half and last:
                        if k == first:
                            top_copy.wait()
                            own_copy.wait()
                            items_launch(top_set, top_block)
                        twins(k)
                        if k < parts - 1:
                            gram(k)
                if first:
                    for k in range(first - window, first)[d - 1 :: half]:
                        twins(k)
                        gram(k)

    gather(2)
    final = parts - 1
    picked = bufs[final][source(front)]
    for at in range(pivots):
        found = source(at)
        part_ref[at] = -(acc[found] + mm(bufs[final][found], picked, NT)).astype(jnp.bfloat16)

    def slice_copy(to, src):
        return pltpu.make_async_remote_copy(
            part_ref.at[to // per_block, pl.ds(to % per_block * rows, rows), :],
            got_slice.at[src], slice_send.at[to], slice_recv.at[src],
            device_id=(base + to, front), device_id_type=MESH,
        )

    def block_copy(to, src):
        return pltpu.make_async_remote_copy(
            part_ref.at[to], got_block.at[src], block_send.at[to], block_recv.at[src],
            device_id=(base + to, front), device_id_type=MESH,
        )

    def piece_copy(to, src):
        return pltpu.make_async_remote_copy(
            piece, pieces.at[pl.ds(pl.multiple_of(src * rows, rows), rows), :], piece_send.at[to], piece_recv.at[src],
            device_id=(base + to, front), device_id_type=MESH,
        )

    inner = front >= pivots

    def send_slice(d, carry):
        slice_copy(other(d), me).start()
        return carry

    def send_block(d, carry):
        to = other(d)

        @pl.when(inner & (to >= pivots))
        def _():
            block_copy(to, me).start()

        return carry

    lax.fori_loop(1, group, send_slice, 0)
    gram(final)
    for at in range(pivots, blocks):
        part_ref[at] = -acc[source(at)].astype(jnp.bfloat16)
    lax.fori_loop(1, EARLY, send_block, 0)
    relay_hop(1, top_set)

    def add_slice(d, total):
        src = other(d)
        slice_copy(src, src).wait_recv()
        return total + got_slice[src].astype(jnp.float32)

    mine = part_ref[me // per_block, pl.ds(pl.multiple_of(me % per_block * rows, rows), rows), :]
    total = lax.fori_loop(1, group, add_slice, mine.astype(jnp.float32))
    piece[...] = total.astype(jnp.bfloat16)
    pieces[pl.ds(pl.multiple_of(me * rows, rows), rows), :] = total.astype(jnp.bfloat16)

    def send_piece(d, carry):
        piece_copy(other(d), me).start()
        return carry

    lax.fori_loop(1, group, send_piece, 0)
    lax.fori_loop(EARLY, group, send_block, 0)

    def wait_piece(d, carry):
        src = other(d)
        piece_copy(src, src).wait_recv()
        return carry

    relay_hop(2, top_set)
    relay_hop(3, top_set)
    lax.fori_loop(1, group, wait_piece, 0)
    items_launch(sum_set, piece_block)
    for t in range(1, half + 1):
        if t == half:
            relay_hop(half, top_set)
        relay_hop(t, sum_set)
    for chosen in (top_set, sum_set):
        for n in range(len(items)):

            @pl.when(jnp.logical_not(roles(items[n][2])[0]))
            def _():
                item_copy(chosen, n, None, 2, twin).wait_recv()

    for p in range(pivots):
        rows_p = slice(p * b, (p + 1) * b)
        col_ref[p] = top_ref[rows_p, :] + pieces[rows_p, :].astype(jnp.float32)
        row_ref[p] = row_top[p] + row_sum[p].astype(jnp.float32)
        for q in range(p + 1):
            corner_ref[p * (p + 1) // 2 + q] = corner_top[p, q] + corner_sum[p, q].astype(jnp.float32)

    own_ref[...] = block_ref[...] + part_ref[me].astype(jnp.float32)

    @pl.when(inner & (me >= pivots))
    def _():
        def add_block(d, carry):
            src = other(d)
            block_copy(src, src).wait_recv()
            own_ref[...] = own_ref[...] + got_block[src].astype(jnp.float32)
            return carry

        lax.fori_loop(1, group, add_block, 0)

    def drain(d, carry):
        to = other(d)
        slice_copy(to, me).wait_send()
        piece_copy(to, me).wait_send()

        @pl.when(inner & (to >= pivots))
        def _():
            block_copy(to, me).wait_send()

        return carry

    lax.fori_loop(1, group, drain, 0)
    for chosen in (top_set, sum_set):
        for n in range(len(items)):
            lane, far, plus, minus = roles(items[n][2])

            @pl.when(plus)
            def _():
                item_copy(chosen, n, None, 0, above).wait_send()

            @pl.when(minus)
            def _():
                item_copy(chosen, n, None, 1, below).wait_send()

            @pl.when(lane)
            def _():
                item_copy(chosen, n, None, 2, twin).wait_send()

    for k in range(parts):
        up, down = reach(k)
        for d in range(half + 1):
            if d < up:
                chunk_copy(k, block_at(-d), chunk_plus, above).wait_send()
            if d < down:
                chunk_copy(k, block_at(d), chunk_minus, below).wait_send()

        def sent(n, carry):
            chunk_copy(k, n * 2 + core, chunk_twin, twin).wait_send()
            return carry

        lax.fori_loop(0, chips, sent, 0)


def assemble(group, chips, coupling, factors, tops, pattern, sizes, maps):
    b = coupling.shape[1]
    blocks = tops.shape[1] // b
    pivots = PIV // b
    rows = PIV // group
    items = pivots * (pivots + 1) // 2 + pivots
    parts = len(CHUNKS)
    vmem = pl.BlockSpec(memory_space=pltpu.VMEM)
    smem = pl.BlockSpec(memory_space=pltpu.SMEM)
    dma = pltpu.SemaphoreType.DMA
    f32 = jnp.float32
    bf16 = jnp.bfloat16
    return pl.pallas_call(
        functools.partial(assemble_kernel, group, chips),
        out_shape=(
            jax.ShapeDtypeStruct((b, b), f32),
            jax.ShapeDtypeStruct((pivots * (pivots + 1) // 2, b, b), f32),
            jax.ShapeDtypeStruct((pivots, b, b), f32),
            jax.ShapeDtypeStruct((pivots, b, b), f32),
        ),
        in_specs=[pl.BlockSpec(memory_space=pltpu.MemorySpace.HBM)] * 3 + [smem] * 3,
        out_specs=[vmem] * 4,
        scratch_shapes=[
            pltpu.VMEM(coupling.shape, bf16),
            pltpu.VMEM(factors.shape, bf16),
            dma((2, parts)),
            [pltpu.VMEM((blocks, b, size * b), bf16) for size in CHUNKS],
            pltpu.VMEM((blocks, b, b), f32),
            pltpu.VMEM((blocks, b, b), bf16),
            pltpu.VMEM((PIV, b), f32),
            pltpu.VMEM((b, b), f32),
            pltpu.VMEM((group, rows, b), bf16),
            pltpu.VMEM((group, b, b), bf16),
            pltpu.VMEM((rows, b), bf16),
            pltpu.VMEM((PIV, b), bf16),
        ]
        + [dma((parts, blocks))] * 4
        + [dma((2,))]
        + [dma((group,))] * 6
        + [
            pltpu.VMEM((pivots, pivots, b, b), f32),
            pltpu.VMEM((pivots, b, b), f32),
            pltpu.VMEM((pivots, pivots, b, b), bf16),
            pltpu.VMEM((pivots, b, b), bf16),
        ]
        + [dma((3, items)), dma((items,))] * 2,
        compiler_params=pltpu.CompilerParams(collective_id=1, has_side_effects=True),
    )(coupling, factors, tops, pattern, sizes, maps)


def shards(coupling, block_pattern, supernode_inverse, subdomain_sizes, block_maps, top_fronts):
    group = lax.axis_size("leaf") // top_fronts.shape[0]
    chips = lax.axis_size("front") // 2
    own, corner, own_row, own_col = assemble(
        group, chips, coupling, supernode_inverse, top_fronts,
        block_pattern.transpose(0, 2, 1), subdomain_sizes, block_maps,
    )
    flat = (PIV, coupling.shape[1])
    return finish(group, corner, own_row.reshape(flat), own_col.reshape(flat), own)


def solution(mesh):
    return jax.shard_map(
        shards,
        mesh=mesh,
        in_specs=(
            P("leaf", "front"),
            P("leaf", None, "front"),
            P("leaf", None, None),
            P("leaf"),
            P(None, "leaf", None),
            P(None, None, "front"),
        ),
        out_specs=P("leaf", "front"),
        check_vma=False,
    )
```

```python
import functools

import jax
import jax.numpy as jnp
from jax import lax
from jax.experimental import pallas as pl
from jax.experimental.pallas import tpu as pltpu
from jax.sharding import PartitionSpec as P

NN = (((1,), (0,)), ((), ()))
NT = (((1,), (1,)), ((), ()))
TN = (((0,), (0,)), ((), ()))


def halves(x):
    hi = x.astype(jnp.bfloat16)
    return hi, (x - hi.astype(jnp.float32)).astype(jnp.bfloat16)


def mm(a, b, dims):
    return lax.dot_general(a, b, dims, preferred_element_type=jnp.float32)


def mm3(a, b, dims):
    ah, al = halves(a)
    bh, bl = halves(b)
    return mm(ah, bh, dims) + (mm(ah, bl, dims) + mm(al, bh, dims))


def finish_kernel(group, corner_ref, ai_ref, aj_ref, aij_ref, out_ref, a_ref, y_ref, w_ref, ah_ref, al_ref):
    n = a_ref.shape[0]
    h = n // 2
    b = ai_ref.shape[1]
    for p in range(n // b):
        for q in range(p + 1):
            block = corner_ref[p * (p + 1) // 2 + q]
            a_ref[p * b : (p + 1) * b, q * b : (q + 1) * b] = block
            if q < p:
                a_ref[q * b : (q + 1) * b, p * b : (p + 1) * b] = block.T
    rows = lax.broadcasted_iota(jnp.int32, (h, h), 0)
    cols = lax.broadcasted_iota(jnp.int32, (h, h), 1)
    eye = (rows == cols).astype(jnp.float32)
    weight = jnp.where(rows > cols, 1.0, jnp.where(rows == cols, 0.5, 0.0))
    for at in (0, h):
        diag = jnp.sum(a_ref[at : at + h, at : at + h] * eye, axis=0, keepdims=True)
        y_ref[at : at + h, at : at + h] = eye * lax.rsqrt(diag)
        y_ref[at : at + h, h - at : n - at] = jnp.zeros((h, h), jnp.float32)
    ah, al = halves(a_ref[...])
    ah_ref[...] = ah
    al_ref[...] = al

    def rough(_, carry):
        ab = ah_ref[...]
        y1 = y_ref[:h, :h].astype(jnp.bfloat16)
        y2 = y_ref[h:, :].astype(jnp.bfloat16)
        g1 = mm(ab[:, :h], y1, NT).astype(jnp.bfloat16)
        g2 = mm(ab, y2, NT).astype(jnp.bfloat16)
        e1 = (mm(y1, g1[:h], NN) - eye) * weight
        e21 = mm(y2, g1, NN)
        e22 = (mm(y2, g2, NN) - eye) * weight
        e1 = e1.astype(jnp.bfloat16)
        e21 = e21.astype(jnp.bfloat16)
        e22 = e22.astype(jnp.bfloat16)
        y_ref[:h, :h] = y_ref[:h, :h] - mm(e1, y1, NN)
        y_ref[h:, :h] = y_ref[h:, :h] - mm(e21, y1, NN) - mm(e22, y2[:, :h], NN)
        y_ref[h:, h:] = y_ref[h:, h:] - mm(e22, y2[:, h:], NN)
        return carry

    lax.fori_loop(0, 2, rough, 0)

    def pair(x, y, dims):
        (xh, xl), (yh, yl) = x, y
        return mm(xh, yh, dims) + (mm(xh, yl, dims) + mm(xl, yh, dims))

    def fine(carry):
        step, _ = carry
        y1 = halves(y_ref[:h, :h])
        y2 = halves(y_ref[h:, :])
        y21 = y2[0][:, :h]
        y22 = y2[0][:, h:]
        g1 = halves(pair((ah_ref[:, :h], al_ref[:, :h]), y1, NT))
        g2 = halves(pair((ah_ref[...], al_ref[...]), y2, NT))
        e1 = (pair(y1, (g1[0][:h], g1[1][:h]), NN) - eye) * weight
        e21 = pair(y2, g1, NN)
        e22 = (pair(y2, g2, NN) - eye) * weight
        worst = jnp.sum(e1 * e1) + jnp.sum(e21 * e21) + jnp.sum(e22 * e22)
        e1 = e1.astype(jnp.bfloat16)
        e21 = e21.astype(jnp.bfloat16)
        e22 = e22.astype(jnp.bfloat16)
        y_ref[:h, :h] = y_ref[:h, :h] - mm(e1, y1[0], NN)
        y_ref[h:, :h] = y_ref[h:, :h] - (mm(e21, y1[0], NN) + mm(e22, y21, NN))
        y_ref[h:, h:] = y_ref[h:, h:] - mm(e22, y22, NN)
        return step + 1, worst

    def unfinished(carry):
        step, worst = carry
        return (step < 40) & jnp.logical_not(worst < LIMIT)

    _, worst = lax.while_loop(unfinished, fine, (jnp.int32(0), jnp.float32(1.0)))

    @pl.when(jnp.logical_not(worst < LIMIT))
    def _():
        row_id = lax.broadcasted_iota(jnp.int32, (n, 1), 0)
        col_id = lax.broadcasted_iota(jnp.int32, (1, n), 1)
        w_ref[...] = a_ref[...]
        y_ref[...] = jnp.where(row_id == col_id, 1.0, 0.0)

        def eliminate(k, carry):
            w = w_ref[...]
            y = y_ref[...]
            row = w_ref[pl.ds(k, 1), :]
            scale = lax.rsqrt(jnp.sum(jnp.where(col_id == k, row, 0.0)))
            row = row * scale
            row_y = y_ref[pl.ds(k, 1), :] * scale
            col = jnp.sum(jnp.where(col_id == k, w, 0.0), axis=1, keepdims=True) * scale
            below = jnp.where(row_id > k, col, 0.0)
            here = row_id == k
            w_ref[...] = jnp.where(here, row, w - below * row)
            y_ref[...] = jnp.where(here, row_y, y - below * row_y)
            return carry

        lax.fori_loop(0, n, eliminate, 0)

    block_row = lax.axis_index("leaf") % group
    block_col = lax.axis_index("front")
    pivots = n // b
    w_ref[:, :b] = ai_ref[...]
    w_ref[:, b : 2 * b] = aj_ref[...]
    right_h, right_l = halves(w_ref[:, : 2 * b])
    y1 = halves(y_ref[:h, :h])
    y2 = halves(y_ref[h:, :])
    w_ref[:h, : 2 * b] = pair(y1, (right_h[:h], right_l[:h]), NN)
    w_ref[h:, : 2 * b] = pair(y2, (right_h, right_l), NN)
    schur = aij_ref[...] - mm3(w_ref[:, :b], w_ref[:, b : 2 * b], TN)
    picked = w_ref[pl.ds(pl.multiple_of(jnp.minimum(block_col, pivots - 1) * b, b), b), :b].T
    r = block_row * b + lax.broadcasted_iota(jnp.int32, (b, b), 0)
    c = block_col * b + lax.broadcasted_iota(jnp.int32, (b, b), 1)
    left = jnp.where(c <= r, picked, 0.0)
    right = jnp.where(block_row >= pivots, schur, 0.0)
    out_ref[...] = jnp.where(block_col >= pivots, right, left)


def finish(group, corner, ai, aj, aij):
    n, b = ai.shape
    vmem = pl.BlockSpec(memory_space=pltpu.VMEM)
    return pl.pallas_call(
        functools.partial(finish_kernel, group),
        out_shape=jax.ShapeDtypeStruct((b, b), jnp.float32),
        in_specs=[vmem] * 4,
        out_specs=vmem,
        scratch_shapes=[pltpu.VMEM((n, n), jnp.float32)] * 3 + [pltpu.VMEM((n, n), jnp.bfloat16)] * 2,
    )(corner, ai, aj, aij)

PIV = 512
LIMIT = 4e-3
CHUNKS = (8, 8)
EARLY = 6
MESH = pl.DeviceIdType.MESH


def assemble_kernel(
    group, chips, coupling_hbm, factor_hbm, tops_ref, pattern_ref, size_ref, map_ref,
    own_ref, corner_ref, row_ref, col_ref,
    coupling_ref, factor_ref, in_sem,
    bufs, acc, part_ref, top_ref, block_ref,
    got_slice, got_block, piece, pieces,
    chunk_recv, chunk_plus, chunk_minus, chunk_twin, top_sem,
    slice_send, slice_recv, block_send, block_recv, piece_send, piece_recv,
    corner_top, row_top, corner_sum, row_sum,
    top_send, top_recv, sum_send, sum_recv,
):
    blocks, b, _ = part_ref.shape
    pivots = row_ref.shape[0]
    rows = piece.shape[0]
    per_block = b // rows
    leaf = lax.axis_index("leaf")
    front = lax.axis_index("front")
    base = leaf // group * group
    me = leaf - base
    z = front // 2
    core = front % 2
    twin = z * 2 + 1 - core
    above = (z + 1) % chips * 2 + core
    below = (z + chips - 1) % chips * 2 + core

    def other(d):
        return (me + d) % group

    parts = len(bufs)
    firsts = [sum(CHUNKS[:k]) for k in range(parts)]

    def input_copies(k):
        first, supers = firsts[k], CHUNKS[k]
        return (
            pltpu.make_async_copy(
                coupling_hbm.at[pl.ds(first * b, supers * b), :],
                coupling_ref.at[pl.ds(first * b, supers * b), :],
                in_sem.at[0, k],
            ),
            pltpu.make_async_copy(
                factor_hbm.at[pl.ds(first, supers)], factor_ref.at[pl.ds(first, supers)],
                in_sem.at[1, k],
            ),
        )

    for k in range(parts):
        for copy in input_copies(k):
            copy.start()
    top_copy = pltpu.make_async_copy(
        tops_ref.at[leaf // group, pl.ds(0, pivots * b), :], top_ref, top_sem.at[0]
    )
    own_copy = pltpu.make_async_copy(
        tops_ref.at[leaf // group, pl.ds(pl.multiple_of(me * b, b), b), :], block_ref, top_sem.at[1]
    )
    top_copy.start()
    own_copy.start()

    barrier = pltpu.get_barrier_semaphore()

    def greet(d, carry):
        pl.semaphore_signal(barrier, 1, device_id=(base + other(d), front), device_id_type=MESH)
        return carry

    lax.fori_loop(1, group, greet, 0)
    for side in (twin, above, below):
        pl.semaphore_signal(barrier, 1, device_id=(leaf, side), device_id_type=MESH)

    half = chips // 2
    row_id = lax.broadcasted_iota(jnp.int32, (b, b), 0)

    def solve(k):
        for copy in input_copies(k):
            copy.wait()
        for r in range(CHUNKS[k]):
            n = firsts[k] + r
            solved = mm(factor_ref[n], coupling_ref[n * b : (n + 1) * b, :], NN)
            live = jnp.where(row_id + n * b < size_ref[0], pattern_ref[0, 0, n], 0)
            kept = jnp.where(live > 0, solved, 0.0)
            bufs[k][front, :, r * b : (r + 1) * b] = kept.T.astype(jnp.bfloat16)

    def chunk_copy(k, block, sem, to):
        return pltpu.make_async_remote_copy(
            bufs[k].at[block], bufs[k].at[block], sem.at[k, block], chunk_recv.at[k, block],
            device_id=(leaf, to), device_id_type=MESH,
        )

    def block_at(d):
        return (z + d + chips) % chips * 2 + core

    def reach(k):
        return (half, half - 1) if k % 2 else (half - 1, half)

    def launch(k):
        chunk_copy(k, front, chunk_plus, above).start()
        chunk_copy(k, front, chunk_minus, below).start()
        chunk_copy(k, front, chunk_twin, twin).start()

    def relay(k, d):
        up, down = reach(k)
        if d <= up:
            block = block_at(-d)
            chunk_copy(k, block, chunk_plus, above).wait_recv()
            if d < up:
                chunk_copy(k, block, chunk_plus, above).start()
            chunk_copy(k, block, chunk_twin, twin).start()
        if d <= down:
            block = block_at(d)
            chunk_copy(k, block, chunk_minus, below).wait_recv()
            if d < down:
                chunk_copy(k, block, chunk_minus, below).start()
            chunk_copy(k, block, chunk_twin, twin).start()

    def twins(k):
        def one(n, carry):
            chunk_copy(k, n * 2 + 1 - core, chunk_twin, twin).wait_recv()
            return carry

        lax.fori_loop(0, chips, one, 0)

    places = []
    for n in range(blocks):
        place = n
        for level in range(map_ref.shape[0]):
            place = map_ref[level, 0, place]
        places.append(place)

    def source(at):
        found = [jnp.where(places[n] == at, n, 0) for n in range(blocks)]
        return functools.reduce(jnp.maximum, found)

    def gram(k):
        picked = bufs[k][source(front)]

        def one(n, carry):
            two = bufs[k][pl.ds(n * 2, 2)].reshape(2 * b, picked.shape[1])
            add = mm(two, picked, NT).reshape(2, b, b)
            if k == 0:
                acc[pl.ds(n * 2, 2)] = add
            else:
                acc[pl.ds(n * 2, 2)] = acc[pl.ds(n * 2, 2)] + add
            return carry

        lax.fori_loop(0, blocks // 2, one, 0, unroll=True)

    items = [(0, (p, q), q) for q in range(pivots) for p in range(q, pivots)]
    items += [(1, (p,), me) for p in range(pivots)]
    top_set = ((corner_top, row_top), top_send, top_recv)
    sum_set = ((corner_sum, row_sum), sum_send, sum_recv)

    def top_block(p):
        return top_ref.at[p * b : (p + 1) * b, :]

    def piece_block(p):
        return pieces.at[p * b : (p + 1) * b, :]

    def item_copy(chosen, n, src, way, to):
        refs, send, recv = chosen
        which, at, _ = items[n]
        dst = refs[which].at[at]
        return pltpu.make_async_remote_copy(
            dst if src is None else src, dst, send.at[way, n], recv.at[n],
            device_id=(leaf, to), device_id_type=MESH,
        )

    def roles(source):
        lane = core == source % 2
        far = (z + chips - source // 2) % chips
        return lane, far, lane & (far < half), lane & ((far == 0) | (far > half + 1))

    def items_launch(chosen, block):
        for n, (which, at, source) in enumerate(items):
            lane, far, plus, minus = roles(source)

            @pl.when(lane & (far == 0))
            def _():
                src = block(at[0])
                item_copy(chosen, n, src, 0, above).start()
                item_copy(chosen, n, src, 1, below).start()
                item_copy(chosen, n, src, 2, twin).start()
                chosen[0][which][at] = src[...]

    def relay_hop(t, chosen):
        for n, (which, at, source) in enumerate(items):
            lane, far, plus, minus = roles(source)

            @pl.when(lane & (jnp.minimum(far, chips - far) == t))
            def _():
                item_copy(chosen, n, None, 2, twin).wait_recv()

                @pl.when(plus)
                def _():
                    item_copy(chosen, n, None, 0, above).start()

                @pl.when(minus)
                def _():
                    item_copy(chosen, n, None, 1, below).start()

                item_copy(chosen, n, None, 2, twin).start()

    def gather(window):
        solve(0)
        pl.semaphore_wait(barrier, group - 1 + 3)
        launch(0)
        for k in range(1, parts):
            solve(k)
            if k < window:
                launch(k)
        for first in range(0, parts, window):
            last = first + window == parts
            for d in range(1, half + 1):
                for k in range(first, first + window):
                    relay(k, d)
                    if d == half - 1 and not last:
                        launch(k + window)
                    if d == half and last:
                        if k == first:
                            top_copy.wait()
                            own_copy.wait()
                            items_launch(top_set, top_block)
                        twins(k)
                        if k < parts - 1:
                            gram(k)
                if first:
                    for k in range(first - window, first)[d - 1 :: half]:
                        twins(k)
                        gram(k)

    gather(2)
    final = parts - 1
    picked = bufs[final][source(front)]
    for at in range(pivots):
        found = source(at)
        part_ref[at] = -(acc[found] + mm(bufs[final][found], picked, NT)).astype(jnp.bfloat16)

    def slice_copy(to, src):
        return pltpu.make_async_remote_copy(
            part_ref.at[to // per_block, pl.ds(to % per_block * rows, rows), :],
            got_slice.at[src], slice_send.at[to], slice_recv.at[src],
            device_id=(base + to, front), device_id_type=MESH,
        )

    def block_copy(to, src):
        return pltpu.make_async_remote_copy(
            part_ref.at[to], got_block.at[src], block_send.at[to], block_recv.at[src],
            device_id=(base + to, front), device_id_type=MESH,
        )

    def piece_copy(to, src):
        return pltpu.make_async_remote_copy(
            piece, pieces.at[pl.ds(pl.multiple_of(src * rows, rows), rows), :], piece_send.at[to], piece_recv.at[src],
            device_id=(base + to, front), device_id_type=MESH,
        )

    inner = front >= pivots

    def send_slice(d, carry):
        slice_copy(other(d), me).start()
        return carry

    def send_block(d, carry):
        to = other(d)

        @pl.when(inner & (to >= pivots))
        def _():
            block_copy(to, me).start()

        return carry

    lax.fori_loop(1, group, send_slice, 0)
    gram(final)
    for at in range(pivots, blocks):
        part_ref[at] = -acc[source(at)].astype(jnp.bfloat16)
    lax.fori_loop(1, EARLY, send_block, 0)
    relay_hop(1, top_set)

    def add_slice(d, total):
        src = other(d)
        slice_copy(src, src).wait_recv()
        return total + got_slice[src].astype(jnp.float32)

    mine = part_ref[me // per_block, pl.ds(pl.multiple_of(me % per_block * rows, rows), rows), :]
    total = lax.fori_loop(1, group, add_slice, mine.astype(jnp.float32))
    piece[...] = total.astype(jnp.bfloat16)
    pieces[pl.ds(pl.multiple_of(me * rows, rows), rows), :] = total.astype(jnp.bfloat16)

    def send_piece(d, carry):
        piece_copy(other(d), me).start()
        return carry

    lax.fori_loop(1, group, send_piece, 0)
    lax.fori_loop(EARLY, group, send_block, 0)

    def wait_piece(d, carry):
        src = other(d)
        piece_copy(src, src).wait_recv()
        return carry

    relay_hop(2, top_set)
    relay_hop(3, top_set)
    lax.fori_loop(1, group, wait_piece, 0)
    items_launch(sum_set, piece_block)
    for t in range(1, half):
        relay_hop(t, sum_set)
    own_ref[...] = block_ref[...] + part_ref[me].astype(jnp.float32)

    @pl.when(inner & (me >= pivots))
    def _():
        def add_block(d, carry):
            src = other(d)
            block_copy(src, src).wait_recv()
            own_ref[...] = own_ref[...] + got_block[src].astype(jnp.float32)
            return carry

        lax.fori_loop(1, group, add_block, 0)

    relay_hop(half, top_set)
    relay_hop(half, sum_set)
    for chosen in (top_set, sum_set):
        for n in range(len(items)):

            @pl.when(jnp.logical_not(roles(items[n][2])[0]))
            def _():
                item_copy(chosen, n, None, 2, twin).wait_recv()

    for p in range(pivots):
        rows_p = slice(p * b, (p + 1) * b)
        col_ref[p] = top_ref[rows_p, :] + pieces[rows_p, :].astype(jnp.float32)
        row_ref[p] = row_top[p] + row_sum[p].astype(jnp.float32)
        for q in range(p + 1):
            corner_ref[p * (p + 1) // 2 + q] = corner_top[p, q] + corner_sum[p, q].astype(jnp.float32)

    def drain(d, carry):
        to = other(d)
        slice_copy(to, me).wait_send()
        piece_copy(to, me).wait_send()

        @pl.when(inner & (to >= pivots))
        def _():
            block_copy(to, me).wait_send()

        return carry

    lax.fori_loop(1, group, drain, 0)
    for chosen in (top_set, sum_set):
        for n in range(len(items)):
            lane, far, plus, minus = roles(items[n][2])

            @pl.when(plus)
            def _():
                item_copy(chosen, n, None, 0, above).wait_send()

            @pl.when(minus)
            def _():
                item_copy(chosen, n, None, 1, below).wait_send()

            @pl.when(lane)
            def _():
                item_copy(chosen, n, None, 2, twin).wait_send()

    for k in range(parts):
        up, down = reach(k)
        for d in range(half + 1):
            if d < up:
                chunk_copy(k, block_at(-d), chunk_plus, above).wait_send()
            if d < down:
                chunk_copy(k, block_at(d), chunk_minus, below).wait_send()

        def sent(n, carry):
            chunk_copy(k, n * 2 + core, chunk_twin, twin).wait_send()
            return carry

        lax.fori_loop(0, chips, sent, 0)


def assemble(group, chips, coupling, factors, tops, pattern, sizes, maps):
    b = coupling.shape[1]
    blocks = tops.shape[1] // b
    pivots = PIV // b
    rows = PIV // group
    items = pivots * (pivots + 1) // 2 + pivots
    parts = len(CHUNKS)
    vmem = pl.BlockSpec(memory_space=pltpu.VMEM)
    smem = pl.BlockSpec(memory_space=pltpu.SMEM)
    dma = pltpu.SemaphoreType.DMA
    f32 = jnp.float32
    bf16 = jnp.bfloat16
    return pl.pallas_call(
        functools.partial(assemble_kernel, group, chips),
        out_shape=(
            jax.ShapeDtypeStruct((b, b), f32),
            jax.ShapeDtypeStruct((pivots * (pivots + 1) // 2, b, b), f32),
            jax.ShapeDtypeStruct((pivots, b, b), f32),
            jax.ShapeDtypeStruct((pivots, b, b), f32),
        ),
        in_specs=[pl.BlockSpec(memory_space=pltpu.MemorySpace.HBM)] * 3 + [smem] * 3,
        out_specs=[vmem] * 4,
        scratch_shapes=[
            pltpu.VMEM(coupling.shape, bf16),
            pltpu.VMEM(factors.shape, bf16),
            dma((2, parts)),
            [pltpu.VMEM((blocks, b, size * b), bf16) for size in CHUNKS],
            pltpu.VMEM((blocks, b, b), f32),
            pltpu.VMEM((blocks, b, b), bf16),
            pltpu.VMEM((PIV, b), f32),
            pltpu.VMEM((b, b), f32),
            pltpu.VMEM((group, rows, b), bf16),
            pltpu.VMEM((group, b, b), bf16),
            pltpu.VMEM((rows, b), bf16),
            pltpu.VMEM((PIV, b), bf16),
        ]
        + [dma((parts, blocks))] * 4
        + [dma((2,))]
        + [dma((group,))] * 6
        + [
            pltpu.VMEM((pivots, pivots, b, b), f32),
            pltpu.VMEM((pivots, b, b), f32),
            pltpu.VMEM((pivots, pivots, b, b), bf16),
            pltpu.VMEM((pivots, b, b), bf16),
        ]
        + [dma((3, items)), dma((items,))] * 2,
        compiler_params=pltpu.CompilerParams(collective_id=1, has_side_effects=True),
    )(coupling, factors, tops, pattern, sizes, maps)


def shards(coupling, block_pattern, supernode_inverse, subdomain_sizes, block_maps, top_fronts):
    group = lax.axis_size("leaf") // top_fronts.shape[0]
    chips = lax.axis_size("front") // 2
    own, corner, own_row, own_col = assemble(
        group, chips, coupling, supernode_inverse, top_fronts,
        block_pattern.transpose(0, 2, 1), subdomain_sizes, block_maps,
    )
    flat = (PIV, coupling.shape[1])
    return finish(group, corner, own_row.reshape(flat), own_col.reshape(flat), own)


def solution(mesh):
    return jax.shard_map(
        shards,
        mesh=mesh,
        in_specs=(
            P("leaf", "front"),
            P("leaf", None, "front"),
            P("leaf", None, None),
            P("leaf"),
            P(None, "leaf", None),
            P(None, None, "front"),
        ),
        out_specs=P("leaf", "front"),
        check_vma=False,
    )
```

```python
import functools

import jax
import jax.numpy as jnp
from jax import lax
from jax.experimental import pallas as pl
from jax.experimental.pallas import tpu as pltpu
from jax.sharding import PartitionSpec as P

NN = (((1,), (0,)), ((), ()))
NT = (((1,), (1,)), ((), ()))
TN = (((0,), (0,)), ((), ()))


def halves(x):
    hi = x.astype(jnp.bfloat16)
    return hi, (x - hi.astype(jnp.float32)).astype(jnp.bfloat16)


def mm(a, b, dims):
    return lax.dot_general(a, b, dims, preferred_element_type=jnp.float32)


def mm3(a, b, dims):
    ah, al = halves(a)
    bh, bl = halves(b)
    return mm(ah, bh, dims) + (mm(ah, bl, dims) + mm(al, bh, dims))


def finish_kernel(
    group, corner_ref, ai_hbm, aj_hbm, aij_hbm, out_ref,
    a_ref, y_ref, w_ref, ah_ref, al_ref, side_ref, aij_ref, side_sem,
):
    n = a_ref.shape[0]
    h = n // 2
    b = ai_hbm.shape[1]
    side_copies = (
        pltpu.make_async_copy(ai_hbm, side_ref.at[0], side_sem.at[0]),
        pltpu.make_async_copy(aj_hbm, side_ref.at[1], side_sem.at[1]),
        pltpu.make_async_copy(aij_hbm, aij_ref, side_sem.at[2]),
    )
    for copy in side_copies:
        copy.start()
    for p in range(n // b):
        for q in range(p + 1):
            block = corner_ref[p * (p + 1) // 2 + q]
            a_ref[p * b : (p + 1) * b, q * b : (q + 1) * b] = block
            if q < p:
                a_ref[q * b : (q + 1) * b, p * b : (p + 1) * b] = block.T
    rows = lax.broadcasted_iota(jnp.int32, (h, h), 0)
    cols = lax.broadcasted_iota(jnp.int32, (h, h), 1)
    eye = (rows == cols).astype(jnp.float32)
    weight = jnp.where(rows > cols, 1.0, jnp.where(rows == cols, 0.5, 0.0))
    for at in (0, h):
        diag = jnp.sum(a_ref[at : at + h, at : at + h] * eye, axis=0, keepdims=True)
        y_ref[at : at + h, at : at + h] = eye * lax.rsqrt(diag)
        y_ref[at : at + h, h - at : n - at] = jnp.zeros((h, h), jnp.float32)
    ah, al = halves(a_ref[...])
    ah_ref[...] = ah
    al_ref[...] = al

    def rough(_, carry):
        ab = ah_ref[...]
        y1 = y_ref[:h, :h].astype(jnp.bfloat16)
        y2 = y_ref[h:, :].astype(jnp.bfloat16)
        g1 = mm(ab[:, :h], y1, NT).astype(jnp.bfloat16)
        g2 = mm(ab, y2, NT).astype(jnp.bfloat16)
        e1 = (mm(y1, g1[:h], NN) - eye) * weight
        e21 = mm(y2, g1, NN)
        e22 = (mm(y2, g2, NN) - eye) * weight
        e1 = e1.astype(jnp.bfloat16)
        e21 = e21.astype(jnp.bfloat16)
        e22 = e22.astype(jnp.bfloat16)
        y_ref[:h, :h] = y_ref[:h, :h] - mm(e1, y1, NN)
        y_ref[h:, :h] = y_ref[h:, :h] - mm(e21, y1, NN) - mm(e22, y2[:, :h], NN)
        y_ref[h:, h:] = y_ref[h:, h:] - mm(e22, y2[:, h:], NN)
        return carry

    lax.fori_loop(0, 2, rough, 0)

    def pair(x, y, dims):
        (xh, xl), (yh, yl) = x, y
        return mm(xh, yh, dims) + (mm(xh, yl, dims) + mm(xl, yh, dims))

    def fine(carry):
        step, _ = carry
        y1 = halves(y_ref[:h, :h])
        y2 = halves(y_ref[h:, :])
        y21 = y2[0][:, :h]
        y22 = y2[0][:, h:]
        g1 = halves(pair((ah_ref[:, :h], al_ref[:, :h]), y1, NT))
        g2 = halves(pair((ah_ref[...], al_ref[...]), y2, NT))
        e1 = (pair(y1, (g1[0][:h], g1[1][:h]), NN) - eye) * weight
        e21 = pair(y2, g1, NN)
        e22 = (pair(y2, g2, NN) - eye) * weight
        worst = jnp.sum(e1 * e1) + jnp.sum(e21 * e21) + jnp.sum(e22 * e22)
        e1 = e1.astype(jnp.bfloat16)
        e21 = e21.astype(jnp.bfloat16)
        e22 = e22.astype(jnp.bfloat16)
        y_ref[:h, :h] = y_ref[:h, :h] - mm(e1, y1[0], NN)
        y_ref[h:, :h] = y_ref[h:, :h] - (mm(e21, y1[0], NN) + mm(e22, y21, NN))
        y_ref[h:, h:] = y_ref[h:, h:] - mm(e22, y22, NN)
        return step + 1, worst

    def unfinished(carry):
        step, worst = carry
        return (step < 40) & jnp.logical_not(worst < LIMIT)

    _, worst = lax.while_loop(unfinished, fine, (jnp.int32(0), jnp.float32(1.0)))

    @pl.when(jnp.logical_not(worst < LIMIT))
    def _():
        row_id = lax.broadcasted_iota(jnp.int32, (n, 1), 0)
        col_id = lax.broadcasted_iota(jnp.int32, (1, n), 1)
        w_ref[...] = a_ref[...]
        y_ref[...] = jnp.where(row_id == col_id, 1.0, 0.0)

        def eliminate(k, carry):
            w = w_ref[...]
            y = y_ref[...]
            row = w_ref[pl.ds(k, 1), :]
            scale = lax.rsqrt(jnp.sum(jnp.where(col_id == k, row, 0.0)))
            row = row * scale
            row_y = y_ref[pl.ds(k, 1), :] * scale
            col = jnp.sum(jnp.where(col_id == k, w, 0.0), axis=1, keepdims=True) * scale
            below = jnp.where(row_id > k, col, 0.0)
            here = row_id == k
            w_ref[...] = jnp.where(here, row, w - below * row)
            y_ref[...] = jnp.where(here, row_y, y - below * row_y)
            return carry

        lax.fori_loop(0, n, eliminate, 0)

    block_row = lax.axis_index("leaf") % group
    block_col = lax.axis_index("front")
    pivots = n // b
    for copy in side_copies:
        copy.wait()
    w_ref[:, :b] = side_ref[0]
    w_ref[:, b : 2 * b] = side_ref[1]
    right_h, right_l = halves(w_ref[:, : 2 * b])
    y1 = halves(y_ref[:h, :h])
    y2 = halves(y_ref[h:, :])
    w_ref[:h, : 2 * b] = pair(y1, (right_h[:h], right_l[:h]), NN)
    w_ref[h:, : 2 * b] = pair(y2, (right_h, right_l), NN)
    schur = aij_ref[...] - mm3(w_ref[:, :b], w_ref[:, b : 2 * b], TN)
    picked = w_ref[pl.ds(pl.multiple_of(jnp.minimum(block_col, pivots - 1) * b, b), b), :b].T
    r = block_row * b + lax.broadcasted_iota(jnp.int32, (b, b), 0)
    c = block_col * b + lax.broadcasted_iota(jnp.int32, (b, b), 1)
    left = jnp.where(c <= r, picked, 0.0)
    right = jnp.where(block_row >= pivots, schur, 0.0)
    out_ref[...] = jnp.where(block_col >= pivots, right, left)


def finish(group, corner, ai, aj, aij):
    n, b = ai.shape
    vmem = pl.BlockSpec(memory_space=pltpu.VMEM)
    return pl.pallas_call(
        functools.partial(finish_kernel, group),
        out_shape=jax.ShapeDtypeStruct((b, b), jnp.float32),
        in_specs=[vmem] + [pl.BlockSpec(memory_space=pl.ANY)] * 3,
        out_specs=vmem,
        scratch_shapes=[pltpu.VMEM((n, n), jnp.float32)] * 3 + [pltpu.VMEM((n, n), jnp.bfloat16)] * 2
        + [pltpu.VMEM((2, n, b), jnp.float32), pltpu.VMEM((b, b), jnp.float32), pltpu.SemaphoreType.DMA((3,))],
    )(corner, ai, aj, aij)

PIV = 512
LIMIT = 4e-3
CHUNKS = (8, 8)
EARLY = 6
MESH = pl.DeviceIdType.MESH


def assemble_kernel(
    group, chips, coupling_hbm, factor_hbm, tops_ref, pattern_ref, size_ref, map_ref,
    own_ref, corner_ref, row_ref, col_ref,
    coupling_ref, factor_ref, in_sem,
    bufs, acc, part_ref, top_ref, block_ref,
    got_slice, got_block, piece, pieces,
    chunk_recv, chunk_plus, chunk_minus, chunk_twin, top_sem,
    slice_send, slice_recv, block_send, block_recv, piece_send, piece_recv,
    corner_top, row_top, corner_sum, row_sum,
    top_send, top_recv, sum_send, sum_recv,
):
    blocks, b, _ = part_ref.shape
    pivots = row_ref.shape[0]
    rows = piece.shape[0]
    per_block = b // rows
    leaf = lax.axis_index("leaf")
    front = lax.axis_index("front")
    base = leaf // group * group
    me = leaf - base
    z = front // 2
    core = front % 2
    twin = z * 2 + 1 - core
    above = (z + 1) % chips * 2 + core
    below = (z + chips - 1) % chips * 2 + core

    def other(d):
        return (me + d) % group

    parts = len(bufs)
    firsts = [sum(CHUNKS[:k]) for k in range(parts)]

    def input_copies(k):
        first, supers = firsts[k], CHUNKS[k]
        return (
            pltpu.make_async_copy(
                coupling_hbm.at[pl.ds(first * b, supers * b), :],
                coupling_ref.at[pl.ds(first * b, supers * b), :],
                in_sem.at[0, k],
            ),
            pltpu.make_async_copy(
                factor_hbm.at[pl.ds(first, supers)], factor_ref.at[pl.ds(first, supers)],
                in_sem.at[1, k],
            ),
        )

    for k in range(parts):
        for copy in input_copies(k):
            copy.start()
    top_copy = pltpu.make_async_copy(
        tops_ref.at[leaf // group, pl.ds(0, pivots * b), :], top_ref, top_sem.at[0]
    )
    own_copy = pltpu.make_async_copy(
        tops_ref.at[leaf // group, pl.ds(pl.multiple_of(me * b, b), b), :], block_ref, top_sem.at[1]
    )
    top_copy.start()
    own_copy.start()

    barrier = pltpu.get_barrier_semaphore()

    def greet(d, carry):
        pl.semaphore_signal(barrier, 1, device_id=(base + other(d), front), device_id_type=MESH)
        return carry

    lax.fori_loop(1, group, greet, 0)
    for side in (twin, above, below):
        pl.semaphore_signal(barrier, 1, device_id=(leaf, side), device_id_type=MESH)

    half = chips // 2
    row_id = lax.broadcasted_iota(jnp.int32, (b, b), 0)

    def solve(k):
        for copy in input_copies(k):
            copy.wait()
        for r in range(CHUNKS[k]):
            n = firsts[k] + r
            solved = mm(factor_ref[n], coupling_ref[n * b : (n + 1) * b, :], NN)
            live = jnp.where(row_id + n * b < size_ref[0], pattern_ref[0, 0, n], 0)
            kept = jnp.where(live > 0, solved, 0.0)
            bufs[k][front, :, r * b : (r + 1) * b] = kept.T.astype(jnp.bfloat16)

    def chunk_copy(k, block, sem, to):
        return pltpu.make_async_remote_copy(
            bufs[k].at[block], bufs[k].at[block], sem.at[k, block], chunk_recv.at[k, block],
            device_id=(leaf, to), device_id_type=MESH,
        )

    def block_at(d):
        return (z + d + chips) % chips * 2 + core

    def reach(k):
        return (half, half - 1) if k % 2 else (half - 1, half)

    def launch(k):
        chunk_copy(k, front, chunk_plus, above).start()
        chunk_copy(k, front, chunk_minus, below).start()
        chunk_copy(k, front, chunk_twin, twin).start()

    def relay(k, d):
        up, down = reach(k)
        if d <= up:
            block = block_at(-d)
            chunk_copy(k, block, chunk_plus, above).wait_recv()
            if d < up:
                chunk_copy(k, block, chunk_plus, above).start()
            chunk_copy(k, block, chunk_twin, twin).start()
        if d <= down:
            block = block_at(d)
            chunk_copy(k, block, chunk_minus, below).wait_recv()
            if d < down:
                chunk_copy(k, block, chunk_minus, below).start()
            chunk_copy(k, block, chunk_twin, twin).start()

    def twins(k):
        def one(n, carry):
            chunk_copy(k, n * 2 + 1 - core, chunk_twin, twin).wait_recv()
            return carry

        lax.fori_loop(0, chips, one, 0)

    places = []
    for n in range(blocks):
        place = n
        for level in range(map_ref.shape[0]):
            place = map_ref[level, 0, place]
        places.append(place)

    def source(at):
        found = [jnp.where(places[n] == at, n, 0) for n in range(blocks)]
        return functools.reduce(jnp.maximum, found)

    def gram(k):
        picked = bufs[k][source(front)]

        def one(n, carry):
            two = bufs[k][pl.ds(n * 2, 2)].reshape(2 * b, picked.shape[1])
            add = mm(two, picked, NT).reshape(2, b, b)
            if k == 0:
                acc[pl.ds(n * 2, 2)] = add
            else:
                acc[pl.ds(n * 2, 2)] = acc[pl.ds(n * 2, 2)] + add
            return carry

        lax.fori_loop(0, blocks // 2, one, 0, unroll=True)

    items = [(0, (p, q), q) for q in range(pivots) for p in range(q, pivots)]
    items += [(1, (p,), me) for p in range(pivots)]
    top_set = ((corner_top, row_top), top_send, top_recv)
    sum_set = ((corner_sum, row_sum), sum_send, sum_recv)

    def top_block(p):
        return top_ref.at[p * b : (p + 1) * b, :]

    def piece_block(p):
        return pieces.at[p * b : (p + 1) * b, :]

    def item_copy(chosen, n, src, way, to):
        refs, send, recv = chosen
        which, at, _ = items[n]
        dst = refs[which].at[at]
        return pltpu.make_async_remote_copy(
            dst if src is None else src, dst, send.at[way, n], recv.at[n],
            device_id=(leaf, to), device_id_type=MESH,
        )

    def roles(source):
        lane = core == source % 2
        far = (z + chips - source // 2) % chips
        return lane, far, lane & (far < half), lane & ((far == 0) | (far > half + 1))

    def items_launch(chosen, block):
        for n, (which, at, source) in enumerate(items):
            lane, far, plus, minus = roles(source)

            @pl.when(lane & (far == 0))
            def _():
                src = block(at[0])
                item_copy(chosen, n, src, 0, above).start()
                item_copy(chosen, n, src, 1, below).start()
                item_copy(chosen, n, src, 2, twin).start()
                chosen[0][which][at] = src[...]

    def relay_hop(t, chosen):
        for n, (which, at, source) in enumerate(items):
            lane, far, plus, minus = roles(source)

            @pl.when(lane & (jnp.minimum(far, chips - far) == t))
            def _():
                item_copy(chosen, n, None, 2, twin).wait_recv()

                @pl.when(plus)
                def _():
                    item_copy(chosen, n, None, 0, above).start()

                @pl.when(minus)
                def _():
                    item_copy(chosen, n, None, 1, below).start()

                item_copy(chosen, n, None, 2, twin).start()

    def gather(window):
        solve(0)
        pl.semaphore_wait(barrier, group - 1 + 3)
        launch(0)
        for k in range(1, parts):
            solve(k)
            if k < window:
                launch(k)
        for first in range(0, parts, window):
            last = first + window == parts
            for d in range(1, half + 1):
                for k in range(first, first + window):
                    relay(k, d)
                    if d == half - 1 and not last:
                        launch(k + window)
                    if d == half and last:
                        if k == first:
                            top_copy.wait()
                            own_copy.wait()
                            items_launch(top_set, top_block)
                        twins(k)
                        if k < parts - 1:
                            gram(k)
                if first:
                    for k in range(first - window, first)[d - 1 :: half]:
                        twins(k)
                        gram(k)

    gather(2)
    final = parts - 1
    picked = bufs[final][source(front)]
    for at in range(pivots):
        found = source(at)
        part_ref[at] = -(acc[found] + mm(bufs[final][found], picked, NT)).astype(jnp.bfloat16)

    def slice_copy(to, src):
        return pltpu.make_async_remote_copy(
            part_ref.at[to // per_block, pl.ds(to % per_block * rows, rows), :],
            got_slice.at[src], slice_send.at[to], slice_recv.at[src],
            device_id=(base + to, front), device_id_type=MESH,
        )

    def block_copy(to, src):
        return pltpu.make_async_remote_copy(
            part_ref.at[to], got_block.at[src], block_send.at[to], block_recv.at[src],
            device_id=(base + to, front), device_id_type=MESH,
        )

    def piece_copy(to, src):
        return pltpu.make_async_remote_copy(
            piece, pieces.at[pl.ds(pl.multiple_of(src * rows, rows), rows), :], piece_send.at[to], piece_recv.at[src],
            device_id=(base + to, front), device_id_type=MESH,
        )

    inner = front >= pivots

    def send_slice(d, carry):
        slice_copy(other(d), me).start()
        return carry

    def send_block(d, carry):
        to = other(d)

        @pl.when(inner & (to >= pivots))
        def _():
            block_copy(to, me).start()

        return carry

    lax.fori_loop(1, group, send_slice, 0)
    gram(final)
    for at in range(pivots, blocks):
        part_ref[at] = -acc[source(at)].astype(jnp.bfloat16)
    lax.fori_loop(1, EARLY, send_block, 0)
    relay_hop(1, top_set)

    def add_slice(d, total):
        src = other(d)
        slice_copy(src, src).wait_recv()
        return total + got_slice[src].astype(jnp.float32)

    mine = part_ref[me // per_block, pl.ds(pl.multiple_of(me % per_block * rows, rows), rows), :]
    total = lax.fori_loop(1, group, add_slice, mine.astype(jnp.float32))
    piece[...] = total.astype(jnp.bfloat16)
    pieces[pl.ds(pl.multiple_of(me * rows, rows), rows), :] = total.astype(jnp.bfloat16)

    def send_piece(d, carry):
        piece_copy(other(d), me).start()
        return carry

    lax.fori_loop(1, group, send_piece, 0)
    lax.fori_loop(EARLY, group, send_block, 0)

    def wait_piece(d, carry):
        src = other(d)
        piece_copy(src, src).wait_recv()
        return carry

    relay_hop(2, top_set)
    relay_hop(3, top_set)
    lax.fori_loop(1, group, wait_piece, 0)
    items_launch(sum_set, piece_block)
    for t in range(1, half):
        relay_hop(t, sum_set)
    own_ref[...] = block_ref[...] + part_ref[me].astype(jnp.float32)

    @pl.when(inner & (me >= pivots))
    def _():
        def add_block(d, carry):
            src = other(d)
            block_copy(src, src).wait_recv()
            own_ref[...] = own_ref[...] + got_block[src].astype(jnp.float32)
            return carry

        lax.fori_loop(1, group, add_block, 0)

    relay_hop(half, top_set)
    relay_hop(half, sum_set)
    for chosen in (top_set, sum_set):
        for n in range(len(items)):

            @pl.when(jnp.logical_not(roles(items[n][2])[0]))
            def _():
                item_copy(chosen, n, None, 2, twin).wait_recv()

    for p in range(pivots):
        rows_p = slice(p * b, (p + 1) * b)
        col_ref[p] = top_ref[rows_p, :] + pieces[rows_p, :].astype(jnp.float32)
        row_ref[p] = row_top[p] + row_sum[p].astype(jnp.float32)
        for q in range(p + 1):
            corner_ref[p * (p + 1) // 2 + q] = corner_top[p, q] + corner_sum[p, q].astype(jnp.float32)

    def drain(d, carry):
        to = other(d)
        slice_copy(to, me).wait_send()
        piece_copy(to, me).wait_send()

        @pl.when(inner & (to >= pivots))
        def _():
            block_copy(to, me).wait_send()

        return carry

    lax.fori_loop(1, group, drain, 0)
    for chosen in (top_set, sum_set):
        for n in range(len(items)):
            lane, far, plus, minus = roles(items[n][2])

            @pl.when(plus)
            def _():
                item_copy(chosen, n, None, 0, above).wait_send()

            @pl.when(minus)
            def _():
                item_copy(chosen, n, None, 1, below).wait_send()

            @pl.when(lane)
            def _():
                item_copy(chosen, n, None, 2, twin).wait_send()

    for k in range(parts):
        up, down = reach(k)
        for d in range(half + 1):
            if d < up:
                chunk_copy(k, block_at(-d), chunk_plus, above).wait_send()
            if d < down:
                chunk_copy(k, block_at(d), chunk_minus, below).wait_send()

        def sent(n, carry):
            chunk_copy(k, n * 2 + core, chunk_twin, twin).wait_send()
            return carry

        lax.fori_loop(0, chips, sent, 0)


def assemble(group, chips, coupling, factors, tops, pattern, sizes, maps):
    b = coupling.shape[1]
    blocks = tops.shape[1] // b
    pivots = PIV // b
    rows = PIV // group
    items = pivots * (pivots + 1) // 2 + pivots
    parts = len(CHUNKS)
    vmem = pl.BlockSpec(memory_space=pltpu.VMEM)
    smem = pl.BlockSpec(memory_space=pltpu.SMEM)
    dma = pltpu.SemaphoreType.DMA
    f32 = jnp.float32
    bf16 = jnp.bfloat16
    return pl.pallas_call(
        functools.partial(assemble_kernel, group, chips),
        out_shape=(
            jax.ShapeDtypeStruct((b, b), f32),
            jax.ShapeDtypeStruct((pivots * (pivots + 1) // 2, b, b), f32),
            jax.ShapeDtypeStruct((pivots, b, b), f32),
            jax.ShapeDtypeStruct((pivots, b, b), f32),
        ),
        in_specs=[pl.BlockSpec(memory_space=pltpu.MemorySpace.HBM)] * 3 + [smem] * 3,
        out_specs=[vmem] * 4,
        scratch_shapes=[
            pltpu.VMEM(coupling.shape, bf16),
            pltpu.VMEM(factors.shape, bf16),
            dma((2, parts)),
            [pltpu.VMEM((blocks, b, size * b), bf16) for size in CHUNKS],
            pltpu.VMEM((blocks, b, b), f32),
            pltpu.VMEM((blocks, b, b), bf16),
            pltpu.VMEM((PIV, b), f32),
            pltpu.VMEM((b, b), f32),
            pltpu.VMEM((group, rows, b), bf16),
            pltpu.VMEM((group, b, b), bf16),
            pltpu.VMEM((rows, b), bf16),
            pltpu.VMEM((PIV, b), bf16),
        ]
        + [dma((parts, blocks))] * 4
        + [dma((2,))]
        + [dma((group,))] * 6
        + [
            pltpu.VMEM((pivots, pivots, b, b), f32),
            pltpu.VMEM((pivots, b, b), f32),
            pltpu.VMEM((pivots, pivots, b, b), bf16),
            pltpu.VMEM((pivots, b, b), bf16),
        ]
        + [dma((3, items)), dma((items,))] * 2,
        compiler_params=pltpu.CompilerParams(collective_id=1, has_side_effects=True),
    )(coupling, factors, tops, pattern, sizes, maps)


def shards(coupling, block_pattern, supernode_inverse, subdomain_sizes, block_maps, top_fronts):
    group = lax.axis_size("leaf") // top_fronts.shape[0]
    chips = lax.axis_size("front") // 2
    own, corner, own_row, own_col = assemble(
        group, chips, coupling, supernode_inverse, top_fronts,
        block_pattern.transpose(0, 2, 1), subdomain_sizes, block_maps,
    )
    flat = (PIV, coupling.shape[1])
    return finish(group, corner, own_row.reshape(flat), own_col.reshape(flat), own)


def solution(mesh):
    return jax.shard_map(
        shards,
        mesh=mesh,
        in_specs=(
            P("leaf", "front"),
            P("leaf", None, "front"),
            P("leaf", None, None),
            P("leaf"),
            P(None, "leaf", None),
            P(None, None, "front"),
        ),
        out_specs=P("leaf", "front"),
        check_vma=False,
    )
```
